128 devices in a mesh: lat: 32 (over x, z, core), lev: 4 (over y).
Axes of the slice: x: 4, y: 4, z: 4, core: 2. Of those that a mesh axis runs over, the one named last changes fastest.
Arguments:
- tracer_dyn: bfloat16 [64, 72, 64, 1024], P(None, 'lev', 'lat'), may hold values from 0.19921875 to 5
- courant_lat: bfloat16 [72, 64, 1024], P('lev', 'lat'), may hold values from -0.44921875 to 0.44921875
- courant_lon: bfloat16 [72, 64, 1024], P('lev', 'lat'), may hold values from -0.44921875 to 0.44921875
- conv_matrix: bfloat16 [72, 72, 65536], P(None, None, ('lat', 'lev'))
- conv_mask: int32 [65536], P(('lat', 'lev')), may hold values from 0 to 1, as said below
- column_order: int32 [65536], P(('lat', 'lev')), may hold values from 0 to 511, as said below
- rain: bfloat16 [72, 65536], P(None, ('lat', 'lev')), may hold values from 0.019897461 to 1
- scav_rate: float32 [64], replicated, may hold values from 0.05 to 2
- pair_flag: int32 [64], replicated, may hold values from 0 to 1
Outputs:
- tracer_phys: bfloat16 [64, 72, 65536], P(None, None, ('lat', 'lev'))
The draws below stay inside these ranges and needn't reach their ends.
Inputs may be any that keep to these rules, and one draw needn't show every extreme that they name: `conv_mask`: in each aligned block of 512 entries (one span) at most 256 are 1, and some block has exactly 256. `column_order`: each aligned block of 512 entries holds every number of 0 to 511 once.
All inputs are finite; a program needn't handle non-finite values.
Results may differ from the reference program's by a relative error of at most 0.005.
Values may be sent and summed in bfloat16 or wider, within the bound.
No kernel may reach another device: no remote copies, remote signals or barrier semaphores. Data moves between devices by JAX's collectives and lax.ppermute only.
A program may use at most 128 MiB of HBM per device.

```python
import math
import jax
import jax.numpy as jnp
from jax import lax

TRACERS = 64
LEV = 72
LON = 1024
LAT_DEV = 2
NLAT = 64
COLS = 65536
LON_BLOCK = 256
COL_DEV = 512
CONV_CAP = 256
PAIRS = 64
N_LAT = 32
N_LEV = 4


def draw_conv_matrix(key, part):
    key_diag = jax.random.fold_in(key, 11)
    key_off = jax.random.fold_in(key, 12)
    diag = jax.random.uniform(key_diag, (COLS, LEV), jnp.float32, 0.5, 1.0)
    off = jax.random.normal(key_off, (COLS, LEV, LEV), jnp.float32) * 0.4 / jnp.sqrt(1.0 * LEV)
    eye = jnp.eye(LEV, dtype=jnp.float32)
    whole = off + diag[:, :, None] * eye[None]
    return jnp.transpose(whole, (1, 2, 0)).astype(jnp.bfloat16)


def draw_conv_mask(key, part):
    spans = COLS // COL_DEV
    key_count = jax.random.fold_in(key, 21)
    key_heavy = jax.random.fold_in(key, 22)
    key_perm = jax.random.fold_in(key, 23)
    raw = jax.random.randint(key_count, (spans,), 0, CONV_CAP + 1)
    counts = jnp.maximum(raw * raw // CONV_CAP, 1)
    heavy = jax.random.randint(key_heavy, (), 0, spans)
    counts = jnp.where(jnp.arange(spans) == heavy, CONV_CAP, counts)
    keys = jax.random.split(key_perm, spans)
    ranks = jax.vmap(lambda single: jax.random.permutation(single, COL_DEV))(keys)
    return (ranks < counts[:, None]).astype(jnp.int32).reshape(COLS)


def draw_column_order(key, part):
    spans = COLS // COL_DEV
    keys = jax.random.split(jax.random.fold_in(key, 31), spans)
    perms = jax.vmap(lambda single: jax.random.permutation(single, COL_DEV))(keys)
    return perms.astype(jnp.int32).reshape(COLS)


def with_ends(values, stream_key, low, high):
    longest = values.shape.index(max(values.shape))
    spots = []
    for shift in (0, 1):
        where = [jax.random.randint(jax.random.fold_in(stream_key, axis), (), 0, length) for axis, length in enumerate(values.shape)]
        where[longest] = (where[longest] + shift) % values.shape[longest]
        spots.append(tuple(where))
    return values.at[spots[0]].set(low).at[spots[1]].set(high)


def block_scale(stream_key, dims, shards, low, high):
    def one(axis_at, parts):
        heights = jax.random.uniform(jax.random.fold_in(jax.random.fold_in(stream_key, 6), axis_at), (parts,), jnp.float32, low / len(shards), high / len(shards))
        return jnp.repeat(jnp.exp(heights), dims[axis_at] // parts).reshape((-1,) + (1,) * (len(dims) - axis_at - 1))

    loudness = one(*shards[0])
    for cut in shards[1:]:
        loudness = loudness * one(*cut)
    return loudness


def setup_inputs(seed: int = 0) -> dict:
    seeds = jax.random.split(jax.random.key(seed), 10)
    return {
        "tracer_dyn": jnp.clip(jnp.exp(math.log(5.0) - 3.2227897 * jax.random.uniform(seeds[0], (TRACERS, LEV, NLAT, LON), jnp.float32) ** block_scale(seeds[0], (TRACERS, LEV, NLAT, LON), ((1, 4), (2, 32)), -0.2, 0.2)), 0.19921875, 5.0).astype(jnp.bfloat16),
        "courant_lat": jnp.clip(jax.random.uniform(seeds[1], (LEV, NLAT, LON), jnp.float32, -0.44921875, 0.44921875) * block_scale(seeds[1], (LEV, NLAT, LON), ((0, 4), (1, 32)), -0.4, 0.0), -0.44921875, 0.44921875).astype(jnp.bfloat16),
        "courant_lon": jnp.clip(jax.random.uniform(seeds[2], (LEV, NLAT, LON), jnp.float32, -0.44921875, 0.44921875) * block_scale(seeds[2], (LEV, NLAT, LON), ((0, 4), (1, 32)), -0.4, 0.0), -0.44921875, 0.44921875).astype(jnp.bfloat16),
        "conv_matrix": draw_conv_matrix(jax.random.fold_in(seeds[9], 71), 0),
        "conv_mask": draw_conv_mask(jax.random.fold_in(seeds[9], 71), 0),
        "column_order": draw_column_order(jax.random.fold_in(seeds[9], 71), 0),
        "rain": jnp.clip(jnp.exp(math.log(1.0) - 3.9171631 * jax.random.uniform(seeds[6], (LEV, COLS), jnp.float32) ** block_scale(seeds[6], (LEV, COLS), ((1, 128),), -0.2, 0.2)), 0.019897461, 1.0).astype(jnp.bfloat16),
        "scav_rate": jnp.clip(jnp.exp(jax.random.uniform(seeds[7], (TRACERS,), jnp.float32, math.log(0.05), math.log(2.0))), 0.05, 2.0),
        "pair_flag": with_ends(jax.random.randint(seeds[8], (PAIRS,), 0, 2), jax.random.fold_in(seeds[8], 1), 0, 1).astype(jnp.int32),
    }


def advect_block(center, south_side, north_side, south_face, north_face, west_face):
    east_face = jnp.roll(west_face, -1, axis=-1)
    south_flux = south_face * jnp.where(south_face > 0, south_side, center)
    north_flux = north_face * jnp.where(north_face > 0, center, north_side)
    west_flux = west_face * jnp.where(west_face > 0, jnp.roll(center, 1, axis=-1), center)
    east_flux = east_face * jnp.where(east_face > 0, center, jnp.roll(center, -1, axis=-1))
    return center - (north_flux - south_flux) - (east_flux - west_flux)


def reference(tracer_dyn, courant_lat, courant_lon, conv_matrix, conv_mask, column_order, rain, scav_rate, pair_flag):
    south_face = courant_lat.astype(jnp.float32)
    west_face = courant_lon.astype(jnp.float32)
    north_face = jnp.concatenate([south_face[:, 1:], jnp.zeros_like(south_face[:, :1])], axis=1)

    def advect_one(tracer):
        center = tracer.astype(jnp.float32)
        zero_row = jnp.zeros_like(center[:, :1])
        south_side = jnp.concatenate([zero_row, center[:, :-1]], axis=1)
        north_side = jnp.concatenate([center[:, 1:], zero_row], axis=1)
        return advect_block(center, south_side, north_side, south_face, north_face, west_face).astype(jnp.bfloat16)

    advected = lax.map(advect_one, tracer_dyn)
    blocked = advected.reshape(TRACERS, LEV, N_LAT, LAT_DEV, N_LEV, LON_BLOCK)
    physics = jnp.transpose(blocked, (0, 1, 2, 4, 3, 5)).reshape(TRACERS, LEV, COLS)
    spans = COLS // COL_DEV
    by_span = physics.reshape(TRACERS, LEV, spans, COL_DEV).transpose(2, 0, 1, 3)
    matrices = conv_matrix.reshape(LEV, LEV, spans, COL_DEV).transpose(2, 0, 1, 3)
    masks = conv_mask.reshape(spans, COL_DEV)
    orders = column_order.reshape(spans, COL_DEV)
    rains = rain.reshape(LEV, spans, COL_DEV).transpose(1, 0, 2)

    def span_physics(items):
        tracers, matrix, mask, order, wet = items
        ordered = tracers[:, :, order].astype(jnp.float32)
        moved = jnp.einsum('kec,tec->tkc', matrix.astype(jnp.float32), ordered)
        convected = jnp.where(mask[None, None, :] > 0, moved, ordered)
        washed = convected * jnp.exp(-scav_rate[:, None, None] * wet.astype(jnp.float32)[None])
        return washed.astype(jnp.bfloat16)

    result = lax.map(span_physics, (by_span, matrices, masks, orders, rains))
    grid = result.reshape(N_LAT, N_LEV, TRACERS, LEV, COL_DEV)
    partner = jnp.roll(grid, N_LAT // 2, axis=0)
    half_flags = pair_flag.reshape(N_LAT // 2, N_LEV)
    flags = jnp.concatenate([half_flags, half_flags], axis=0)
    final = jnp.where(flags[:, :, None, None, None] > 0, partner, grid)
    return final.transpose(2, 3, 0, 1, 4).reshape(TRACERS, LEV, COLS)
```

```python
import functools

import jax
import jax.numpy as jnp
from jax import lax
from jax.experimental import pallas as pl
from jax.experimental.pallas import tpu as pltpu
from jax.sharding import PartitionSpec as P

GROUP = 8
CHUNKS = (1, 1, 2, 2, 2)
CAP = 256
K_BLOCK = 8
F32 = jnp.float32
BF16 = jnp.bfloat16


def odd_rows(rows):
    return lax.broadcasted_iota(jnp.int32, (rows, 128), 0) % 2 == 1


def extract_kernel(q_ref, north_ref, south_ref):
    levels = q_ref.shape[1]
    odd = odd_rows(16)

    def level(k, carry):
        for pair in range(GROUP // 2):
            a = q_ref[2 * pair, k].astype(F32)
            b = q_ref[2 * pair + 1, k].astype(F32)
            north_ref[0, k, pair] = jnp.where(odd, a, pltpu.roll(b, 15, 0)).astype(BF16)
            south_ref[0, k, pair] = jnp.where(odd, pltpu.roll(b, 1, 0), a).astype(BF16)
        return carry

    lax.fori_loop(0, levels, level, 0)


def extract(q, first, groups):
    levels = q.shape[1]
    shape = jax.ShapeDtypeStruct((groups, levels, GROUP // 2, 16, 128), BF16)
    block = pl.BlockSpec((1, levels, GROUP // 2, 16, 128), lambda g: (g, 0, 0, 0, 0))
    return pl.pallas_call(
        extract_kernel,
        grid=(groups,),
        in_specs=[pl.BlockSpec((GROUP, levels, 16, 128), lambda g: (g + first, 0, 0, 0))],
        out_specs=[block, block],
        out_shape=[shape, shape],
        cost_estimate=pl.CostEstimate(
            flops=groups * 10**6, bytes_accessed=groups * 1200000, transcendentals=0
        ),
        compiler_params=pltpu.CompilerParams(vmem_limit_bytes=16 << 20),
        name="extract",
    )(q)


def lane_shift(x, lane, toward_east):
    if toward_east:
        turned = pltpu.roll(x, 127, 1)
        return jnp.where(lane == 127, pltpu.roll(turned, 14, 0), turned)
    turned = pltpu.roll(x, 1, 1)
    return jnp.where(lane == 0, pltpu.roll(turned, 2, 0), turned)


def advect_kernel(place_ref, q_ref, low_ref, high_ref, lat_ref, lon_ref, above_ref, *refs):
    outs, held = refs[:-1], refs[-1]
    levels = q_ref.shape[1]
    rows = levels * GROUP
    odd = odd_rows(16)
    lane = lax.broadcasted_iota(jnp.int32, (16, 128), 1)

    def level(k, carry):
        south = lat_ref[k].astype(F32)
        north = jnp.where(
            odd, pltpu.roll(above_ref[k].astype(F32), 1, 0), pltpu.roll(south, 15, 0)
        )
        west = lon_ref[k].astype(F32)
        east = lane_shift(west, lane, True)
        from_south, from_west = jnp.maximum(south, 0.0), jnp.maximum(west, 0.0)
        from_north, from_east = -jnp.minimum(north, 0.0), -jnp.minimum(east, 0.0)
        own = (
            1.0
            - (jnp.maximum(north, 0.0) - jnp.minimum(south, 0.0))
            - (jnp.maximum(east, 0.0) - jnp.minimum(west, 0.0))
        )
        for pair in range(GROUP // 2):
            low = low_ref[0, k, pair].astype(F32)
            high = high_ref[0, k, pair].astype(F32)
            for part in range(2):
                q = q_ref[2 * pair + part, k].astype(F32)
                below = low if part else pltpu.roll(low, 15, 0)
                above = high if part else pltpu.roll(high, 1, 0)
                q_s = jnp.where(odd, pltpu.roll(q, 1, 0), below)
                q_n = jnp.where(odd, above, pltpu.roll(q, 15, 0))
                q_w = lane_shift(q, lane, False)
                q_e = lane_shift(q, lane, True)
                new = (
                    own * q
                    + (from_south * q_s + from_north * q_n)
                    + (from_west * q_w + from_east * q_e)
                )
                start = k * GROUP + (2 * pair + part)
                held[pl.ds(start, 16, stride=rows), :] = new
        return carry

    lax.fori_loop(0, levels, level, 0)
    place = place_ref[0]
    for shift, out in enumerate(outs):
        target = lax.rem(place + shift, 4)
        for lat in range(2):
            for half in range(2):
                base = pl.multiple_of((4 * target + (2 * half + lat)) * rows, 8)
                column = (2 * lat + half) * 128
                out[0, :, column : column + 128] = held[pl.ds(base, rows), :].astype(BF16)


def advect(place, q, low, high, lat, lon, above, first, halo_first, groups):
    levels = q.shape[1]
    rows = levels * GROUP
    halo = pl.BlockSpec(
        (1, levels, GROUP // 2, 16, 128), lambda g, p: (g + halo_first, 0, 0, 0, 0)
    )
    face = pl.BlockSpec((levels, 16, 128), lambda g, p: (0, 0, 0))
    return pl.pallas_call(
        advect_kernel,
        grid_spec=pltpu.PrefetchScalarGridSpec(
            num_scalar_prefetch=1,
            grid=(groups,),
            in_specs=[
                pl.BlockSpec((GROUP, levels, 16, 128), lambda g, p: (g + first, 0, 0, 0)),
                halo,
                halo,
                face,
                face,
                face,
            ],
            out_specs=[pl.BlockSpec((1, rows, 512), lambda g, p: (g, 0, 0))] * 4,
            scratch_shapes=[pltpu.VMEM((16 * rows, 128), F32)],
        ),
        out_shape=[jax.ShapeDtypeStruct((groups, rows, 512), BF16)] * 4,
        cost_estimate=pl.CostEstimate(
            flops=groups * 10**7, bytes_accessed=groups * 2000000, transcendentals=0
        ),
        compiler_params=pltpu.CompilerParams(vmem_limit_bytes=24 << 20),
        name="advect",
    )(place, q, low, high, lat, lon, above)


def table_kernel(
    matrix_ref, mask_ref, order_ref, rain_ref, small_ref, placing_ref, back_ref, wet_ref, all_ref
):
    columns = mask_ref.shape[1]

    @pl.when(pl.program_id(0) == 0)
    def _():
        mask = mask_ref[...]
        order = order_ref[...]
        row = lax.broadcasted_iota(jnp.int32, (columns, columns), 0)
        column = lax.broadcasted_iota(jnp.int32, (columns, columns), 1)
        earlier = jnp.where(row < column, 1.0, 0.0).astype(BF16)
        ones = jnp.where(mask > 0, 1.0, 0.0)
        wide = jnp.broadcast_to(ones, (8, columns)).astype(BF16)
        rank = jnp.dot(wide, earlier, preferred_element_type=F32)[0:1]
        rank = jnp.where(mask > 0, rank, -1.0).astype(jnp.int32)
        slot = lax.broadcasted_iota(jnp.int32, (CAP, columns), 0)
        back = jnp.where(slot == rank, 1.0, 0.0).astype(BF16)
        back_ref[...] = back
        whole = jnp.where(row == order, 1.0, 0.0)
        placing_ref[:, :columns] = jnp.where(mask > 0, 0.0, whole).astype(BF16)
        placing_ref[:, columns:] = lax.dot_general(
            whole.astype(BF16), back, (((1,), (1,)), ((), ())), preferred_element_type=F32
        ).astype(BF16)
        wet = lax.dot_general(
            rain_ref[...], back, (((1,), (1,)), ((), ())), preferred_element_type=F32
        )
        for tile in range(CAP // 128):
            wet_ref[tile] = wet[:, tile * 128 : (tile + 1) * 128]
        for tile in range(columns // 128):
            all_ref[tile] = rain_ref[:, tile * 128 : (tile + 1) * 128].astype(F32)

    small = lax.dot_general(
        matrix_ref[...], back_ref[...], (((1,), (1,)), ((), ())), preferred_element_type=F32
    )
    for tile in range(CAP // 128):
        small_ref[tile] = small[:, tile * 128 : (tile + 1) * 128]


def tables(matrix, mask, order, rain):
    rows, columns = matrix.shape
    levels = rain.shape[0]
    steps = 9
    whole = lambda *shape: pl.BlockSpec(shape, lambda i: (0,) * len(shape))
    return pl.pallas_call(
        table_kernel,
        grid=(steps,),
        in_specs=[
            pl.BlockSpec((rows // steps, columns), lambda i: (i, 0)),
            whole(1, columns),
            whole(1, columns),
            whole(levels, columns),
        ],
        out_specs=[
            pl.BlockSpec((CAP // 128, rows // steps, 128), lambda i: (0, i, 0)),
            whole(columns, columns + CAP),
            whole(CAP, columns),
            whole(CAP // 128, levels, 128),
            whole(columns // 128, levels, 128),
        ],
        out_shape=[
            jax.ShapeDtypeStruct((CAP // 128, rows, 128), F32),
            jax.ShapeDtypeStruct((columns, columns + CAP), BF16),
            jax.ShapeDtypeStruct((CAP, columns), BF16),
            jax.ShapeDtypeStruct((CAP // 128, levels, 128), F32),
            jax.ShapeDtypeStruct((columns // 128, levels, 128), F32),
        ],
        cost_estimate=pl.CostEstimate(
            flops=2 * rows * columns * CAP, bytes_accessed=12 * 10**6, transcendentals=0
        ),
        compiler_params=pltpu.CompilerParams(vmem_limit_bytes=24 << 20),
        name="tables",
    )(matrix, mask, order, rain)


def physics_kernel(
    place_ref,
    part0_ref,
    part1_ref,
    part2_ref,
    part3_ref,
    placing_ref,
    back_ref,
    matrix_ref,
    rain_ref,
    wet_ref,
    rate_ref,
    out_ref,
    dry,
    moist,
    held,
):
    groups, rows, columns = part0_ref.shape
    levels = dry.shape[1] // GROUP
    step = pl.program_id(0)

    @pl.when(step == 0)
    def _():
        for shift, part in enumerate((part0_ref, part1_ref, part2_ref, part3_ref)):
            source = lax.rem(place_ref[0] + (4 - shift), 4)
            base = pl.multiple_of(source * rows, 8)
            for g in range(groups):
                placed = jnp.dot(part[g], placing_ref[...], preferred_element_type=F32)
                dry[g, pl.ds(base, rows), :] = placed[:, :columns]
                moist[g, pl.ds(base, rows), :] = placed[:, columns:]

    first = step * K_BLOCK
    rates = [rate_ref[g] for g in range(groups)]
    washed = [[[None] * 2 for _ in range(K_BLOCK)] for _ in range(groups)]
    for tile in range(CAP // 128):
        lanes = slice(tile * 128, (tile + 1) * 128)

        def source_levels(block, sums, tile=tile, lanes=lanes):
            sums = list(sums)
            for inner in range(8):
                e = block * 8 + inner
                spot = pl.multiple_of(block * (8 * GROUP) + inner * GROUP, GROUP)
                values = [moist[g, pl.ds(spot, GROUP), lanes] for g in range(groups)]
                for k in range(K_BLOCK):
                    weight = matrix_ref[tile, k, pl.ds(e, GROUP, stride=0), :]
                    for g in range(groups):
                        at = g * K_BLOCK + k
                        sums[at] = sums[at] + weight * values[g]
            return tuple(sums)

        zero = jnp.zeros((GROUP, 128), F32)
        sums = lax.fori_loop(
            0, levels // 8, source_levels, (zero,) * (groups * K_BLOCK)
        )
        for k in range(K_BLOCK):
            wet = wet_ref[tile, pl.ds(first + k, GROUP, stride=0), :]
            for g in range(groups):
                washed[g][k][tile] = sums[g * K_BLOCK + k] * jnp.exp(-rates[g] * wet)
    for g in range(groups):
        packed = jnp.concatenate(
            [jnp.concatenate(washed[g][k], axis=1) for k in range(K_BLOCK)], axis=0
        ).astype(BF16)
        spread = jnp.dot(packed, back_ref[...], preferred_element_type=F32)
        for k in range(K_BLOCK):
            spot = pl.multiple_of((first + k) * GROUP, GROUP)
            plain = dry[g, pl.ds(spot, GROUP), :]
            for tile in range(columns // 128):
                lanes = slice(tile * 128, (tile + 1) * 128)
                wet = rain_ref[tile, pl.ds(first + k, GROUP, stride=0), :]
                held[tile, pl.ds(g * GROUP * levels + first + k, GROUP, stride=levels), :] = (
                    spread[k * GROUP : (k + 1) * GROUP, lanes]
                    + plain[:, lanes] * jnp.exp(-rates[g] * wet)
                )

    @pl.when(step == pl.num_programs(0) - 1)
    def _():
        for tile in range(columns // 128):
            out_ref[:, tile * 128 : (tile + 1) * 128] = held[tile].astype(BF16)


def physics(place, parts, placing, back, matrix, rain, wet, rates, first, groups):
    rows, columns = parts[0].shape[1:]
    levels = rain.shape[1]
    whole = lambda *shape: pl.BlockSpec(shape, lambda i, p: (0,) * len(shape))
    flops = groups * 2 * GROUP * levels * (columns * (columns + 2 * CAP) + levels * CAP * 20)
    return pl.pallas_call(
        physics_kernel,
        grid_spec=pltpu.PrefetchScalarGridSpec(
            num_scalar_prefetch=1,
            grid=(levels // K_BLOCK,),
            in_specs=[whole(groups, rows, columns)] * 4
            + [
                whole(columns, columns + CAP),
                whole(CAP, columns),
                pl.BlockSpec((CAP // 128, K_BLOCK, levels, 128), lambda i, p: (0, i, 0, 0)),
                whole(columns // 128, levels, 128),
                whole(CAP // 128, levels, 128),
                pl.BlockSpec((groups, GROUP, 128), lambda i, p: (first // groups, 0, 0)),
            ],
            out_specs=whole(groups * GROUP * levels, columns),
            scratch_shapes=[
                pltpu.VMEM((groups, levels * GROUP, columns), F32),
                pltpu.VMEM((groups, levels * GROUP, CAP), F32),
                pltpu.VMEM((columns // 128, groups * GROUP * levels, 128), F32),
            ],
        ),
        out_shape=jax.ShapeDtypeStruct((groups * GROUP * levels, columns), BF16),
        cost_estimate=pl.CostEstimate(
            flops=flops, bytes_accessed=groups * 1200000 + 6500000, transcendentals=0
        ),
        compiler_params=pltpu.CompilerParams(vmem_limit_bytes=32 << 20),
        name="physics",
    )(place, *parts, placing, back, matrix, rain, wet, rates)


def choose_kernel(flag_ref, own_ref, partner_ref, *refs):
    out_ref = refs[-1]

    @pl.when(flag_ref[0] > 0)
    def _():
        out_ref[...] = partner_ref[...]

    @pl.when(flag_ref[0] <= 0)
    def _():
        out_ref[...] = own_ref[...]


def choose(flag, own, partner, whole, shape, first, groups):
    rows = shape[0] // (sum(CHUNKS))
    columns = shape[1]
    operands = [own, partner]
    specs = [
        pl.BlockSpec((rows, columns), lambda g, f: (jnp.where(f[0] > 0, 0, g), 0)),
        pl.BlockSpec((rows, columns), lambda g, f: (jnp.where(f[0] > 0, g, 0), 0)),
    ]
    aliases = {}
    if whole is not None:
        operands.append(whole)
        specs.append(pl.BlockSpec(memory_space=pl.ANY))
        aliases = {3: 0}
    return pl.pallas_call(
        choose_kernel,
        grid_spec=pltpu.PrefetchScalarGridSpec(
            num_scalar_prefetch=1,
            grid=(groups,),
            in_specs=specs,
            out_specs=pl.BlockSpec((rows, columns), lambda g, f: (g + first, 0)),
        ),
        out_shape=jax.ShapeDtypeStruct(shape, BF16),
        input_output_aliases=aliases,
        cost_estimate=pl.CostEstimate(
            flops=0, bytes_accessed=groups * 1200000, transcendentals=0
        ),
        compiler_params=pltpu.CompilerParams(vmem_limit_bytes=16 << 20),
        name="choose",
    )(flag, *operands)


def shifted(value, axis, steps):
    count = lax.axis_size(axis)
    pairs = [(i, i + steps) for i in range(count) if 0 <= i + steps < count]
    return lax.ppermute(value, axis, pairs)


def turned(value, axis, steps):
    count = lax.axis_size(axis)
    return lax.ppermute(value, axis, [(i, (i + steps) % count) for i in range(count)])


def paired(value, axis):
    count = lax.axis_size(axis)
    return lax.ppermute(value, axis, [(i, i ^ (count // 2)) for i in range(count)])


def tiled_rows(value):
    lead = value.shape[:-2]
    lats, lons = value.shape[-2:]
    split = value.reshape(*lead, lats, lons // 128, 128)
    return jnp.swapaxes(split, -3, -2).reshape(*lead, lats * lons // 128, 128)


def local(
    tracer_dyn,
    courant_lat,
    courant_lon,
    conv_matrix,
    conv_mask,
    column_order,
    rain,
    scav_rate,
    pair_flag,
):
    n_lat = lax.axis_size("lat")
    n_lev = lax.axis_size("lev")
    tracers = tracer_dyn.shape[0]
    levels, columns = rain.shape
    lev_place = lax.axis_index("lev")
    place = lev_place.astype(jnp.int32).reshape(1)
    pair_index = lax.axis_index("lat") % (n_lat // 2) * n_lev + lev_place
    flag = lax.dynamic_slice_in_dim(pair_flag, pair_index, 1)
    rates = jnp.broadcast_to(
        scav_rate.reshape(tracers // GROUP, GROUP, 1), (tracers // GROUP, GROUP, 128)
    )

    q = tiled_rows(tracer_dyn)
    lat, lon = tiled_rows(courant_lat), tiled_rows(courant_lon)
    above = tiled_rows(shifted(courant_lat, "lat", -1))
    halos = []
    spans = ((0, CHUNKS[0]), (CHUNKS[0], sum(CHUNKS) - CHUNKS[0]))
    for first, groups in spans:
        north, south = extract(q, first, groups)
        halos.append((shifted(north, "lat", 1), shifted(south, "lat", -1)))
    small, placing, back, wet, wet_all = tables(
        conv_matrix.reshape(levels * levels, columns),
        conv_mask.reshape(1, columns),
        column_order.reshape(1, columns),
        rain,
    )
    small = small.reshape(CAP // 128, levels, levels, 128)

    out = None
    first = 0
    for number, groups in enumerate(CHUNKS):
        low, high = halos[min(number, 1)]
        halo_first = first - spans[min(number, 1)][0]
        parts = advect(place, q, low, high, lat, lon, above, first, halo_first, groups)
        parts = [parts[0]] + [turned(parts[s], "lev", s) for s in range(1, n_lev)]
        own = physics(place, parts, placing, back, small, wet_all, wet, rates, first, groups)
        partner = paired(own, "lat")
        out = choose(flag, own, partner, out, (tracers * levels, columns), first, groups)
        first += groups
    return out.reshape(tracers, levels, columns)


def solution(mesh):
    placed = (
        P(None, "lev", "lat", None),
        P("lev", "lat", None),
        P("lev", "lat", None),
        P(None, None, ("lat", "lev")),
        P(("lat", "lev")),
        P(("lat", "lev")),
        P(None, ("lat", "lev")),
        P(),
        P(),
    )
    return jax.shard_map(
        local, mesh=mesh, in_specs=placed, out_specs=P(None, None, ("lat", "lev")), check_vma=False
    )
```

```python
import itertools

import jax
import jax.numpy as jnp
import numpy as np
from jax import lax
from jax.experimental import pallas as pl
from jax.experimental.pallas import tpu as pltpu
from jax.sharding import PartitionSpec as P

GROUP = 8
CHUNKS = (1, 1, 2, 2, 2)
SPANS = ((0, 1), (1, 3), (4, 4))
ORDER = (
    ("extract", 0),
    ("extract", 1),
    ("advect", 0),
    ("tables", 0),
    ("advect", 1),
    ("physics", 0),
    ("extract", 2),
    ("advect", 2),
    ("physics", 1),
    ("advect", 3),
    ("physics", 2),
    ("choose", 0),
    ("advect", 4),
    ("physics", 3),
    ("choose", 1),
    ("physics", 4),
    ("choose", 2),
    ("choose", 3),
    ("choose", 4),
)
CAP = 256
K_BLOCK = 8
F32 = jnp.float32
BF16 = jnp.bfloat16


def deinterleave():
    move = np.zeros((256, 256), np.float32)
    for k, a, t, i in itertools.product(range(2), range(2), range(GROUP), range(8)):
        move[((k * 2 + a) * GROUP + t) * 8 + i, ((t * 2 + k) * 8 + i) * 2 + a] = 1
    return jnp.asarray(move, BF16)


def regroup(n_lev):
    move = np.zeros((n_lev, 256, 256), np.float32)
    for j, s, a, h in itertools.product(range(n_lev), range(n_lev), range(2), range(2)):
        tile = 2 * ((j + s) % n_lev) + h
        for k, t in itertools.product(range(2), range(GROUP)):
            row = (((s * 2 + a) * 2 + h) * 2 + k) * GROUP + t
            move[j, row, ((k * 2 + a) * GROUP + t) * 8 + tile] = 1
    return jnp.asarray(move, BF16)


def face_rows(levels):
    rows = levels * 8
    move = np.zeros((2 * rows, 2 * rows), np.float32)
    for a, r in itertools.product(range(2), range(rows)):
        move[a * rows + r, r * 2 + a] = 1
    return jnp.asarray(move, BF16)


def product(a, b):
    return jnp.dot(a, b, preferred_element_type=F32)


def two_levels(q_ref, pair):
    return q_ref[:, pl.ds(2 * pair, 2)].reshape(2 * GROUP * 16, 128)


def extract_kernel(apart_ref, face_move_ref, q_ref, lat_ref, *refs):
    north_ref, south_ref = refs[-2:]
    levels = q_ref.shape[1]
    rows = levels * GROUP * 8

    def body(pair, carry):
        apart = product(apart_ref[...], two_levels(q_ref, pair)).astype(BF16)
        spot = pl.multiple_of(pair * 128, 128)
        south_ref[0, pl.ds(spot, 64), :] = apart[0:64]
        north_ref[0, pl.ds(spot, 64), :] = apart[64:128]
        south_ref[0, pl.ds(spot + 64, 64), :] = apart[128:192]
        north_ref[0, pl.ds(spot + 64, 64), :] = apart[192:256]
        return carry

    lax.fori_loop(0, levels // 2, body, 0)
    if south_ref.shape[1] > rows:
        faces = lat_ref[...].reshape(levels * 16, 128)
        south_ref[0, rows:, :] = product(face_move_ref[: levels * 8], faces).astype(BF16)


def whole_block(*shape):
    return pl.BlockSpec(shape, lambda *_: (0,) * len(shape))


def extract(apart, face_move, q, lat, first, groups, after):
    levels = q.shape[1]
    rows = levels * GROUP * 8
    extra = levels * 8 if first == 0 else 0
    return pl.pallas_call(
        extract_kernel,
        grid=(groups,),
        in_specs=[
            whole_block(*apart.shape),
            whole_block(*face_move.shape),
            pl.BlockSpec((GROUP, levels, 16, 128), lambda g: (g + first, 0, 0, 0)),
            whole_block(*lat.shape),
        ]
        + [pl.BlockSpec(memory_space=pl.ANY)] * len(after),
        out_specs=[
            pl.BlockSpec((1, rows, 128), lambda g: (g, 0, 0)),
            pl.BlockSpec((1, rows + extra, 128), lambda g: (g, 0, 0)),
        ],
        out_shape=[
            jax.ShapeDtypeStruct((groups, rows, 128), BF16),
            jax.ShapeDtypeStruct((groups, rows + extra, 128), BF16),
        ],
        cost_estimate=pl.CostEstimate(
            flops=groups * 10**6, bytes_accessed=groups * 1200000, transcendentals=0
        ),
        compiler_params=pltpu.CompilerParams(vmem_limit_bytes=16 << 20),
        name="extract",
    )(apart, face_move, q, lat, *after)


def beside(x, lane, toward_east):
    if toward_east:
        turned = pltpu.roll(x, 127, 1)
        return jnp.where(lane == 127, pltpu.roll(turned, 7, 0), turned)
    turned = pltpu.roll(x, 1, 1)
    return jnp.where(lane == 0, pltpu.roll(turned, 1, 0), turned)


def advect_kernel(
    place_ref, apart_ref, group_ref, face_move_ref, q_ref, low_ref, high_ref, lat_ref, lon_ref,
    above_ref, *refs
):
    outs, faces = refs[-5:-1], refs[-1]
    levels = q_ref.shape[1]
    lane = lax.broadcasted_iota(jnp.int32, (8, 128), 1)

    @pl.when(pl.program_id(0) == 0)
    def _():
        for at, ref in ((0, lat_ref), (2, lon_ref)):
            both = product(face_move_ref[...], ref[...].reshape(levels * 16, 128))
            faces[at] = both[: levels * 8]
            faces[at + 1] = both[levels * 8 :]
        faces[4] = above_ref[0].astype(F32)

    def body(pair, carry):
        apart = product(apart_ref[...], two_levels(q_ref, pair))
        spot = pl.multiple_of(pair * 128, 128)
        low = low_ref[0, pl.ds(spot, 128), :].astype(F32)
        high = high_ref[0, pl.ds(spot, 128), :].astype(F32)
        results = []
        for k in range(2):
            at = pl.ds(pl.multiple_of((2 * pair + k) * 8, 8), 8)
            edge = [faces[0, at, :], faces[1, at, :], faces[4, at, :]]
            terms = []
            for lat in range(2):
                south, north, west = edge[lat], edge[lat + 1], faces[2 + lat, at, :]
                east = beside(west, lane, True)
                own = (
                    1.0
                    - (jnp.maximum(north, 0.0) - jnp.minimum(south, 0.0))
                    - (jnp.maximum(east, 0.0) - jnp.minimum(west, 0.0))
                )
                terms.append(
                    (
                        own,
                        jnp.maximum(south, 0.0),
                        -jnp.minimum(north, 0.0),
                        jnp.maximum(west, 0.0),
                        -jnp.minimum(east, 0.0),
                    )
                )
            made = [[], []]
            for t in range(GROUP):
                rows = [
                    apart[(k * 2 + lat) * 64 + t * 8 : (k * 2 + lat) * 64 + t * 8 + 8]
                    for lat in range(2)
                ]
                outer = [x[k * 64 + t * 8 : k * 64 + t * 8 + 8] for x in (low, high)]
                column = [outer[0], rows[0], rows[1], outer[1]]
                for lat in range(2):
                    own, from_s, from_n, from_w, from_e = terms[lat]
                    made[lat].append(
                        own * rows[lat]
                        + (from_s * column[lat] + from_n * column[lat + 2])
                        + (
                            from_w * beside(rows[lat], lane, False)
                            + from_e * beside(rows[lat], lane, True)
                        )
                    )
            results += made[0] + made[1]
        sent = product(group_ref[0], jnp.concatenate(results, axis=0).astype(BF16)).astype(BF16)
        spot = pl.multiple_of(pair * 16, 16)
        for shift, out in enumerate(outs):
            for quarter in range(4):
                row = (shift * 4 + quarter) * 16
                out[0, pl.ds(spot, 16), quarter * 128 : (quarter + 1) * 128] = sent[row : row + 16]
        return carry

    lax.fori_loop(0, levels // 2, body, 0)


def advect(
    place, apart, group, face_move, q, low, high, lat, lon, above, first, halo_first, groups, after
):
    levels = q.shape[1]
    rows = levels * GROUP
    halo = pl.BlockSpec((1, rows * 8, 128), lambda g, p: (g + halo_first, 0, 0))
    return pl.pallas_call(
        advect_kernel,
        grid_spec=pltpu.PrefetchScalarGridSpec(
            num_scalar_prefetch=1,
            grid=(groups,),
            in_specs=[
                whole_block(*apart.shape),
                pl.BlockSpec((1, 256, 256), lambda g, p: (p[0], 0, 0)),
                whole_block(*face_move.shape),
                pl.BlockSpec((GROUP, levels, 16, 128), lambda g, p: (g + first, 0, 0, 0)),
                halo,
                halo,
                whole_block(*lat.shape),
                whole_block(*lon.shape),
                pl.BlockSpec((1, levels * 8, 128), lambda g, p: (0, GROUP, 0)),
            ]
            + [pl.BlockSpec(memory_space=pl.ANY)] * len(after),
            out_specs=[pl.BlockSpec((1, rows, 512), lambda g, p: (g, 0, 0))] * 4,
            scratch_shapes=[pltpu.VMEM((5, levels * 8, 128), F32)],
        ),
        out_shape=[jax.ShapeDtypeStruct((groups, rows, 512), BF16)] * 4,
        cost_estimate=pl.CostEstimate(
            flops=groups * 10**7, bytes_accessed=groups * 2000000, transcendentals=0
        ),
        compiler_params=pltpu.CompilerParams(vmem_limit_bytes=24 << 20),
        name="advect",
    )(place, apart, group, face_move, q, low, high, lat, lon, above, *after)


def table_kernel(matrix_ref, mask_ref, order_ref, rain_ref, *refs):
    small_ref, placing_ref, back_ref, wet_ref, all_ref = refs[-5:]
    columns = mask_ref.shape[1]

    @pl.when(pl.program_id(0) == 0)
    def _():
        mask = mask_ref[...]
        order = order_ref[...]
        row = lax.broadcasted_iota(jnp.int32, (columns, columns), 0)
        column = lax.broadcasted_iota(jnp.int32, (columns, columns), 1)
        earlier = jnp.where(row < column, 1.0, 0.0).astype(BF16)
        ones = jnp.where(mask > 0, 1.0, 0.0)
        wide = jnp.broadcast_to(ones, (8, columns)).astype(BF16)
        rank = jnp.dot(wide, earlier, preferred_element_type=F32)[0:1]
        rank = jnp.where(mask > 0, rank, -1.0).astype(jnp.int32)
        slot = lax.broadcasted_iota(jnp.int32, (CAP, columns), 0)
        back = jnp.where(slot == rank, 1.0, 0.0).astype(BF16)
        back_ref[...] = back
        whole = jnp.where(row == order, 1.0, 0.0)
        placing_ref[:, :columns] = jnp.where(mask > 0, 0.0, whole).astype(BF16)
        placing_ref[:, columns:] = lax.dot_general(
            whole.astype(BF16), back, (((1,), (1,)), ((), ())), preferred_element_type=F32
        ).astype(BF16)
        wet = lax.dot_general(
            rain_ref[...], back, (((1,), (1,)), ((), ())), preferred_element_type=F32
        )
        for tile in range(CAP // 128):
            wet_ref[tile] = wet[:, tile * 128 : (tile + 1) * 128]
        for tile in range(columns // 128):
            all_ref[tile] = rain_ref[:, tile * 128 : (tile + 1) * 128].astype(F32)

    small = lax.dot_general(
        matrix_ref[...], back_ref[...], (((1,), (1,)), ((), ())), preferred_element_type=F32
    )
    for tile in range(CAP // 128):
        small_ref[tile] = small[:, tile * 128 : (tile + 1) * 128]


def tables(matrix, mask, order, rain, after):
    rows, columns = matrix.shape
    levels = rain.shape[0]
    steps = 9
    whole = lambda *shape: pl.BlockSpec(shape, lambda i: (0,) * len(shape))
    return pl.pallas_call(
        table_kernel,
        grid=(steps,),
        in_specs=[
            pl.BlockSpec((rows // steps, columns), lambda i: (i, 0)),
            whole(1, columns),
            whole(1, columns),
            whole(levels, columns),
        ]
        + [pl.BlockSpec(memory_space=pl.ANY)] * len(after),
        out_specs=[
            pl.BlockSpec((CAP // 128, rows // steps, 128), lambda i: (0, i, 0)),
            whole(columns, columns + CAP),
            whole(CAP, columns),
            whole(CAP // 128, levels, 128),
            whole(columns // 128, levels, 128),
        ],
        out_shape=[
            jax.ShapeDtypeStruct((CAP // 128, rows, 128), F32),
            jax.ShapeDtypeStruct((columns, columns + CAP), BF16),
            jax.ShapeDtypeStruct((CAP, columns), BF16),
            jax.ShapeDtypeStruct((CAP // 128, levels, 128), F32),
            jax.ShapeDtypeStruct((columns // 128, levels, 128), F32),
        ],
        cost_estimate=pl.CostEstimate(
            flops=2 * rows * columns * CAP, bytes_accessed=12 * 10**6, transcendentals=0
        ),
        compiler_params=pltpu.CompilerParams(vmem_limit_bytes=24 << 20),
        name="tables",
    )(matrix, mask, order, rain, *after)


def physics_kernel(
    place_ref,
    part0_ref,
    part1_ref,
    part2_ref,
    part3_ref,
    placing_ref,
    back_ref,
    matrix_ref,
    rain_ref,
    wet_ref,
    rate_ref,
    *refs,
):
    out_ref, dry, moist, turned, held = refs[-5:]
    groups, rows, columns = part0_ref.shape
    levels = matrix_ref.shape[1]
    tiles = CAP // 128
    rates = [rate_ref[g] for g in range(groups)]

    for shift, part in enumerate((part0_ref, part1_ref, part2_ref, part3_ref)):
        source = lax.rem(place_ref[0] + (4 - shift), 4)
        base = pl.multiple_of(source * rows, 8)
        for g in range(groups):
            placed = product(part[g], placing_ref[...])
            dry[g, pl.ds(base, rows), :] = placed[:, :columns]
            for tile in range(tiles):
                at = columns + tile * 128
                moist[g, tile, pl.ds(base, rows), :] = placed[:, at : at + 128]

    def contract(step, carry):
        block, tile = step // tiles, step % tiles
        first = block * K_BLOCK
        sums = [[jnp.zeros((GROUP, 128), F32)] * K_BLOCK for _ in range(groups)]
        for e in range(levels):
            values = [moist[g, tile, e * GROUP : (e + 1) * GROUP, :] for g in range(groups)]
            for k in range(K_BLOCK):
                weight = matrix_ref[tile, first + k, pl.ds(e, GROUP, stride=0), :]
                for g in range(groups):
                    sums[g][k] = sums[g][k] + weight * values[g]
        wets = [wet_ref[tile, pl.ds(first + k, GROUP, stride=0), :] for k in range(K_BLOCK)]
        spot = pl.multiple_of(first * GROUP, GROUP * K_BLOCK)
        for g in range(groups):
            washed = [sums[g][k] * jnp.exp(-rates[g] * wets[k]) for k in range(K_BLOCK)]
            turned[g, tile, pl.ds(spot, GROUP * K_BLOCK), :] = jnp.concatenate(
                washed, axis=0
            ).astype(BF16)
        return carry

    lax.fori_loop(0, levels // K_BLOCK * tiles, contract, 0)

    some = 24

    def finish(block, carry):
        first = block * some
        spot = pl.multiple_of(first * GROUP, GROUP * some)
        for g in range(groups):
            spread = sum(
                product(
                    turned[g, tile, pl.ds(spot, GROUP * some), :],
                    back_ref[tile * 128 : (tile + 1) * 128],
                )
                for tile in range(tiles)
            )
            for k in range(some):
                for tile in range(columns // 128):
                    lanes = slice(tile * 128, (tile + 1) * 128)
                    wet = rain_ref[tile, pl.ds(first + k, GROUP, stride=0), :]
                    plain = dry[g, pl.ds(spot + k * GROUP, GROUP), lanes]
                    held[tile, pl.ds(g * GROUP * levels + first + k, GROUP, stride=levels), :] = (
                        spread[k * GROUP : (k + 1) * GROUP, lanes] + plain * jnp.exp(-rates[g] * wet)
                    )
        return carry

    lax.fori_loop(0, levels // some, finish, 0)
    for tile in range(columns // 128):
        out_ref[:, tile * 128 : (tile + 1) * 128] = held[tile].astype(BF16)


def physics(place, parts, placing, back, matrix, rain, wet, rates, first, groups, after):
    rows, columns = parts[0].shape[1:]
    levels = rain.shape[1]
    flops = groups * 2 * GROUP * levels * (columns * (columns + 2 * CAP) + levels * CAP * 20)
    return pl.pallas_call(
        physics_kernel,
        grid_spec=pltpu.PrefetchScalarGridSpec(
            num_scalar_prefetch=1,
            grid=(1,),
            in_specs=[whole_block(groups, rows, columns)] * 4
            + [whole_block(*x.shape) for x in (placing, back, matrix, rain, wet)]
            + [pl.BlockSpec((groups, GROUP, 128), lambda i, p: (first // groups, 0, 0))]
            + [pl.BlockSpec(memory_space=pl.ANY)] * len(after),
            out_specs=whole_block(groups * GROUP * levels, columns),
            scratch_shapes=[
                pltpu.VMEM((groups, levels * GROUP, columns), F32),
                pltpu.VMEM((groups, CAP // 128, levels * GROUP, 128), F32),
                pltpu.VMEM((groups, CAP // 128, levels * GROUP, 128), BF16),
                pltpu.VMEM((columns // 128, groups * GROUP * levels, 128), F32),
            ],
        ),
        out_shape=jax.ShapeDtypeStruct((groups * GROUP * levels, columns), BF16),
        cost_estimate=pl.CostEstimate(
            flops=flops, bytes_accessed=groups * 1200000 + 6500000, transcendentals=0
        ),
        compiler_params=pltpu.CompilerParams(vmem_limit_bytes=32 << 20),
        name="physics",
    )(place, *parts, placing, back, matrix, rain, wet, rates, *after)


def choose_kernel(flag_ref, own_ref, partner_ref, *refs):
    out_ref = refs[-1]

    @pl.when(flag_ref[0] > 0)
    def _():
        out_ref[...] = partner_ref[...]

    @pl.when(flag_ref[0] <= 0)
    def _():
        out_ref[...] = own_ref[...]


def choose(flag, own, partner, whole, shape, first, groups, after):
    rows = shape[0] // (2 * sum(CHUNKS))
    columns = shape[1]
    operands = [own, partner]
    specs = [
        pl.BlockSpec((rows, columns), lambda g, f: (jnp.where(f[0] > 0, 0, g), 0)),
        pl.BlockSpec((rows, columns), lambda g, f: (jnp.where(f[0] > 0, g, 0), 0)),
    ]
    aliases = {}
    if whole is not None:
        operands.append(whole)
        specs.append(pl.BlockSpec(memory_space=pl.ANY))
        aliases = {3: 0}
    operands += after
    specs += [pl.BlockSpec(memory_space=pl.ANY)] * len(after)
    return pl.pallas_call(
        choose_kernel,
        grid_spec=pltpu.PrefetchScalarGridSpec(
            num_scalar_prefetch=1,
            grid=(2 * groups,),
            in_specs=specs,
            out_specs=pl.BlockSpec((rows, columns), lambda g, f: (g + 2 * first, 0)),
        ),
        out_shape=jax.ShapeDtypeStruct(shape, BF16),
        input_output_aliases=aliases,
        cost_estimate=pl.CostEstimate(
            flops=0, bytes_accessed=groups * 1200000, transcendentals=0
        ),
        compiler_params=pltpu.CompilerParams(vmem_limit_bytes=16 << 20),
        name="choose",
    )(flag, *operands)


def shifted(value, axis, steps):
    count = lax.axis_size(axis)
    pairs = [(i, i + steps) for i in range(count) if 0 <= i + steps < count]
    return lax.ppermute(value, axis, pairs)


def turned(value, axis, steps):
    count = lax.axis_size(axis)
    return lax.ppermute(value, axis, [(i, (i + steps) % count) for i in range(count)])


def paired(value, axis):
    count = lax.axis_size(axis)
    return lax.ppermute(value, axis, [(i, i ^ (count // 2)) for i in range(count)])


def tiled_rows(value):
    lead = value.shape[:-2]
    lats, lons = value.shape[-2:]
    split = value.reshape(*lead, lats, lons // 128, 128)
    return jnp.swapaxes(split, -3, -2).reshape(*lead, lats * lons // 128, 128)


def local(
    tracer_dyn,
    courant_lat,
    courant_lon,
    conv_matrix,
    conv_mask,
    column_order,
    rain,
    scav_rate,
    pair_flag,
):
    n_lat = lax.axis_size("lat")
    n_lev = lax.axis_size("lev")
    tracers = tracer_dyn.shape[0]
    levels, columns = rain.shape
    lev_place = lax.axis_index("lev")
    place = lev_place.astype(jnp.int32).reshape(1)
    pair_index = lax.axis_index("lat") % (n_lat // 2) * n_lev + lev_place
    flag = lax.dynamic_slice_in_dim(pair_flag, pair_index, 1)
    rates = jnp.broadcast_to(
        scav_rate.reshape(tracers // GROUP, GROUP, 1), (tracers // GROUP, GROUP, 128)
    )

    q = pltpu.with_memory_space_constraint(tiled_rows(tracer_dyn), pltpu.HBM)
    lat, lon = tiled_rows(courant_lat), tiled_rows(courant_lon)
    apart, group, face_move = deinterleave(), regroup(n_lev), face_rows(lat.shape[0])
    firsts = [sum(CHUNKS[:number]) for number in range(len(CHUNKS))]
    halos, sections, owns, partners, made = {}, {}, {}, {}, {}
    out = last = None
    for kind, number in ORDER:
        after = [] if last is None else [last]
        if kind == "extract":
            north, south = extract(apart, face_move, q, lat, *SPANS[number], after)
            last = north
            halos[number] = (shifted(north, "lat", 1), shifted(south, "lat", -1))
        elif kind == "tables":
            made = tables(
                conv_matrix.reshape(levels * levels, columns),
                conv_mask.reshape(1, columns),
                column_order.reshape(1, columns),
                rain,
                after,
            )
            last = made[2]
        elif kind == "advect":
            first, groups = firsts[number], CHUNKS[number]
            span = max(i for i in range(len(SPANS)) if SPANS[i][0] <= first)
            parts = advect(
                place, apart, group, face_move, q, *halos[span], lat, lon, halos[0][1],
                first, first - SPANS[span][0], groups, after,
            )
            last = parts[0]
            sections[number] = [parts[0]] + [turned(parts[s], "lev", s) for s in range(1, n_lev)]
        elif kind == "physics":
            small, placing, back, wet, wet_all = made
            small = small.reshape(CAP // 128, levels, levels, 128)
            own = physics(
                place, sections[number], placing, back, small, wet_all, wet, rates,
                firsts[number], CHUNKS[number], after,
            )
            last = owns[number] = own
            partners[number] = paired(own, "lat")
        else:
            out = choose(
                flag, owns[number], partners[number], out, (tracers * levels, columns),
                firsts[number], CHUNKS[number], after,
            )
    return out.reshape(tracers, levels, columns)


def solution(mesh):
    placed = (
        P(None, "lev", "lat", None),
        P("lev", "lat", None),
        P("lev", "lat", None),
        P(None, None, ("lat", "lev")),
        P(("lat", "lev")),
        P(("lat", "lev")),
        P(None, ("lat", "lev")),
        P(),
        P(),
    )
    return jax.shard_map(
        local, mesh=mesh, in_specs=placed, out_specs=P(None, None, ("lat", "lev")), check_vma=False
    )
```

```python
import functools

import jax
import jax.numpy as jnp
from jax import lax
from jax.experimental import pallas as pl
from jax.experimental.pallas import tpu as pltpu
from jax.sharding import PartitionSpec as P


GROUP = 8
CHUNKS = (1, 1, 2, 2, 2)
SPANS = ((0, 1), (1, 3), (4, 4))
ORDER = (
    ("extract", 0),
    ("extract", 1),
    ("advect", 0),
    ("tables", 0),
    ("advect", 1),
    ("physics", 0),
    ("extract", 2),
    ("advect", 2),
    ("physics", 1),
    ("advect", 3),
    ("physics", 2),
    ("advect", 4),
    ("physics", 3),
    ("physics", 4),
    ("choose", 0),
    ("choose", 1),
    ("choose", 2),
    ("choose", 3),
    ("choose", 4),
)
CAP = 256
K_BLOCK = 8
F32 = jnp.float32
BF16 = jnp.bfloat16


def ones_where(row_target, columns):
    column = lax.broadcasted_iota(jnp.int32, (row_target.shape[0], columns), 1)
    return jnp.where(column == row_target, 1.0, 0.0).astype(BF16)


def deinterleave():
    row = lax.broadcasted_iota(jnp.int32, (256, 256), 0)
    level, lat, tracer, tile = row >> 7, (row >> 6) & 1, (row >> 3) & 7, row & 7
    return ones_where((((tracer * 2 + level) * 8) + tile) * 2 + lat, 256)


def regroup(place):
    row = lax.broadcasted_iota(jnp.int32, (256, 256), 0)
    target = ((row >> 6) + place) & 3
    lat, half, level, tracer = (row >> 5) & 1, (row >> 4) & 1, (row >> 3) & 1, row & 7
    return ones_where(((level * 2 + lat) * 8 + tracer) * 8 + 2 * target + half, 256)


def face_rows(rows, lats):
    row = lax.broadcasted_iota(jnp.int32, (lats * rows, 2 * rows), 0)
    lat = (row >= rows).astype(jnp.int32)
    return ones_where(2 * (row - lat * rows) + lat, 2 * rows)


def product(a, b):
    return jnp.dot(a, b, preferred_element_type=F32)


def two_levels(q_ref, pair):
    return q_ref[:, pl.ds(2 * pair, 2)].reshape(2 * GROUP * 16, 128)


def extract_kernel(q_ref, lat_ref, *refs):
    north_ref, south_ref, apart_ref = refs[-3:]
    levels = q_ref.shape[1]
    rows = levels * GROUP * 8

    @pl.when(pl.program_id(0) == 0)
    def _():
        apart_ref[...] = deinterleave()

    for pair in range(levels // 2):
        apart = product(apart_ref[...], two_levels(q_ref, pair)).astype(BF16)
        for k in range(2):
            spot = pair * 128 + k * 64
            south_ref[0, spot : spot + 64, :] = apart[k * 128 : k * 128 + 64]
            north_ref[0, spot : spot + 64, :] = apart[k * 128 + 64 : k * 128 + 128]
    if south_ref.shape[1] > rows:
        faces = lat_ref[...].reshape(levels * 16, 128)
        south_ref[0, rows:, :] = product(face_rows(levels * 8, 1), faces).astype(BF16)


def whole_block(*shape):
    return pl.BlockSpec(shape, lambda *_: (0,) * len(shape))


def extract(q, lat, first, groups, after):
    levels = q.shape[1]
    rows = levels * GROUP * 8
    extra = levels * 8 if first == 0 else 0
    return pl.pallas_call(
        extract_kernel,
        grid=(groups,),
        in_specs=[
            pl.BlockSpec((GROUP, levels, 16, 128), lambda g: (g + first, 0, 0, 0)),
            whole_block(*lat.shape),
        ]
        + [pl.BlockSpec(memory_space=pl.ANY)] * len(after),
        out_specs=[
            pl.BlockSpec((1, rows, 128), lambda g: (g, 0, 0)),
            pl.BlockSpec((1, rows + extra, 128), lambda g: (g, 0, 0)),
        ],
        scratch_shapes=[pltpu.VMEM((256, 256), BF16)],
        out_shape=[
            jax.ShapeDtypeStruct((groups, rows, 128), BF16),
            jax.ShapeDtypeStruct((groups, rows + extra, 128), BF16),
        ],
        cost_estimate=pl.CostEstimate(
            flops=groups * 10**6, bytes_accessed=groups * 1200000, transcendentals=0
        ),
        compiler_params=pltpu.CompilerParams(vmem_limit_bytes=16 << 20),
        name="extract",
    )(q, lat, *after)


def beside(x, lane, toward_east):
    if toward_east:
        turned = pltpu.roll(x, 127, 1)
        return jnp.where(lane == 127, pltpu.roll(turned, 7, 0), turned)
    turned = pltpu.roll(x, 1, 1)
    return jnp.where(lane == 0, pltpu.roll(turned, 1, 0), turned)


def advect_kernel(
    place_ref, q_ref, low_ref, high_ref, lat_ref, lon_ref, above_ref, *refs
):
    outs = refs[-10:-6]
    faces, apart_ref, group_ref, apart, made, edges = refs[-6:]
    levels = q_ref.shape[1]
    lane = lax.broadcasted_iota(jnp.int32, (8, 128), 1)

    @pl.when(pl.program_id(0) == 0)
    def _():
        apart_ref[...] = deinterleave()
        group_ref[...] = regroup(place_ref[0])
        move = face_rows(levels * 8, 2)
        for at, ref in ((0, lat_ref), (2, lon_ref)):
            both = product(move, ref[...].reshape(levels * 16, 128))
            faces[at] = both[: levels * 8]
            faces[at + 1] = both[levels * 8 :]
        faces[4] = above_ref[0].astype(F32)

    for pair in range(levels // 2):
        apart[pair] = product(apart_ref[...], two_levels(q_ref, pair))
    edges[0] = low_ref[0].astype(F32)
    edges[1] = high_ref[0].astype(F32)

    def body(pair, carry):
        for k in range(2):
            at = pl.ds(pl.multiple_of((2 * pair + k) * 8, 8), 8)
            edge = [faces[0, at, :], faces[1, at, :], faces[4, at, :]]
            terms = []
            for lat in range(2):
                south, north, west = edge[lat], edge[lat + 1], faces[2 + lat, at, :]
                east = beside(west, lane, True)
                own = (
                    1.0
                    - (jnp.maximum(north, 0.0) - jnp.minimum(south, 0.0))
                    - (jnp.maximum(east, 0.0) - jnp.minimum(west, 0.0))
                )
                terms.append(
                    (
                        own,
                        jnp.maximum(south, 0.0),
                        -jnp.minimum(north, 0.0),
                        jnp.maximum(west, 0.0),
                        -jnp.minimum(east, 0.0),
                    )
                )
            results = [[], []]
            for t in range(GROUP):
                rows = [
                    apart[pair, (k * 2 + lat) * 64 + t * 8 : (k * 2 + lat) * 64 + t * 8 + 8, :]
                    for lat in range(2)
                ]
                spot = pl.multiple_of(pair * 128 + (k * 64 + t * 8), 8)
                column = [edges[0, pl.ds(spot, 8), :], *rows, edges[1, pl.ds(spot, 8), :]]
                for lat in range(2):
                    own, from_s, from_n, from_w, from_e = terms[lat]
                    results[lat].append(
                        own * rows[lat]
                        + (from_s * column[lat] + from_n * column[lat + 2])
                        + (
                            from_w * beside(rows[lat], lane, False)
                            + from_e * beside(rows[lat], lane, True)
                        )
                    )
            for lat in range(2):
                row = (k * 2 + lat) * 64
                made[pair, row : row + 64, :] = jnp.concatenate(results[lat], axis=0).astype(BF16)
        return carry

    lax.fori_loop(0, levels // 2, body, 0)
    for pair in range(levels // 2):
        sent = product(group_ref[...], made[pair]).astype(BF16)
        for shift, out in enumerate(outs):
            for quarter in range(4):
                row = (shift * 4 + quarter) * 16
                lanes = slice(quarter * 128, (quarter + 1) * 128)
                out[0, pair * 16 : pair * 16 + 16, lanes] = sent[row : row + 16]


def advect(
    place, q, low, high, lat, lon, above, first, halo_first, groups, after
):
    levels = q.shape[1]
    rows = levels * GROUP
    halo = pl.BlockSpec((1, rows * 8, 128), lambda g, p: (g + halo_first, 0, 0))
    return pl.pallas_call(
        advect_kernel,
        grid_spec=pltpu.PrefetchScalarGridSpec(
            num_scalar_prefetch=1,
            grid=(groups,),
            in_specs=[
                pl.BlockSpec((GROUP, levels, 16, 128), lambda g, p: (g + first, 0, 0, 0)),
                halo,
                halo,
                whole_block(*lat.shape),
                whole_block(*lon.shape),
                pl.BlockSpec((1, levels * 8, 128), lambda g, p: (0, GROUP, 0)),
            ]
            + [pl.BlockSpec(memory_space=pl.ANY)] * len(after),
            out_specs=[pl.BlockSpec((1, rows, 512), lambda g, p: (g, 0, 0))] * 4,
            scratch_shapes=[
                pltpu.VMEM((5, levels * 8, 128), F32),
                pltpu.VMEM((256, 256), BF16),
                pltpu.VMEM((256, 256), BF16),
                pltpu.VMEM((levels // 2, 256, 128), F32),
                pltpu.VMEM((levels // 2, 256, 128), BF16),
                pltpu.VMEM((2, rows * 8, 128), F32),
            ],
        ),
        out_shape=[jax.ShapeDtypeStruct((groups, rows, 512), BF16)] * 4,
        cost_estimate=pl.CostEstimate(
            flops=groups * 10**7, bytes_accessed=groups * 2000000, transcendentals=0
        ),
        compiler_params=pltpu.CompilerParams(vmem_limit_bytes=24 << 20),
        name="advect",
    )(place, q, low, high, lat, lon, above, *after)


def table_kernel(matrix_ref, mask_ref, order_ref, rain_ref, *refs):
    small_ref, placing_ref, back_ref, wet_ref, all_ref = refs[-5:]
    columns = mask_ref.shape[1]

    @pl.when(pl.program_id(0) == 0)
    def _():
        mask = mask_ref[...]
        order = order_ref[...]
        row = lax.broadcasted_iota(jnp.int32, (columns, columns), 0)
        column = lax.broadcasted_iota(jnp.int32, (columns, columns), 1)
        earlier = jnp.where(row < column, 1.0, 0.0).astype(BF16)
        ones = jnp.where(mask > 0, 1.0, 0.0)
        wide = jnp.broadcast_to(ones, (8, columns)).astype(BF16)
        rank = jnp.dot(wide, earlier, preferred_element_type=F32)[0:1]
        rank = jnp.where(mask > 0, rank, -1.0).astype(jnp.int32)
        slot = lax.broadcasted_iota(jnp.int32, (CAP, columns), 0)
        back = jnp.where(slot == rank, 1.0, 0.0).astype(BF16)
        back_ref[...] = back
        whole = jnp.where(row == order, 1.0, 0.0)
        placing_ref[:, :columns] = jnp.where(mask > 0, 0.0, whole).astype(BF16)
        placing_ref[:, columns:] = lax.dot_general(
            whole.astype(BF16), back, (((1,), (1,)), ((), ())), preferred_element_type=F32
        ).astype(BF16)
        wet = lax.dot_general(
            rain_ref[...], back, (((1,), (1,)), ((), ())), preferred_element_type=F32
        )
        for tile in range(CAP // 128):
            wet_ref[tile] = wet[:, tile * 128 : (tile + 1) * 128]
        for tile in range(columns // 128):
            all_ref[tile] = rain_ref[:, tile * 128 : (tile + 1) * 128].astype(F32)

    small = lax.dot_general(
        matrix_ref[...], back_ref[...], (((1,), (1,)), ((), ())), preferred_element_type=F32
    )
    for tile in range(CAP // 128):
        small_ref[tile] = small[:, tile * 128 : (tile + 1) * 128]


def tables(matrix, mask, order, rain, after):
    rows, columns = matrix.shape
    levels = rain.shape[0]
    steps = 9
    whole = lambda *shape: pl.BlockSpec(shape, lambda i: (0,) * len(shape))
    return pl.pallas_call(
        table_kernel,
        grid=(steps,),
        in_specs=[
            pl.BlockSpec((rows // steps, columns), lambda i: (i, 0)),
            whole(1, columns),
            whole(1, columns),
            whole(levels, columns),
        ]
        + [pl.BlockSpec(memory_space=pl.ANY)] * len(after),
        out_specs=[
            pl.BlockSpec((CAP // 128, rows // steps, 128), lambda i: (0, i, 0)),
            whole(columns, columns + CAP),
            whole(CAP, columns),
            whole(CAP // 128, levels, 128),
            whole(columns // 128, levels, 128),
        ],
        out_shape=[
            jax.ShapeDtypeStruct((CAP // 128, rows, 128), F32),
            jax.ShapeDtypeStruct((columns, columns + CAP), BF16),
            jax.ShapeDtypeStruct((CAP, columns), BF16),
            jax.ShapeDtypeStruct((CAP // 128, levels, 128), F32),
            jax.ShapeDtypeStruct((columns // 128, levels, 128), F32),
        ],
        cost_estimate=pl.CostEstimate(
            flops=2 * rows * columns * CAP, bytes_accessed=12 * 10**6, transcendentals=0
        ),
        compiler_params=pltpu.CompilerParams(vmem_limit_bytes=24 << 20),
        name="tables",
    )(matrix, mask, order, rain, *after)


def physics_kernel(
    place_ref,
    part0_ref,
    part1_ref,
    part2_ref,
    part3_ref,
    placing_ref,
    back_ref,
    matrix_ref,
    rain_ref,
    wet_ref,
    rate_ref,
    *refs,
):
    out_ref, dry, moist, turned, held = refs[-5:]
    groups, rows, columns = part0_ref.shape
    levels = matrix_ref.shape[1]
    tiles = CAP // 128
    rates = [rate_ref[g] for g in range(groups)]

    for shift, part in enumerate((part0_ref, part1_ref, part2_ref, part3_ref)):
        source = lax.rem(place_ref[0] + (4 - shift), 4)
        base = pl.multiple_of(source * rows, 8)
        for g in range(groups):
            placed = product(part[g], placing_ref[...])
            dry[g, pl.ds(base, rows), :] = placed[:, :columns]
            for tile in range(tiles):
                at = columns + tile * 128
                moist[g, tile, pl.ds(base, rows), :] = placed[:, at : at + 128]

    def contract(step, carry):
        block, tile = step // tiles, step % tiles
        first = block * K_BLOCK
        sums = [[jnp.zeros((GROUP, 128), F32)] * K_BLOCK for _ in range(groups)]
        for e in range(levels):
            values = [moist[g, tile, e * GROUP : (e + 1) * GROUP, :] for g in range(groups)]
            for k in range(K_BLOCK):
                weight = matrix_ref[tile, first + k, pl.ds(e, GROUP, stride=0), :]
                for g in range(groups):
                    sums[g][k] = sums[g][k] + weight * values[g]
        wets = [wet_ref[tile, pl.ds(first + k, GROUP, stride=0), :] for k in range(K_BLOCK)]
        spot = pl.multiple_of(first * GROUP, GROUP * K_BLOCK)
        for g in range(groups):
            washed = [sums[g][k] * jnp.exp(-rates[g] * wets[k]) for k in range(K_BLOCK)]
            turned[g, tile, pl.ds(spot, GROUP * K_BLOCK), :] = jnp.concatenate(
                washed, axis=0
            ).astype(BF16)
        return carry

    lax.fori_loop(0, levels // K_BLOCK * tiles, contract, 0)

    some = 24

    def finish(block, carry):
        first = block * some
        spot = pl.multiple_of(first * GROUP, GROUP * some)
        for g in range(groups):
            spread = sum(
                product(
                    turned[g, tile, pl.ds(spot, GROUP * some), :],
                    back_ref[tile * 128 : (tile + 1) * 128],
                )
                for tile in range(tiles)
            )
            for k in range(some):
                for tile in range(columns // 128):
                    lanes = slice(tile * 128, (tile + 1) * 128)
                    wet = rain_ref[tile, pl.ds(first + k, GROUP, stride=0), :]
                    plain = dry[g, pl.ds(spot + k * GROUP, GROUP), lanes]
                    held[tile, pl.ds(g * GROUP * levels + first + k, GROUP, stride=levels), :] = (
                        spread[k * GROUP : (k + 1) * GROUP, lanes] + plain * jnp.exp(-rates[g] * wet)
                    )
        return carry

    lax.fori_loop(0, levels // some, finish, 0)
    for tile in range(columns // 128):
        out_ref[:, tile * 128 : (tile + 1) * 128] = held[tile].astype(BF16)


def physics(place, parts, placing, back, matrix, rain, wet, rates, first, groups, after):
    rows, columns = parts[0].shape[1:]
    levels = rain.shape[1]
    flops = groups * 2 * GROUP * levels * (columns * (columns + 2 * CAP) + levels * CAP * 20)
    return pl.pallas_call(
        physics_kernel,
        grid_spec=pltpu.PrefetchScalarGridSpec(
            num_scalar_prefetch=1,
            grid=(1,),
            in_specs=[whole_block(groups, rows, columns)] * 4
            + [whole_block(*x.shape) for x in (placing, back, matrix, rain, wet)]
            + [pl.BlockSpec((groups, GROUP, 128), lambda i, p: (first // groups, 0, 0))]
            + [pl.BlockSpec(memory_space=pl.ANY)] * len(after),
            out_specs=whole_block(groups * GROUP * levels, columns),
            scratch_shapes=[
                pltpu.VMEM((groups, levels * GROUP, columns), F32),
                pltpu.VMEM((groups, CAP // 128, levels * GROUP, 128), F32),
                pltpu.VMEM((groups, CAP // 128, levels * GROUP, 128), BF16),
                pltpu.VMEM((columns // 128, groups * GROUP * levels, 128), F32),
            ],
        ),
        out_shape=jax.ShapeDtypeStruct((groups * GROUP * levels, columns), BF16),
        cost_estimate=pl.CostEstimate(
            flops=flops, bytes_accessed=groups * 1200000 + 6500000, transcendentals=0
        ),
        compiler_params=pltpu.CompilerParams(vmem_limit_bytes=32 << 20),
        name="physics",
    )(place, *parts, placing, back, matrix, rain, wet, rates, *after)


def choose_kernel(flag_ref, own_ref, partner_ref, *refs):
    out_ref = refs[-1]

    @pl.when(flag_ref[0] > 0)
    def _():
        out_ref[...] = partner_ref[...]

    @pl.when(flag_ref[0] <= 0)
    def _():
        out_ref[...] = own_ref[...]


def choose(flag, own, partner, whole, shape, first, groups, after):
    rows = shape[0] // (2 * sum(CHUNKS))
    columns = shape[1]
    operands = [own, partner]
    specs = [
        pl.BlockSpec((rows, columns), lambda g, f: (jnp.where(f[0] > 0, 0, g), 0)),
        pl.BlockSpec((rows, columns), lambda g, f: (jnp.where(f[0] > 0, g, 0), 0)),
    ]
    aliases = {}
    if whole is not None:
        operands.append(whole)
        specs.append(pl.BlockSpec(memory_space=pl.ANY))
        aliases = {3: 0}
    operands += after
    specs += [pl.BlockSpec(memory_space=pl.ANY)] * len(after)
    return pl.pallas_call(
        choose_kernel,
        grid_spec=pltpu.PrefetchScalarGridSpec(
            num_scalar_prefetch=1,
            grid=(2 * groups,),
            in_specs=specs,
            out_specs=pl.BlockSpec((rows, columns), lambda g, f: (g + 2 * first, 0)),
        ),
        out_shape=jax.ShapeDtypeStruct(shape, BF16),
        input_output_aliases=aliases,
        cost_estimate=pl.CostEstimate(
            flops=0, bytes_accessed=groups * 1200000, transcendentals=0
        ),
        compiler_params=pltpu.CompilerParams(vmem_limit_bytes=16 << 20),
        name="choose",
    )(flag, *operands)


def shifted(value, axis, steps):
    count = lax.axis_size(axis)
    pairs = [(i, i + steps) for i in range(count) if 0 <= i + steps < count]
    return lax.ppermute(value, axis, pairs)


def turned(value, axis, steps):
    count = lax.axis_size(axis)
    return lax.ppermute(value, axis, [(i, (i + steps) % count) for i in range(count)])


def paired(value, axis):
    count = lax.axis_size(axis)
    return lax.ppermute(value, axis, [(i, i ^ (count // 2)) for i in range(count)])


def tiled_rows(value):
    lead = value.shape[:-2]
    lats, lons = value.shape[-2:]
    split = value.reshape(*lead, lats, lons // 128, 128)
    return jnp.swapaxes(split, -3, -2).reshape(*lead, lats * lons // 128, 128)


def local(
    tracer_dyn,
    courant_lat,
    courant_lon,
    conv_matrix,
    conv_mask,
    column_order,
    rain,
    scav_rate,
    pair_flag,
):
    n_lat = lax.axis_size("lat")
    n_lev = lax.axis_size("lev")
    tracers = tracer_dyn.shape[0]
    levels, columns = rain.shape
    lev_place = lax.axis_index("lev")
    place = lev_place.astype(jnp.int32).reshape(1)
    pair_index = lax.axis_index("lat") % (n_lat // 2) * n_lev + lev_place
    flag = lax.dynamic_slice_in_dim(pair_flag, pair_index, 1)
    rates = jnp.broadcast_to(
        scav_rate.reshape(tracers // GROUP, GROUP, 1), (tracers // GROUP, GROUP, 128)
    )

    in_hbm = functools.partial(pltpu.with_memory_space_constraint, memory_space=pltpu.HBM)
    q = in_hbm(tiled_rows(tracer_dyn))
    lat, lon = in_hbm(tiled_rows(courant_lat)), in_hbm(tiled_rows(courant_lon))
    firsts = [sum(CHUNKS[:number]) for number in range(len(CHUNKS))]
    halos, sections, owns, partners, made = {}, {}, {}, {}, {}
    out = last = None
    for kind, number in ORDER:
        after = [] if last is None else [last]
        if kind == "extract":
            north, south = extract(q, lat, *SPANS[number], after)
            last = north
            high = shifted(south, "lat", -1)
            low = shifted(north, "lat", 1)
            halos[number] = (low, high)
        elif kind == "tables":
            made = tables(
                in_hbm(conv_matrix.reshape(levels * levels, columns)),
                in_hbm(conv_mask.reshape(1, columns)),
                in_hbm(column_order.reshape(1, columns)),
                in_hbm(rain),
                after,
            )
            last = made[2]
        elif kind == "advect":
            first, groups = firsts[number], CHUNKS[number]
            span = max(i for i in range(len(SPANS)) if SPANS[i][0] <= first)
            parts = advect(
                place, q, *halos[span], lat, lon, halos[0][1],
                first, first - SPANS[span][0], groups, after,
            )
            parts = list(parts)
            last = parts[0]
            for s in (2, 1, 3):
                parts[s] = turned(parts[s], "lev", s)
            sections[number] = parts
        elif kind == "physics":
            small, placing, back, wet, wet_all = made
            small = small.reshape(CAP // 128, levels, levels, 128)
            own = physics(
                place, sections[number], placing, back, small, wet_all, wet, rates,
                firsts[number], CHUNKS[number], after,
            )
            last = owns[number] = own
            partners[number] = paired(own, "lat")
        else:
            out = choose(
                flag, owns[number], partners[number], out, (tracers * levels, columns),
                firsts[number], CHUNKS[number], after,
            )
    return out.reshape(tracers, levels, columns)


def solution(mesh):
    placed = (
        P(None, "lev", "lat", None),
        P("lev", "lat", None),
        P("lev", "lat", None),
        P(None, None, ("lat", "lev")),
        P(("lat", "lev")),
        P(("lat", "lev")),
        P(None, ("lat", "lev")),
        P(),
        P(),
    )

    return jax.shard_map(
        local, mesh=mesh, in_specs=placed, out_specs=P(None, None, ("lat", "lev")), check_vma=False
    )
```

```python
import functools
import itertools

import jax
import jax.numpy as jnp
import numpy as np
from jax import lax
from jax.experimental import pallas as pl
from jax.experimental.pallas import tpu as pltpu
from jax.sharding import PartitionSpec as P


GROUP = 8
CHUNKS = (1, 1, 2, 2, 1, 1)
SPANS = ((0, 1), (1, 3), (4, 4))
ORDER = (
    ("extract", 0),
    ("extract", 1),
    ("advect", 0),
    ("tables", 0),
    ("advect", 1),
    ("physics", 0),
    ("extract", 2),
    ("advect", 2),
    ("physics", 1),
    ("advect", 3),
    ("physics", 2),
    ("advect", 4),
    ("physics", 3),
    ("advect", 5),
    ("physics", 4),
    ("physics", 5),
    ("choose", 0),
    ("choose", 1),
    ("choose", 2),
    ("choose", 3),
    ("choose", 4),
    ("choose", 5),
)
CAP = 256
K_BLOCK = 8
F32 = jnp.float32
BF16 = jnp.bfloat16


def deinterleave():
    move = np.zeros((256, 256), np.float32)
    for k, a, t, i in itertools.product(range(2), range(2), range(GROUP), range(8)):
        move[((k * 2 + a) * GROUP + t) * 8 + i, ((t * 2 + k) * 8 + i) * 2 + a] = 1
    return jnp.asarray(move, BF16)


def regroup(n_lev):
    move = np.zeros((n_lev, 256, 256), np.float32)
    for j, s, a, h in itertools.product(range(n_lev), range(n_lev), range(2), range(2)):
        tile = 2 * ((j + s) % n_lev) + h
        for k, t in itertools.product(range(2), range(GROUP)):
            row = (((s * 2 + a) * 2 + h) * 2 + k) * GROUP + t
            move[j, row, ((k * 2 + a) * GROUP + t) * 8 + tile] = 1
    return jnp.asarray(move, BF16)


def face_rows(levels):
    rows = levels * 8
    move = np.zeros((2 * rows, 2 * rows), np.float32)
    for a, r in itertools.product(range(2), range(rows)):
        move[a * rows + r, r * 2 + a] = 1
    return jnp.asarray(move, BF16)


def product(a, b):
    return jnp.dot(a, b, preferred_element_type=F32)


def two_levels(q_ref, pair):
    return q_ref[:, 2 * pair : 2 * pair + 2].reshape(2 * GROUP * 16, 128)


def moved_rows(move, blocks):
    moved = []
    for at in range(0, len(blocks), 2):
        some = blocks[at : at + 2]
        both = product(move, jnp.concatenate(some, axis=1))
        moved += [both[:, i * 128 : (i + 1) * 128] for i in range(len(some))]
    return moved


def extract_kernel(apart_ref, face_move_ref, q_ref, lat_ref, *refs):
    north_ref, south_ref = refs[-2:]
    levels = q_ref.shape[1]
    rows = levels * GROUP * 8
    blocks = [two_levels(q_ref, pair) for pair in range(levels // 2)]
    for pair, apart in enumerate(moved_rows(apart_ref[...], blocks)):
        for k in range(2):
            spot = pair * 128 + k * 64
            south_ref[0, spot : spot + 64, :] = apart[k * 128 : k * 128 + 64].astype(BF16)
            north_ref[0, spot : spot + 64, :] = apart[k * 128 + 64 : k * 128 + 128].astype(BF16)
    if south_ref.shape[1] > rows:
        faces = lat_ref[...].reshape(levels * 16, 128)
        south_ref[0, rows:, :] = product(face_move_ref[: levels * 8], faces).astype(BF16)


def whole_block(*shape):
    return pl.BlockSpec(shape, lambda *_: (0,) * len(shape))


def extract(apart, face_move, q, lat, first, groups, after):
    levels = q.shape[1]
    rows = levels * GROUP * 8
    extra = levels * 8 if first == 0 else 0
    return pl.pallas_call(
        extract_kernel,
        grid=(groups,),
        in_specs=[
            whole_block(*apart.shape),
            whole_block(*face_move.shape),
            pl.BlockSpec((GROUP, levels, 16, 128), lambda g: (g + first, 0, 0, 0)),
            whole_block(*lat.shape),
        ]
        + [pl.BlockSpec(memory_space=pl.ANY)] * len(after),
        out_specs=[
            pl.BlockSpec((1, rows, 128), lambda g: (g, 0, 0)),
            pl.BlockSpec((1, rows + extra, 128), lambda g: (g, 0, 0)),
        ],
        out_shape=[
            jax.ShapeDtypeStruct((groups, rows, 128), BF16),
            jax.ShapeDtypeStruct((groups, rows + extra, 128), BF16),
        ],
        cost_estimate=pl.CostEstimate(
            flops=groups * 10**6, bytes_accessed=groups * 1200000, transcendentals=0
        ),
        compiler_params=pltpu.CompilerParams(vmem_limit_bytes=16 << 20),
        name="extract",
    )(apart, face_move, q, lat, *after)


def beside(x, lane, toward_east):
    if toward_east:
        turned = pltpu.roll(x, 127, 1)
        return jnp.where(lane == 127, pltpu.roll(turned, 7, 0), turned)
    turned = pltpu.roll(x, 1, 1)
    return jnp.where(lane == 0, pltpu.roll(turned, 1, 0), turned)


def advect_kernel(
    place_ref, apart_ref, group_ref, face_move_ref, q_ref, low_ref, high_ref, lat_ref, lon_ref,
    above_ref, *refs
):
    outs = refs[-7:-3]
    faces, apart, made = refs[-3:]
    levels = q_ref.shape[1]
    lane = lax.broadcasted_iota(jnp.int32, (8, 128), 1)

    @pl.when(pl.program_id(0) == 0)
    def _():
        blocks = [ref[...].reshape(levels * 16, 128) for ref in (lat_ref, lon_ref)]
        for at, both in enumerate(moved_rows(face_move_ref[...], blocks)):
            faces[2 * at] = both[: levels * 8]
            faces[2 * at + 1] = both[levels * 8 :]
        faces[4] = above_ref[0].astype(F32)

    blocks = [two_levels(q_ref, pair) for pair in range(levels // 2)]
    for pair, rows in enumerate(moved_rows(apart_ref[...], blocks)):
        apart[2 * pair] = rows[:128]
        apart[2 * pair + 1] = rows[128:]

    def body(k, carry):
        at = pl.ds(pl.multiple_of(k * 8, 8), 8)
        edge = [faces[0, at, :], faces[1, at, :], faces[4, at, :]]
        terms = []
        for lat in range(2):
            south, north, west = edge[lat], edge[lat + 1], faces[2 + lat, at, :]
            east = beside(west, lane, True)
            own = (
                1.0
                - (jnp.maximum(north, 0.0) - jnp.minimum(south, 0.0))
                - (jnp.maximum(east, 0.0) - jnp.minimum(west, 0.0))
            )
            terms.append(
                (
                    own,
                    jnp.maximum(south, 0.0),
                    -jnp.minimum(north, 0.0),
                    jnp.maximum(west, 0.0),
                    -jnp.minimum(east, 0.0),
                )
            )
        for t in range(0, GROUP, 2):
            spot = pl.multiple_of(k * 64 + t * 8, 16)
            outer = [ref[0, pl.ds(spot, 16), :].astype(F32) for ref in (low_ref, high_ref)]
            results = [[], []]
            for part in range(2):
                row = (t + part) * 8
                rows = [apart[k, lat * 64 + row : lat * 64 + row + 8, :] for lat in range(2)]
                beyond = [x[part * 8 : part * 8 + 8] for x in outer]
                column = [beyond[0], *rows, beyond[1]]
                for lat in range(2):
                    own, from_s, from_n, from_w, from_e = terms[lat]
                    results[lat].append(
                        own * rows[lat]
                        + (from_s * column[lat] + from_n * column[lat + 2])
                        + (
                            from_w * beside(rows[lat], lane, False)
                            + from_e * beside(rows[lat], lane, True)
                        )
                    )
            for lat in range(2):
                row = lat * 64 + t * 8
                made[k, row : row + 16, :] = jnp.concatenate(results[lat], axis=0).astype(BF16)
        return carry

    lax.fori_loop(0, levels, body, 0)
    blocks = [made[2 * pair : 2 * pair + 2].reshape(256, 128) for pair in range(levels // 2)]
    for pair, sent in enumerate(moved_rows(group_ref[0], blocks)):
        for shift, out in enumerate(outs):
            for quarter in range(4):
                row = (shift * 4 + quarter) * 16
                lanes = slice(quarter * 128, (quarter + 1) * 128)
                out[0, pair * 16 : pair * 16 + 16, lanes] = sent[row : row + 16].astype(BF16)


def advect(
    place, apart, group, face_move, q, low, high, lat, lon, above, first, halo_first, groups, after
):
    levels = q.shape[1]
    rows = levels * GROUP
    halo = pl.BlockSpec((1, rows * 8, 128), lambda g, p: (g + halo_first, 0, 0))
    return pl.pallas_call(
        advect_kernel,
        grid_spec=pltpu.PrefetchScalarGridSpec(
            num_scalar_prefetch=1,
            grid=(groups,),
            in_specs=[
                whole_block(*apart.shape),
                pl.BlockSpec((1, 256, 256), lambda g, p: (p[0], 0, 0)),
                whole_block(*face_move.shape),
                pl.BlockSpec((GROUP, levels, 16, 128), lambda g, p: (g + first, 0, 0, 0)),
                halo,
                halo,
                whole_block(*lat.shape),
                whole_block(*lon.shape),
                pl.BlockSpec((1, levels * 8, 128), lambda g, p: (0, GROUP, 0)),
            ]
            + [pl.BlockSpec(memory_space=pl.ANY)] * len(after),
            out_specs=[pl.BlockSpec((1, rows, 512), lambda g, p: (g, 0, 0))] * 4,
            scratch_shapes=[
                pltpu.VMEM((5, levels * 8, 128), F32),
                pltpu.VMEM((levels, 128, 128), F32),
                pltpu.VMEM((levels, 128, 128), BF16),
            ],
        ),
        out_shape=[jax.ShapeDtypeStruct((groups, rows, 512), BF16)] * 4,
        cost_estimate=pl.CostEstimate(
            flops=groups * 10**7, bytes_accessed=groups * 2000000, transcendentals=0
        ),
        compiler_params=pltpu.CompilerParams(vmem_limit_bytes=24 << 20),
        name="advect",
    )(place, apart, group, face_move, q, low, high, lat, lon, above, *after)


def table_kernel(matrix_ref, mask_ref, order_ref, rain_ref, *refs):
    small_ref, placing_ref, back_ref, wet_ref, all_ref, held, sems = refs[-7:]
    columns = mask_ref.shape[1]
    pieces, rows = held.shape[:2]
    copies = [
        pltpu.make_async_copy(matrix_ref.at[pl.ds(i * rows, rows)], held.at[i], sems.at[i])
        for i in range(pieces)
    ]
    for copy in copies:
        copy.start()

    mask = mask_ref[...]
    order = order_ref[...]
    row = lax.broadcasted_iota(jnp.int32, (columns, columns), 0)
    column = lax.broadcasted_iota(jnp.int32, (columns, columns), 1)
    earlier = jnp.where(row < column, 1.0, 0.0).astype(BF16)
    ones = jnp.where(mask > 0, 1.0, 0.0)
    wide = jnp.broadcast_to(ones, (8, columns)).astype(BF16)
    rank = product(wide, earlier)[0:1]
    rank = jnp.where(mask > 0, rank, -1.0).astype(jnp.int32)
    slot = lax.broadcasted_iota(jnp.int32, (CAP, columns), 0)
    back = jnp.where(slot == rank, 1.0, 0.0).astype(BF16)
    back_ref[...] = back
    whole = jnp.where(row == order, 1.0, 0.0)
    placing_ref[:, :columns] = jnp.where(mask > 0, 0.0, whole).astype(BF16)
    placing_ref[:, columns:] = crossed(whole.astype(BF16), back).astype(BF16)
    wet = crossed(rain_ref[...], back)
    for tile in range(CAP // 128):
        wet_ref[tile] = wet[:, tile * 128 : (tile + 1) * 128]
    for tile in range(columns // 128):
        all_ref[tile] = rain_ref[:, tile * 128 : (tile + 1) * 128].astype(F32)
    for i in range(pieces):
        copies[i].wait()
        small = crossed(held[i], back_ref[...])
        for tile in range(CAP // 128):
            small_ref[tile, i * rows : (i + 1) * rows, :] = small[:, tile * 128 : (tile + 1) * 128]


def crossed(a, b):
    return lax.dot_general(a, b, (((1,), (1,)), ((), ())), preferred_element_type=F32)


def tables(matrix, mask, order, rain, after):
    rows, columns = matrix.shape
    levels = rain.shape[0]
    pieces = 9
    shapes = [
        ((CAP // 128, rows, 128), F32),
        ((columns, columns + CAP), BF16),
        ((CAP, columns), BF16),
        ((CAP // 128, levels, 128), F32),
        ((columns // 128, levels, 128), F32),
    ]
    return pl.pallas_call(
        table_kernel,
        grid=(1,),
        in_specs=[
            pl.BlockSpec(memory_space=pl.ANY),
            whole_block(1, columns),
            whole_block(1, columns),
            whole_block(levels, columns),
        ]
        + [pl.BlockSpec(memory_space=pl.ANY)] * len(after),
        out_specs=[whole_block(*shape) for shape, _ in shapes],
        out_shape=[jax.ShapeDtypeStruct(*x) for x in shapes],
        scratch_shapes=[
            pltpu.VMEM((pieces, rows // pieces, columns), BF16),
            pltpu.SemaphoreType.DMA((pieces,)),
        ],
        cost_estimate=pl.CostEstimate(
            flops=2 * rows * columns * CAP, bytes_accessed=12 * 10**6, transcendentals=0
        ),
        compiler_params=pltpu.CompilerParams(vmem_limit_bytes=24 << 20),
        name="tables",
    )(matrix, mask, order, rain, *after)


def physics_kernel(
    place_ref,
    part0_ref,
    part1_ref,
    part2_ref,
    part3_ref,
    placing_ref,
    back_ref,
    matrix_ref,
    rain_ref,
    wet_ref,
    rate_ref,
    *refs,
):
    out_ref, dry, moist, turned, held = refs[-5:]
    groups, rows, columns = part0_ref.shape
    levels = matrix_ref.shape[1]
    tiles = CAP // 128
    rates = [rate_ref[g] for g in range(groups)]

    for shift, part in enumerate((part0_ref, part1_ref, part2_ref, part3_ref)):
        source = lax.rem(place_ref[0] + (4 - shift), 4)
        base = pl.multiple_of(source * rows, 8)
        for g in range(groups):
            placed = product(part[g], placing_ref[...])
            dry[g, pl.ds(base, rows), :] = placed[:, :columns]
            for tile in range(tiles):
                at = columns + tile * 128
                moist[g, tile, pl.ds(base, rows), :] = placed[:, at : at + 128]

    def contract(step, carry):
        block, tile = step // tiles, step % tiles
        first = block * K_BLOCK
        sums = [[jnp.zeros((GROUP, 128), F32)] * K_BLOCK for _ in range(groups)]
        for e in range(levels):
            values = [moist[g, tile, e * GROUP : (e + 1) * GROUP, :] for g in range(groups)]
            for k in range(K_BLOCK):
                weight = matrix_ref[tile, first + k, pl.ds(e, GROUP, stride=0), :]
                for g in range(groups):
                    sums[g][k] = sums[g][k] + weight * values[g]
        wets = [wet_ref[tile, pl.ds(first + k, GROUP, stride=0), :] for k in range(K_BLOCK)]
        spot = pl.multiple_of(first * GROUP, GROUP * K_BLOCK)
        for g in range(groups):
            washed = [sums[g][k] * jnp.exp(-rates[g] * wets[k]) for k in range(K_BLOCK)]
            turned[g, tile, pl.ds(spot, GROUP * K_BLOCK), :] = jnp.concatenate(
                washed, axis=0
            ).astype(BF16)
        return carry

    lax.fori_loop(0, levels // K_BLOCK * tiles, contract, 0)

    some = 24

    def finish(block, carry):
        first = block * some
        spot = pl.multiple_of(first * GROUP, GROUP * some)
        for g in range(groups):
            spread = sum(
                product(
                    turned[g, tile, pl.ds(spot, GROUP * some), :],
                    back_ref[tile * 128 : (tile + 1) * 128],
                )
                for tile in range(tiles)
            )
            for k in range(some):
                for tile in range(columns // 128):
                    lanes = slice(tile * 128, (tile + 1) * 128)
                    wet = rain_ref[tile, pl.ds(first + k, GROUP, stride=0), :]
                    plain = dry[g, pl.ds(spot + k * GROUP, GROUP), lanes]
                    held[tile, pl.ds(g * GROUP * levels + first + k, GROUP, stride=levels), :] = (
                        spread[k * GROUP : (k + 1) * GROUP, lanes] + plain * jnp.exp(-rates[g] * wet)
                    )
        return carry

    lax.fori_loop(0, levels // some, finish, 0)
    for tile in range(columns // 128):
        out_ref[:, tile * 128 : (tile + 1) * 128] = held[tile].astype(BF16)


def physics(place, parts, placing, back, matrix, rain, wet, rates, first, groups, after):
    rows, columns = parts[0].shape[1:]
    levels = rain.shape[1]
    flops = groups * 2 * GROUP * levels * (columns * (columns + 2 * CAP) + levels * CAP * 20)
    return pl.pallas_call(
        physics_kernel,
        grid_spec=pltpu.PrefetchScalarGridSpec(
            num_scalar_prefetch=1,
            grid=(1,),
            in_specs=[whole_block(groups, rows, columns)] * 4
            + [whole_block(*x.shape) for x in (placing, back, matrix, rain, wet)]
            + [pl.BlockSpec((groups, GROUP, 128), lambda i, p: (first // groups, 0, 0))]
            + [pl.BlockSpec(memory_space=pl.ANY)] * len(after),
            out_specs=whole_block(groups * GROUP * levels, columns),
            scratch_shapes=[
                pltpu.VMEM((groups, levels * GROUP, columns), F32),
                pltpu.VMEM((groups, CAP // 128, levels * GROUP, 128), F32),
                pltpu.VMEM((groups, CAP // 128, levels * GROUP, 128), BF16),
                pltpu.VMEM((columns // 128, groups * GROUP * levels, 128), F32),
            ],
        ),
        out_shape=jax.ShapeDtypeStruct((groups * GROUP * levels, columns), BF16),
        cost_estimate=pl.CostEstimate(
            flops=flops, bytes_accessed=groups * 1200000 + 6500000, transcendentals=0
        ),
        compiler_params=pltpu.CompilerParams(vmem_limit_bytes=32 << 20),
        name="physics",
    )(place, *parts, placing, back, matrix, rain, wet, rates, *after)


def choose_kernel(flag_ref, own_ref, partner_ref, *refs, first):
    out_ref, held, in_sems, out_sems = refs[-4:]
    pieces, rows = held.shape[:2]

    def copied_from(source):
        ins = [
            pltpu.make_async_copy(source.at[pl.ds(i * rows, rows)], held.at[i], in_sems.at[i])
            for i in range(pieces)
        ]
        outs = [
            pltpu.make_async_copy(
                held.at[i], out_ref.at[pl.ds(first + i * rows, rows)], out_sems.at[i]
            )
            for i in range(pieces)
        ]
        for copy in ins:
            copy.start()
        for i in range(pieces):
            ins[i].wait()
            outs[i].start()
        for copy in outs:
            copy.wait()

    @pl.when(flag_ref[0] > 0)
    def _():
        copied_from(partner_ref)

    @pl.when(flag_ref[0] <= 0)
    def _():
        copied_from(own_ref)


def choose(flag, own, partner, whole, shape, first, groups, after):
    rows = shape[0] // sum(CHUNKS)
    pieces = 4 * groups
    operands = [own, partner]
    aliases = {}
    if whole is not None:
        operands.append(whole)
        aliases = {3: 0}
    operands += after
    anywhere = pl.BlockSpec(memory_space=pl.ANY)
    return pl.pallas_call(
        functools.partial(choose_kernel, first=first * rows),
        in_specs=[pl.BlockSpec(memory_space=pltpu.SMEM)] + [anywhere] * len(operands),
        out_specs=anywhere,
        scratch_shapes=[
            pltpu.VMEM((pieces, rows * groups // pieces, shape[1]), BF16),
            pltpu.SemaphoreType.DMA((pieces,)),
            pltpu.SemaphoreType.DMA((pieces,)),
        ],
        out_shape=jax.ShapeDtypeStruct(shape, BF16),
        input_output_aliases=aliases,
        cost_estimate=pl.CostEstimate(
            flops=0, bytes_accessed=groups * 1200000, transcendentals=0
        ),
        compiler_params=pltpu.CompilerParams(vmem_limit_bytes=8 << 20),
        name="choose",
    )(flag, *operands)


def shifted(value, axis, steps):
    count = lax.axis_size(axis)
    pairs = [(i, i + steps) for i in range(count) if 0 <= i + steps < count]
    return lax.ppermute(value, axis, pairs)


def turned(value, axis, steps):
    count = lax.axis_size(axis)
    return lax.ppermute(value, axis, [(i, (i + steps) % count) for i in range(count)])


def paired(value, axis):
    count = lax.axis_size(axis)
    return lax.ppermute(value, axis, [(i, i ^ (count // 2)) for i in range(count)])


def tiled_rows(value):
    lead = value.shape[:-2]
    lats, lons = value.shape[-2:]
    split = value.reshape(*lead, lats, lons // 128, 128)
    return jnp.swapaxes(split, -3, -2).reshape(*lead, lats * lons // 128, 128)


def local(
    tracer_dyn,
    courant_lat,
    courant_lon,
    conv_matrix,
    conv_mask,
    column_order,
    rain,
    scav_rate,
    pair_flag,
):
    n_lat = lax.axis_size("lat")
    n_lev = lax.axis_size("lev")
    tracers = tracer_dyn.shape[0]
    levels, columns = rain.shape
    lev_place = lax.axis_index("lev")
    place = lev_place.astype(jnp.int32).reshape(1)
    pair_index = lax.axis_index("lat") % (n_lat // 2) * n_lev + lev_place
    flag = lax.dynamic_slice_in_dim(pair_flag, pair_index, 1)
    rates = jnp.broadcast_to(
        scav_rate.reshape(tracers // GROUP, GROUP, 1), (tracers // GROUP, GROUP, 128)
    )

    in_hbm = functools.partial(pltpu.with_memory_space_constraint, memory_space=pltpu.HBM)
    q = in_hbm(tiled_rows(tracer_dyn))
    lat, lon = in_hbm(tiled_rows(courant_lat)), in_hbm(tiled_rows(courant_lon))
    firsts = [sum(CHUNKS[:number]) for number in range(len(CHUNKS))]
    apart, group, face_move = (
        in_hbm(x) for x in (deinterleave(), regroup(n_lev), face_rows(lat.shape[0]))
    )
    halos, sections, owns, partners, made = {}, {}, {}, {}, {}
    out = last = None
    for kind, number in ORDER:
        after = [] if last is None else [last]
        if kind == "extract":
            north, south = extract(apart, face_move, q, lat, *SPANS[number], after)
            last = north
            high = shifted(south, "lat", -1)
            low = shifted(north, "lat", 1)
            halos[number] = (low, high)
        elif kind == "tables":
            made = tables(
                in_hbm(conv_matrix.reshape(levels * levels, columns)),
                in_hbm(conv_mask.reshape(1, columns)),
                in_hbm(column_order.reshape(1, columns)),
                in_hbm(rain),
                after,
            )
            last = made[2]
        elif kind == "advect":
            first, groups = firsts[number], CHUNKS[number]
            span = max(i for i in range(len(SPANS)) if SPANS[i][0] <= first)
            parts = advect(
                place, apart, group, face_move, q, *halos[span], lat, lon, halos[0][1],
                first, first - SPANS[span][0], groups, after,
            )
            parts = list(parts)
            last = parts[0]
            for s in (2, 1, 3):
                parts[s] = turned(parts[s], "lev", s)
            sections[number] = parts
        elif kind == "physics":
            small, placing, back, wet, wet_all = made
            small = small.reshape(CAP // 128, levels, levels, 128)
            own = physics(
                place, sections[number], placing, back, small, wet_all, wet, rates,
                firsts[number], CHUNKS[number], after,
            )
            last = owns[number] = own
            partners[number] = paired(own, "lat")
        else:
            out = choose(
                flag, owns[number], partners[number], out, (tracers * levels, columns),
                firsts[number], CHUNKS[number], after,
            )
    return out.reshape(tracers, levels, columns)


def solution(mesh):
    placed = (
        P(None, "lev", "lat", None),
        P("lev", "lat", None),
        P("lev", "lat", None),
        P(None, None, ("lat", "lev")),
        P(("lat", "lev")),
        P(("lat", "lev")),
        P(None, ("lat", "lev")),
        P(),
        P(),
    )

    return jax.shard_map(
        local, mesh=mesh, in_specs=placed, out_specs=P(None, None, ("lat", "lev")), check_vma=False
    )
```

```python
import functools
import itertools

import jax
import jax.numpy as jnp
import numpy as np
from jax import lax
from jax.experimental import pallas as pl
from jax.experimental.pallas import tpu as pltpu
from jax.sharding import PartitionSpec as P


GROUP = 8
CHUNKS = (1, 2, 2, 2, 1)
SPANS = ((0, 1), (1, 2), (3, 5))
ORDER = (
    ("extract", 0),
    ("extract", 1),
    ("advect", 0),
    ("tables", 0),
    ("advect", 1),
    ("physics", 0),
    ("extract", 2),
    ("advect", 2),
    ("physics", 1),
    ("advect", 3),
    ("physics", 2),
    ("advect", 4),
    ("physics", 3),
    ("physics", 4),
    ("choose", 0),
    ("choose", 1),
    ("choose", 2),
    ("choose", 3),
    ("choose", 4),
)
CAP = 256
P_BLOCK = 16
F32 = jnp.float32
BF16 = jnp.bfloat16


def deinterleave():
    move = np.zeros((256, 256), np.float32)
    for k, a, t, i in itertools.product(range(2), range(2), range(GROUP), range(8)):
        move[((k * 2 + a) * GROUP + t) * 8 + i, ((t * 2 + k) * 8 + i) * 2 + a] = 1
    return jnp.asarray(move, BF16)


def face_rows(levels):
    rows = levels * 8
    move = np.zeros((2 * rows, 2 * rows), np.float32)
    for a, r in itertools.product(range(2), range(rows)):
        move[a * rows + r, r * 2 + a] = 1
    return jnp.asarray(move, BF16)


def product(a, b):
    return jnp.dot(a, b, preferred_element_type=F32)


def two_levels(q_ref, pair):
    return q_ref[:, 2 * pair : 2 * pair + 2].reshape(2 * GROUP * 16, 128)


def moved_rows(move, blocks):
    moved = []
    for at in range(0, len(blocks), 2):
        some = blocks[at : at + 2]
        both = product(move, jnp.concatenate(some, axis=1))
        moved += [both[:, i * 128 : (i + 1) * 128] for i in range(len(some))]
    return moved


def extract_kernel(apart_ref, face_move_ref, q_ref, lat_ref, lon_ref, *refs, faces_too):
    outs = refs[-3:] if faces_too else refs[-2:]
    north_ref, south_ref = outs[:2]
    levels = q_ref.shape[1]
    rows = levels * GROUP * 8
    blocks = [two_levels(q_ref, pair) for pair in range(levels // 2)]
    for pair, apart in enumerate(moved_rows(apart_ref[...], blocks)):
        for k in range(2):
            spot = pair * 128 + k * 64
            south_ref[0, spot : spot + 64, :] = apart[k * 128 : k * 128 + 64].astype(BF16)
            north_ref[0, spot : spot + 64, :] = apart[k * 128 + 64 : k * 128 + 128].astype(BF16)
    if south_ref.shape[1] > rows:
        faces = lat_ref[...].reshape(levels * 16, 128)
        south_ref[0, rows:, :] = product(face_move_ref[: levels * 8], faces).astype(BF16)
    if faces_too:

        @pl.when(pl.program_id(0) == 0)
        def _():
            blocks = [ref[...].reshape(levels * 16, 128) for ref in (lat_ref, lon_ref)]
            for at, both in enumerate(moved_rows(face_move_ref[...], blocks)):
                outs[2][2 * at] = both[: levels * 8]
                outs[2][2 * at + 1] = both[levels * 8 :]


def whole_block(*shape, once=False):
    mode = {"pipeline_mode": pl.Buffered(1)} if once else {}
    return pl.BlockSpec(shape, lambda *_: (0,) * len(shape), **mode)


def extract(apart, face_move, q, lat, lon, first, groups, faces_too, after):
    levels = q.shape[1]
    rows = levels * GROUP * 8
    extra = levels * 8 if first == 0 else 0
    faces = (4, levels * 8, 128)
    return pl.pallas_call(
        functools.partial(extract_kernel, faces_too=faces_too),
        grid=(groups,),
        in_specs=[
            whole_block(*apart.shape),
            whole_block(*face_move.shape),
            pl.BlockSpec((GROUP, levels, 16, 128), lambda g: (g + first, 0, 0, 0)),
            whole_block(*lat.shape),
            whole_block(*lon.shape),
        ]
        + [pl.BlockSpec(memory_space=pl.ANY)] * len(after),
        out_specs=[
            pl.BlockSpec((1, rows, 128), lambda g: (g, 0, 0)),
            pl.BlockSpec((1, rows + extra, 128), lambda g: (g, 0, 0)),
        ]
        + [whole_block(*faces)] * faces_too,
        out_shape=[
            jax.ShapeDtypeStruct((groups, rows, 128), BF16),
            jax.ShapeDtypeStruct((groups, rows + extra, 128), BF16),
        ]
        + [jax.ShapeDtypeStruct(faces, F32)] * faces_too,
        cost_estimate=pl.CostEstimate(
            flops=groups * 10**6, bytes_accessed=groups * 1200000, transcendentals=0
        ),
        compiler_params=pltpu.CompilerParams(vmem_limit_bytes=7 << 20),
        name="extract",
    )(apart, face_move, q, lat, lon, *after)


def beside(x, lane, toward_east):
    if toward_east:
        turned = pltpu.roll(x, 127, 1)
        return jnp.where(lane == 127, pltpu.roll(turned, 7, 0), turned)
    turned = pltpu.roll(x, 1, 1)
    return jnp.where(lane == 0, pltpu.roll(turned, 1, 0), turned)


def advect_kernel(
    place_ref, south_ref, north_ref, low_ref, high_ref, faces_ref, above_ref, *refs
):
    outs, made = refs[-5:-1], refs[-1]
    levels = faces_ref.shape[1] // 8
    lane = lax.broadcasted_iota(jnp.int32, (8, 128), 1)

    def body(k, carry):
        at = pl.ds(pl.multiple_of(k * 8, 8), 8)
        edge = [faces_ref[0, at, :], faces_ref[1, at, :], above_ref[0, at, :].astype(F32)]
        terms = []
        for lat in range(2):
            south, north, west = edge[lat], edge[lat + 1], faces_ref[2 + lat, at, :]
            east = beside(west, lane, True)
            own = (
                1.0
                - (jnp.maximum(north, 0.0) - jnp.minimum(south, 0.0))
                - (jnp.maximum(east, 0.0) - jnp.minimum(west, 0.0))
            )
            terms.append(
                (
                    own,
                    jnp.maximum(south, 0.0),
                    -jnp.minimum(north, 0.0),
                    jnp.maximum(west, 0.0),
                    -jnp.minimum(east, 0.0),
                )
            )
        for t in range(0, GROUP, 2):
            spot = pl.multiple_of(k * 64 + t * 8, 16)
            columns = [
                ref[0, pl.ds(spot, 16), :].astype(F32)
                for ref in (low_ref, south_ref, north_ref, high_ref)
            ]
            results = [[], []]
            for part in range(2):
                column = [x[part * 8 : part * 8 + 8] for x in columns]
                rows = column[1:3]
                for lat in range(2):
                    own, from_s, from_n, from_w, from_e = terms[lat]
                    results[lat].append(
                        own * rows[lat]
                        + (from_s * column[lat] + from_n * column[lat + 2])
                        + (
                            from_w * beside(rows[lat], lane, False)
                            + from_e * beside(rows[lat], lane, True)
                        )
                    )
            for lat in range(2):
                spot = pl.multiple_of(k * 128 + (lat * 64 + t * 8), 16)
                made[pl.ds(spot, 16), :] = jnp.concatenate(results[lat], axis=0)
        return carry

    lax.fori_loop(0, levels, body, 0)
    for shift, out in enumerate(outs):
        tile = 2 * lax.rem(place_ref[0] + shift, 4)
        for t, lat, half in itertools.product(range(GROUP), range(2), range(2)):
            start = tile + (lat * 64 + t * 8 + half)
            column = (2 * lat + half) * 128
            out[0, t * levels : (t + 1) * levels, column : column + 128] = made[
                pl.ds(start, levels, stride=128), :
            ].astype(BF16)


def advect(place, south, north, low, high, faces, above, halo_first, groups, after):
    levels = faces.shape[1] // 8
    rows = levels * GROUP
    halo = pl.BlockSpec((1, rows * 8, 128), lambda g: (g + halo_first, 0, 0))
    return pl.pallas_call(
        advect_kernel,
        grid=(groups,),
        in_specs=[
            pl.BlockSpec(memory_space=pltpu.SMEM),
            halo,
            halo,
            halo,
            halo,
            whole_block(*faces.shape),
            pl.BlockSpec((1, levels * 8, 128), lambda g: (0, GROUP, 0)),
        ]
        + [pl.BlockSpec(memory_space=pl.ANY)] * len(after),
        out_specs=[pl.BlockSpec((1, rows, 512), lambda g: (g, 0, 0))] * 4,
        scratch_shapes=[pltpu.VMEM((levels * 128, 128), F32)],
        out_shape=[jax.ShapeDtypeStruct((groups, rows, 512), BF16)] * 4,
        cost_estimate=pl.CostEstimate(
            flops=groups * 10**7, bytes_accessed=groups * 2000000, transcendentals=0
        ),
        compiler_params=pltpu.CompilerParams(vmem_limit_bytes=10 << 20),
        name="advect",
    )(place, south, north, low, high, faces, above, *after)


def table_kernel(matrix_ref, mask_ref, order_ref, rain_ref, *refs):
    small_ref, placing_ref, picking_ref, back_ref, wet_ref, all_ref, held, turned, sems = refs[-9:]
    columns = mask_ref.shape[1]
    levels = rain_ref.shape[0]
    pieces, per_piece = held.shape[:2]
    copies = [
        pltpu.make_async_copy(
            matrix_ref.at[pl.ds(i * per_piece, per_piece)], held.at[i], sems.at[i]
        )
        for i in range(pieces)
    ]
    for copy in copies:
        copy.start()

    mask = mask_ref[...]
    order = order_ref[...]
    row = lax.broadcasted_iota(jnp.int32, (columns, columns), 0)
    column = lax.broadcasted_iota(jnp.int32, (columns, columns), 1)
    earlier = jnp.where(row < column, 1.0, 0.0).astype(BF16)
    ones = jnp.where(mask > 0, 1.0, 0.0)
    wide = jnp.broadcast_to(ones, (8, columns)).astype(BF16)
    rank = product(wide, earlier)[0:1]
    rank = jnp.where(mask > 0, rank, -1.0).astype(jnp.int32)
    slot = lax.broadcasted_iota(jnp.int32, (CAP, columns), 0)
    back = jnp.where(slot == rank, 1.0, 0.0).astype(BF16)
    back_ref[...] = back
    whole = jnp.where(row == order, 1.0, 0.0)
    placing_ref[...] = jnp.where(mask > 0, 0.0, whole).astype(BF16)
    picking_ref[...] = crossed(back, whole.astype(BF16)).astype(BF16)
    rain = rain_ref[...]
    all_ref[...] = rain.astype(F32)
    nothing = jnp.zeros((CAP, 128 - levels), F32)
    wet_ref[...] = jnp.concatenate([crossed(back, rain), nothing], axis=1)
    for piece in range(pieces):
        copies[piece].wait()
        for k in range(per_piece):
            picked = crossed(back_ref[...], held[piece, k])
            turned[pl.ds(k, CAP, stride=per_piece), :] = jnp.concatenate([picked, nothing], axis=1)
        spot = piece * per_piece
        small_ref[:, spot : spot + per_piece, :] = (
            turned[...].reshape(CAP, per_piece, 128).astype(BF16)
        )


def crossed(a, b):
    return lax.dot_general(a, b, (((1,), (1,)), ((), ())), preferred_element_type=F32)


def tables(matrix, mask, order, rain, after):
    levels, _, columns = matrix.shape
    per_piece = 8
    shapes = [
        ((CAP, levels, 128), BF16),
        ((columns, columns), BF16),
        ((CAP, columns), BF16),
        ((CAP, columns), BF16),
        ((CAP, 128), F32),
        ((levels, columns), F32),
    ]
    return pl.pallas_call(
        table_kernel,
        grid=(1,),
        in_specs=[
            pl.BlockSpec(memory_space=pl.ANY),
            whole_block(1, columns),
            whole_block(1, columns),
            whole_block(levels, columns),
        ]
        + [pl.BlockSpec(memory_space=pl.ANY)] * len(after),
        out_specs=[whole_block(*shape, once=True) for shape, _ in shapes],
        out_shape=[jax.ShapeDtypeStruct(*x) for x in shapes],
        scratch_shapes=[
            pltpu.VMEM((levels // per_piece, per_piece, levels, columns), BF16),
            pltpu.VMEM((CAP * per_piece, 128), F32),
            pltpu.SemaphoreType.DMA((levels // per_piece,)),
        ],
        cost_estimate=pl.CostEstimate(
            flops=2 * levels * 128 * columns * CAP, bytes_accessed=12 * 10**6, transcendentals=0
        ),
        compiler_params=pltpu.CompilerParams(vmem_limit_bytes=20 << 20),
        name="tables",
    )(matrix, mask, order, rain, *after)


def physics_kernel(
    place_ref, scav_ref, part0, part1, part2, part3, placing_ref, picking_ref, back_ref,
    matrix_ref, rain_ref, wet_ref, rate_ref, *refs, first
):
    out_ref, columns_in, picked, mixed = refs[-4:]
    groups = part0.shape[0]
    levels = rain_ref.shape[0]
    part = part0.shape[1] // GROUP
    tracers = groups * GROUP

    columns_in[:, levels:, :] = jnp.zeros((tracers, 128 - levels, part0.shape[2]), BF16)
    for place in range(4):

        @pl.when(place_ref[0] == place)
        def _(place=place):
            for shift, ref in enumerate((part0, part1, part2, part3)):
                base = (place - shift) % 4 * part
                for g, t in itertools.product(range(groups), range(GROUP)):
                    columns_in[g * GROUP + t, base : base + part, :] = ref[
                        g, t * part : (t + 1) * part, :
                    ]

    for t in range(tracers):
        picked[t * CAP : (t + 1) * CAP, :] = crossed(picking_ref[...], columns_in[t])

    rate = jnp.concatenate([rate_ref[first + g] for g in range(groups)], axis=0)
    nothing = jnp.zeros((128 - levels, 128), BF16)

    def contract(block, carry):
        for inner in range(P_BLOCK):
            p = block * P_BLOCK + inner
            mine = picked[pl.ds(p, tracers, stride=CAP), :].astype(BF16)
            matrix = jnp.concatenate([matrix_ref[p], nothing], axis=0)
            wet = wet_ref[pl.ds(p, tracers, stride=0), :]
            mixed[pl.ds(p, tracers, stride=CAP), :] = crossed(mine, matrix) * jnp.exp(-rate * wet)
        return carry

    lax.fori_loop(0, CAP // P_BLOCK, contract, 0)

    def finish(block, carry):
        for inner in range(2):
            t = block * 2 + inner
            spot = pl.multiple_of(t * CAP, CAP)
            spread = lax.dot_general(
                mixed[pl.ds(spot, CAP), :].astype(BF16),
                back_ref[...],
                (((0,), (0,)), ((), ())),
                preferred_element_type=F32,
            )[:levels]
            plain = product(columns_in[t, :levels], placing_ref[...])
            scav = scav_ref[first * GROUP + t]
            out_ref[t] = (spread + plain * jnp.exp(-scav * rain_ref[...])).astype(BF16)
        return carry

    lax.fori_loop(0, tracers // 2, finish, 0)


def physics(place, scav, parts, made, rates, first, groups, after):
    matrix, placing, picking, back, wet, rain = made
    columns = parts[0].shape[2]
    levels = rain.shape[0]
    tracers = groups * GROUP
    flops = 2 * tracers * levels * columns * (columns + 3 * CAP)
    scalars = pl.BlockSpec(memory_space=pltpu.SMEM)
    operands = (placing, picking, back, matrix, rain, wet)
    return pl.pallas_call(
        functools.partial(physics_kernel, first=first),
        grid=(1,),
        in_specs=[scalars, scalars]
        + [whole_block(*x.shape, once=True) for x in (*parts, *operands)]
        + [whole_block(*rates.shape)]
        + [pl.BlockSpec(memory_space=pl.ANY)] * len(after),
        out_specs=whole_block(tracers, levels, columns, once=True),
        scratch_shapes=[
            pltpu.VMEM((tracers, 128, columns), BF16),
            pltpu.VMEM((tracers * CAP, 128), F32),
            pltpu.VMEM((tracers * CAP, 128), F32),
        ],
        out_shape=jax.ShapeDtypeStruct((tracers, levels, columns), BF16),
        cost_estimate=pl.CostEstimate(
            flops=flops, bytes_accessed=groups * 1200000 + 6500000, transcendentals=0
        ),
        compiler_params=pltpu.CompilerParams(vmem_limit_bytes=(9 + 8 * groups) << 20),
        name="physics",
    )(place, scav, *parts, *operands, rates, *after)


def choose_kernel(flag_ref, own_ref, partner_ref, *refs, first):
    out_ref, held, in_sems, out_sems = refs[-4:]
    pieces, rows = held.shape[:2]

    def copied_from(source):
        ins = [
            pltpu.make_async_copy(source.at[pl.ds(i * rows, rows)], held.at[i], in_sems.at[i])
            for i in range(pieces)
        ]
        outs = [
            pltpu.make_async_copy(
                held.at[i], out_ref.at[pl.ds(first + i * rows, rows)], out_sems.at[i]
            )
            for i in range(pieces)
        ]
        for copy in ins:
            copy.start()
        for i in range(pieces):
            ins[i].wait()
            outs[i].start()
        for copy in outs:
            copy.wait()

    @pl.when(flag_ref[0] > 0)
    def _():
        copied_from(partner_ref)

    @pl.when(flag_ref[0] <= 0)
    def _():
        copied_from(own_ref)


def choose(flag, own, partner, whole, shape, first, groups, after):
    rows = shape[0] // sum(CHUNKS)
    pieces = 4 * groups
    operands = [own, partner]
    aliases = {}
    if whole is not None:
        operands.append(whole)
        aliases = {3: 0}
    operands += after
    anywhere = pl.BlockSpec(memory_space=pl.ANY)
    return pl.pallas_call(
        functools.partial(choose_kernel, first=first * rows),
        in_specs=[pl.BlockSpec(memory_space=pltpu.SMEM)] + [anywhere] * len(operands),
        out_specs=anywhere,
        scratch_shapes=[
            pltpu.VMEM((pieces, rows * groups // pieces, shape[1]), BF16),
            pltpu.SemaphoreType.DMA((pieces,)),
            pltpu.SemaphoreType.DMA((pieces,)),
        ],
        out_shape=jax.ShapeDtypeStruct(shape, BF16),
        input_output_aliases=aliases,
        cost_estimate=pl.CostEstimate(
            flops=0, bytes_accessed=groups * 1200000, transcendentals=0
        ),
        compiler_params=pltpu.CompilerParams(vmem_limit_bytes=8 << 20),
        name="choose",
    )(flag, *operands)


def shifted(value, axis, steps):
    count = lax.axis_size(axis)
    pairs = [(i, i + steps) for i in range(count) if 0 <= i + steps < count]
    return lax.ppermute(value, axis, pairs)


def turned(value, axis, steps):
    count = lax.axis_size(axis)
    return lax.ppermute(value, axis, [(i, (i + steps) % count) for i in range(count)])


def paired(value, axis):
    count = lax.axis_size(axis)
    return lax.ppermute(value, axis, [(i, i ^ (count // 2)) for i in range(count)])


def tiled_rows(value):
    lead = value.shape[:-2]
    lats, lons = value.shape[-2:]
    split = value.reshape(*lead, lats, lons // 128, 128)
    return jnp.swapaxes(split, -3, -2).reshape(*lead, lats * lons // 128, 128)


def local(
    tracer_dyn,
    courant_lat,
    courant_lon,
    conv_matrix,
    conv_mask,
    column_order,
    rain,
    scav_rate,
    pair_flag,
):
    n_lat = lax.axis_size("lat")
    n_lev = lax.axis_size("lev")
    tracers = tracer_dyn.shape[0]
    levels, columns = rain.shape
    lev_place = lax.axis_index("lev")
    pair_index = lax.axis_index("lat") % (n_lat // 2) * n_lev + lev_place
    flag = lax.dynamic_slice_in_dim(pair_flag, pair_index, 1)
    rates = jnp.broadcast_to(
        scav_rate.reshape(tracers // GROUP, GROUP, 1), (tracers // GROUP, GROUP, 128)
    )

    in_hbm = functools.partial(pltpu.with_memory_space_constraint, memory_space=pltpu.HBM)
    q = in_hbm(tiled_rows(tracer_dyn))
    lat, lon = in_hbm(tiled_rows(courant_lat)), in_hbm(tiled_rows(courant_lon))
    firsts = [sum(CHUNKS[:number]) for number in range(len(CHUNKS))]
    apart, face_move = (in_hbm(x) for x in (deinterleave(), face_rows(lat.shape[0])))
    place = lev_place.astype(jnp.int32).reshape(1)
    halos, sections, owns, partners, made = {}, {}, {}, {}, {}
    out = last = None
    for kind, number in ORDER:
        after = [] if last is None else [last]
        if kind == "extract":
            found = extract(
                apart, face_move, q, lat, lon, *SPANS[number], number == 0, after
            )
            north, south = found[:2]
            faces = found[2] if number == 0 else faces
            last = north
            high = shifted(south, "lat", -1)
            low = shifted(north, "lat", 1)
            halos[number] = (south, north, low, high)
        elif kind == "tables":
            made = tables(
                in_hbm(conv_matrix),
                in_hbm(conv_mask.reshape(1, columns)),
                in_hbm(column_order.reshape(1, columns)),
                in_hbm(rain),
                after,
            )
            last = made[2]
        elif kind == "advect":
            first, groups = firsts[number], CHUNKS[number]
            span = max(i for i in range(len(SPANS)) if SPANS[i][0] <= first)
            parts = advect(
                place, *halos[span], faces, halos[0][3], first - SPANS[span][0], groups, after
            )
            parts = list(parts)
            last = parts[0]
            for shift in (2, 1, 3):
                parts[shift] = turned(parts[shift], "lev", shift)
            sections[number] = parts
        elif kind == "physics":
            own = physics(
                place, scav_rate, sections[number], made, rates,
                firsts[number], CHUNKS[number], after,
            )
            own = own.reshape(-1, columns)
            last = owns[number] = own
            partners[number] = paired(own, "lat")
        else:
            out = choose(
                flag, owns[number], partners[number], out, (tracers * levels, columns),
                firsts[number], CHUNKS[number], after,
            )
    return out.reshape(tracers, levels, columns)


def solution(mesh):
    placed = (
        P(None, "lev", "lat", None),
        P("lev", "lat", None),
        P("lev", "lat", None),
        P(None, None, ("lat", "lev")),
        P(("lat", "lev")),
        P(("lat", "lev")),
        P(None, ("lat", "lev")),
        P(),
        P(),
    )

    return jax.shard_map(
        local, mesh=mesh, in_specs=placed, out_specs=P(None, None, ("lat", "lev")), check_vma=False
    )
```

```python
import functools
import itertools

import jax
import jax.numpy as jnp
import numpy as np
from jax import lax
from jax.experimental import pallas as pl
from jax.experimental.pallas import tpu as pltpu
from jax.sharding import PartitionSpec as P


GROUP = 8
CHUNKS = (1, 2, 2, 2, 1)
SPANS = ((0, 3), (3, 5))
ORDER = (
    ("extract", 0),
    ("extract", 1),
    ("advect", 0),
    ("tables", 0),
    ("advect", 1),
    ("physics", 0),
    ("physics", 1),
    ("advect", 2),
    ("advect", 3),
    ("physics", 2),
    ("advect", 4),
    ("physics", 3),
    ("physics", 4),
    ("choose", 0),
    ("choose", 1),
    ("choose", 2),
    ("choose", 3),
    ("choose", 4),
)
CAP = 256
P_BLOCK = 32
F32 = jnp.float32
BF16 = jnp.bfloat16


def deinterleave():
    move = np.zeros((256, 256), np.float32)
    for k, a, t, i in itertools.product(range(2), range(2), range(GROUP), range(8)):
        move[((k * 2 + a) * GROUP + t) * 8 + i, ((t * 2 + k) * 8 + i) * 2 + a] = 1
    return jnp.asarray(move, BF16)


def face_rows(levels):
    rows = levels * 8
    move = np.zeros((2 * rows, 2 * rows), np.float32)
    for a, r in itertools.product(range(2), range(rows)):
        move[a * rows + r, r * 2 + a] = 1
    return jnp.asarray(move, BF16)


def product(a, b):
    return jnp.dot(a, b, preferred_element_type=F32)


def two_levels(q_ref, pair):
    return q_ref[:, 2 * pair : 2 * pair + 2].reshape(2 * GROUP * 16, 128)


def moved_rows(move, blocks):
    moved = []
    for at in range(0, len(blocks), 2):
        some = blocks[at : at + 2]
        both = product(move, jnp.concatenate(some, axis=1))
        moved += [both[:, i * 128 : (i + 1) * 128] for i in range(len(some))]
    return moved


def extract_kernel(apart_ref, face_move_ref, q_ref, lat_ref, lon_ref, *refs, faces_too):
    outs = refs[-3:] if faces_too else refs[-2:]
    north_ref, south_ref = outs[:2]
    levels = q_ref.shape[1]
    rows = levels * GROUP * 8
    blocks = [two_levels(q_ref, pair) for pair in range(levels // 2)]
    for pair, apart in enumerate(moved_rows(apart_ref[...], blocks)):
        for k in range(2):
            spot = pair * 128 + k * 64
            south_ref[0, spot : spot + 64, :] = apart[k * 128 : k * 128 + 64].astype(BF16)
            north_ref[0, spot : spot + 64, :] = apart[k * 128 + 64 : k * 128 + 128].astype(BF16)
    if south_ref.shape[1] > rows:
        faces = lat_ref[...].reshape(levels * 16, 128)
        south_ref[0, rows:, :] = product(face_move_ref[: levels * 8], faces).astype(BF16)
    if faces_too:

        @pl.when(pl.program_id(0) == 0)
        def _():
            blocks = [ref[...].reshape(levels * 16, 128) for ref in (lat_ref, lon_ref)]
            for at, both in enumerate(moved_rows(face_move_ref[...], blocks)):
                outs[2][2 * at] = both[: levels * 8]
                outs[2][2 * at + 1] = both[levels * 8 :]


def whole_block(*shape, once=False):
    mode = {"pipeline_mode": pl.Buffered(1)} if once else {}
    return pl.BlockSpec(shape, lambda *_: (0,) * len(shape), **mode)


def extract(apart, face_move, q, lat, lon, first, groups, faces_too, after):
    levels = q.shape[1]
    rows = levels * GROUP * 8
    extra = levels * 8 if first == 0 else 0
    faces = (4, levels * 8, 128)
    return pl.pallas_call(
        functools.partial(extract_kernel, faces_too=faces_too),
        grid=(groups,),
        in_specs=[
            whole_block(*apart.shape),
            whole_block(*face_move.shape),
            pl.BlockSpec((GROUP, levels, 16, 128), lambda g: (g + first, 0, 0, 0)),
            whole_block(*lat.shape),
            whole_block(*lon.shape),
        ]
        + [pl.BlockSpec(memory_space=pl.ANY)] * len(after),
        out_specs=[
            pl.BlockSpec((1, rows, 128), lambda g: (g, 0, 0)),
            pl.BlockSpec((1, rows + extra, 128), lambda g: (g, 0, 0)),
        ]
        + [whole_block(*faces)] * faces_too,
        out_shape=[
            jax.ShapeDtypeStruct((groups, rows, 128), BF16),
            jax.ShapeDtypeStruct((groups, rows + extra, 128), BF16),
        ]
        + [jax.ShapeDtypeStruct(faces, F32)] * faces_too,
        cost_estimate=pl.CostEstimate(
            flops=groups * 10**6, bytes_accessed=groups * 1200000, transcendentals=0
        ),
        compiler_params=pltpu.CompilerParams(vmem_limit_bytes=7 << 20),
        name="extract",
    )(apart, face_move, q, lat, lon, *after)


def beside(x, lane, toward_east):
    if toward_east:
        turned = pltpu.roll(x, 127, 1)
        return jnp.where(lane == 127, pltpu.roll(turned, 7, 0), turned)
    turned = pltpu.roll(x, 1, 1)
    return jnp.where(lane == 0, pltpu.roll(turned, 1, 0), turned)


def advect_kernel(
    place_ref, south_ref, north_ref, low_ref, high_ref, faces_ref, above_ref, *refs
):
    outs, made = refs[-5:-1], refs[-1]
    levels = faces_ref.shape[1] // 8
    lane = lax.broadcasted_iota(jnp.int32, (8, 128), 1)

    def body(k, carry):
        at = pl.ds(pl.multiple_of(k * 8, 8), 8)
        edge = [faces_ref[0, at, :], faces_ref[1, at, :], above_ref[0, at, :].astype(F32)]
        terms = []
        for lat in range(2):
            south, north, west = edge[lat], edge[lat + 1], faces_ref[2 + lat, at, :]
            east = beside(west, lane, True)
            own = (
                1.0
                - (jnp.maximum(north, 0.0) - jnp.minimum(south, 0.0))
                - (jnp.maximum(east, 0.0) - jnp.minimum(west, 0.0))
            )
            terms.append(
                (
                    own,
                    jnp.maximum(south, 0.0),
                    -jnp.minimum(north, 0.0),
                    jnp.maximum(west, 0.0),
                    -jnp.minimum(east, 0.0),
                )
            )
        for t in range(0, GROUP, 2):
            spot = pl.multiple_of(k * 64 + t * 8, 16)
            columns = [
                ref[0, pl.ds(spot, 16), :].astype(F32)
                for ref in (low_ref, south_ref, north_ref, high_ref)
            ]
            results = [[], []]
            for part in range(2):
                column = [x[part * 8 : part * 8 + 8] for x in columns]
                rows = column[1:3]
                for lat in range(2):
                    own, from_s, from_n, from_w, from_e = terms[lat]
                    results[lat].append(
                        own * rows[lat]
                        + (from_s * column[lat] + from_n * column[lat + 2])
                        + (
                            from_w * beside(rows[lat], lane, False)
                            + from_e * beside(rows[lat], lane, True)
                        )
                    )
            for lat in range(2):
                for part in range(2):
                    spot = ((lat * GROUP + t + part) * levels + k) * 8
                    made[pl.ds(pl.multiple_of(spot, 8), 8), :] = results[lat][part]
        return carry

    lax.fori_loop(0, levels, body, 0)
    for shift, out in enumerate(outs):
        tile = 2 * lax.rem(place_ref[0] + shift, 4)
        for t, lat, half in itertools.product(range(GROUP), range(2), range(2)):
            start = tile + (lat * GROUP + t) * levels * 8 + half
            column = (2 * lat + half) * 128
            out[0, t * levels : (t + 1) * levels, column : column + 128] = made[
                pl.ds(start, levels, stride=8), :
            ].astype(BF16)


def advect(place, south, north, low, high, faces, above, halo_first, groups, after):
    levels = faces.shape[1] // 8
    rows = levels * GROUP
    halo = pl.BlockSpec((1, rows * 8, 128), lambda g: (g + halo_first, 0, 0))
    return pl.pallas_call(
        advect_kernel,
        grid=(groups,),
        in_specs=[
            pl.BlockSpec(memory_space=pltpu.SMEM),
            halo,
            halo,
            halo,
            halo,
            whole_block(*faces.shape),
            pl.BlockSpec((1, levels * 8, 128), lambda g: (0, GROUP, 0)),
        ]
        + [pl.BlockSpec(memory_space=pl.ANY)] * len(after),
        out_specs=[pl.BlockSpec((1, rows, 512), lambda g: (g, 0, 0))] * 4,
        scratch_shapes=[pltpu.VMEM((levels * 128, 128), F32)],
        out_shape=[jax.ShapeDtypeStruct((groups, rows, 512), BF16)] * 4,
        cost_estimate=pl.CostEstimate(
            flops=groups * 10**7, bytes_accessed=groups * 2000000, transcendentals=0
        ),
        compiler_params=pltpu.CompilerParams(vmem_limit_bytes=10 << 20),
        name="advect",
    )(place, south, north, low, high, faces, above, *after)


def table_kernel(matrix_ref, mask_ref, order_ref, rain_ref, *refs):
    small_ref, placing_ref, picking_ref, back_ref, wet_ref, all_ref, held, turned, sems = refs[-9:]
    columns = mask_ref.shape[1]
    levels = rain_ref.shape[0]
    pieces, per_piece = held.shape[:2]
    copies = [
        pltpu.make_async_copy(
            matrix_ref.at[pl.ds(i * per_piece, per_piece)], held.at[i], sems.at[i]
        )
        for i in range(pieces)
    ]
    for copy in copies:
        copy.start()

    mask = mask_ref[...]
    order = order_ref[...]
    row = lax.broadcasted_iota(jnp.int32, (columns, columns), 0)
    column = lax.broadcasted_iota(jnp.int32, (columns, columns), 1)
    earlier = jnp.where(row < column, 1.0, 0.0).astype(BF16)
    ones = jnp.where(mask > 0, 1.0, 0.0)
    wide = jnp.broadcast_to(ones, (8, columns)).astype(BF16)
    rank = product(wide, earlier)[0:1]
    rank = jnp.where(mask > 0, rank, -1.0).astype(jnp.int32)
    slot = lax.broadcasted_iota(jnp.int32, (CAP, columns), 0)
    back = jnp.where(slot == rank, 1.0, 0.0).astype(BF16)
    back_ref[...] = back
    whole = jnp.where(row == order, 1.0, 0.0)
    placing_ref[...] = jnp.where(mask > 0, 0.0, whole).astype(BF16)
    picking_ref[...] = crossed(back, whole.astype(BF16)).astype(BF16)
    rain = rain_ref[...]
    all_ref[...] = rain.astype(F32)
    nothing = jnp.zeros((CAP, 128 - levels), F32)
    wet_ref[...] = jnp.concatenate([crossed(back, rain), nothing], axis=1)
    gap = jnp.zeros((128 - levels, columns), BF16)
    for piece in range(pieces):
        copies[piece].wait()
        for k in range(0, per_piece, 2):
            both = jnp.concatenate([held[piece, k], gap, held[piece, k + 1], gap], axis=0)
            found = crossed(back_ref[...], both)
            for part in range(2):
                lanes = slice(part * 128, (part + 1) * 128)
                turned[pl.ds(k + part, CAP, stride=per_piece), :] = found[:, lanes]
        spot = piece * per_piece
        small_ref[:, spot : spot + per_piece, :] = (
            turned[...].reshape(CAP, per_piece, 128).astype(BF16)
        )


def crossed(a, b):
    return lax.dot_general(a, b, (((1,), (1,)), ((), ())), preferred_element_type=F32)


def tables(matrix, mask, order, rain, after):
    levels, _, columns = matrix.shape
    per_piece = 8
    shapes = [
        ((CAP, levels, 128), BF16),
        ((columns, columns), BF16),
        ((CAP, columns), BF16),
        ((CAP, columns), BF16),
        ((CAP, 128), F32),
        ((levels, columns), F32),
    ]
    return pl.pallas_call(
        table_kernel,
        grid=(1,),
        in_specs=[
            pl.BlockSpec(memory_space=pl.ANY),
            whole_block(1, columns),
            whole_block(1, columns),
            whole_block(levels, columns),
        ]
        + [pl.BlockSpec(memory_space=pl.ANY)] * len(after),
        out_specs=[whole_block(*shape, once=True) for shape, _ in shapes],
        out_shape=[jax.ShapeDtypeStruct(*x) for x in shapes],
        scratch_shapes=[
            pltpu.VMEM((levels // per_piece, per_piece, levels, columns), BF16),
            pltpu.VMEM((CAP * per_piece, 128), F32),
            pltpu.SemaphoreType.DMA((levels // per_piece,)),
        ],
        cost_estimate=pl.CostEstimate(
            flops=2 * levels * 128 * columns * CAP, bytes_accessed=12 * 10**6, transcendentals=0
        ),
        compiler_params=pltpu.CompilerParams(vmem_limit_bytes=20 << 20),
        name="tables",
    )(matrix, mask, order, rain, *after)


def physics_kernel(
    place_ref, scav_ref, part0, part1, part2, part3, placing_ref, picking_ref, back_ref,
    matrix_ref, rain_ref, wet_ref, rate_ref, *refs, first
):
    out_ref, columns_in, picked, mixed = refs[-4:]
    groups = part0.shape[0]
    levels = rain_ref.shape[0]
    part = part0.shape[1] // GROUP
    tracers = groups * GROUP

    columns_in[:, levels:, :] = jnp.zeros((tracers, 128 - levels, part0.shape[2]), BF16)
    for place in range(4):

        @pl.when(place_ref[0] == place)
        def _(place=place):
            for shift, ref in enumerate((part0, part1, part2, part3)):
                base = (place - shift) % 4 * part
                for g, t in itertools.product(range(groups), range(GROUP)):
                    columns_in[g * GROUP + t, base : base + part, :] = ref[
                        g, t * part : (t + 1) * part, :
                    ]

    for t in range(0, tracers, 2):
        both = crossed(picking_ref[...], columns_in[t : t + 2].reshape(256, part0.shape[2]))
        for part_at in range(2):
            lanes = slice(part_at * 128, (part_at + 1) * 128)
            g, row = divmod(t + part_at, GROUP)
            picked[g, pl.ds(row, CAP, stride=GROUP), :] = both[:, lanes]

    rate = jnp.concatenate([rate_ref[first + g] for g in range(groups)], axis=0)
    nothing = jnp.zeros((128 - levels, 128), BF16)

    def contract(block, carry):
        for inner in range(P_BLOCK):
            p = block * P_BLOCK + inner
            spot = pl.ds(pl.multiple_of(p * GROUP, GROUP), GROUP)
            mine = jnp.concatenate([picked[g, spot, :] for g in range(groups)], axis=0).astype(BF16)
            matrix = jnp.concatenate([matrix_ref[p], nothing], axis=0)
            wet = wet_ref[pl.ds(p, tracers, stride=0), :]
            washed = crossed(mine, matrix) * jnp.exp(-rate * wet)
            for g in range(groups):
                mixed[g, spot, :] = washed[g * GROUP : (g + 1) * GROUP]
        return carry

    lax.fori_loop(0, CAP // P_BLOCK, contract, 0)

    for g in range(groups):

        def finish(block, carry, g=g):
            row = block * 2
            at = g * GROUP + row
            both = columns_in[pl.ds(at, 2)].reshape(256, columns_in.shape[2])
            plain = product(both, placing_ref[...])
            for inner in range(2):
                spread = lax.dot_general(
                    mixed[g, pl.ds(row + inner, CAP, stride=GROUP), :].astype(BF16),
                    back_ref[...],
                    (((0,), (0,)), ((), ())),
                    preferred_element_type=F32,
                )[:levels]
                scav = scav_ref[first * GROUP + at + inner]
                dry = plain[inner * 128 : inner * 128 + levels]
                out_ref[at + inner] = (spread + dry * jnp.exp(-scav * rain_ref[...])).astype(BF16)
            return carry

        lax.fori_loop(0, GROUP // 2, finish, 0)


def physics(place, scav, parts, made, rates, first, groups, after):
    matrix, placing, picking, back, wet, rain = made
    columns = parts[0].shape[2]
    levels = rain.shape[0]
    tracers = groups * GROUP
    flops = 2 * tracers * levels * columns * (columns + 3 * CAP)
    scalars = pl.BlockSpec(memory_space=pltpu.SMEM)
    operands = (placing, picking, back, matrix, rain, wet)
    return pl.pallas_call(
        functools.partial(physics_kernel, first=first),
        grid=(1,),
        in_specs=[scalars, scalars]
        + [whole_block(*x.shape, once=True) for x in (*parts, *operands)]
        + [whole_block(*rates.shape)]
        + [pl.BlockSpec(memory_space=pl.ANY)] * len(after),
        out_specs=whole_block(tracers, levels, columns, once=True),
        scratch_shapes=[
            pltpu.VMEM((tracers, 128, columns), BF16),
            pltpu.VMEM((groups, CAP * GROUP, 128), F32),
            pltpu.VMEM((groups, CAP * GROUP, 128), F32),
        ],
        out_shape=jax.ShapeDtypeStruct((tracers, levels, columns), BF16),
        cost_estimate=pl.CostEstimate(
            flops=flops, bytes_accessed=groups * 1200000 + 6500000, transcendentals=0
        ),
        compiler_params=pltpu.CompilerParams(vmem_limit_bytes=(12 + 4 * groups) << 20),
        name="physics",
    )(place, scav, *parts, *operands, rates, *after)


def choose_kernel(flag_ref, own_ref, partner_ref, *refs, first):
    out_ref, held, in_sems, out_sems = refs[-4:]
    pieces, rows = held.shape[:2]

    def copied_from(source):
        ins = [
            pltpu.make_async_copy(source.at[pl.ds(i * rows, rows)], held.at[i], in_sems.at[i])
            for i in range(pieces)
        ]
        outs = [
            pltpu.make_async_copy(
                held.at[i], out_ref.at[pl.ds(first + i * rows, rows)], out_sems.at[i]
            )
            for i in range(pieces)
        ]
        for copy in ins:
            copy.start()
        for i in range(pieces):
            ins[i].wait()
            outs[i].start()
        for copy in outs:
            copy.wait()

    @pl.when(flag_ref[0] > 0)
    def _():
        copied_from(partner_ref)

    @pl.when(flag_ref[0] <= 0)
    def _():
        copied_from(own_ref)


def choose(flag, own, partner, whole, shape, first, groups, after):
    rows = shape[0] // sum(CHUNKS)
    pieces = 4 * groups
    operands = [own, partner]
    aliases = {}
    if whole is not None:
        operands.append(whole)
        aliases = {3: 0}
    operands += after
    anywhere = pl.BlockSpec(memory_space=pl.ANY)
    return pl.pallas_call(
        functools.partial(choose_kernel, first=first * rows),
        in_specs=[pl.BlockSpec(memory_space=pltpu.SMEM)] + [anywhere] * len(operands),
        out_specs=anywhere,
        scratch_shapes=[
            pltpu.VMEM((pieces, rows * groups // pieces, shape[1]), BF16),
            pltpu.SemaphoreType.DMA((pieces,)),
            pltpu.SemaphoreType.DMA((pieces,)),
        ],
        out_shape=jax.ShapeDtypeStruct(shape, BF16),
        input_output_aliases=aliases,
        cost_estimate=pl.CostEstimate(
            flops=0, bytes_accessed=groups * 1200000, transcendentals=0
        ),
        compiler_params=pltpu.CompilerParams(vmem_limit_bytes=8 << 20),
        name="choose",
    )(flag, *operands)


def shifted(value, axis, steps):
    count = lax.axis_size(axis)
    pairs = [(i, i + steps) for i in range(count) if 0 <= i + steps < count]
    return lax.ppermute(value, axis, pairs)


def turned(value, axis, steps):
    count = lax.axis_size(axis)
    return lax.ppermute(value, axis, [(i, (i + steps) % count) for i in range(count)])


def paired(value, axis):
    count = lax.axis_size(axis)
    return lax.ppermute(value, axis, [(i, i ^ (count // 2)) for i in range(count)])


def tiled_rows(value):
    lead = value.shape[:-2]
    lats, lons = value.shape[-2:]
    split = value.reshape(*lead, lats, lons // 128, 128)
    return jnp.swapaxes(split, -3, -2).reshape(*lead, lats * lons // 128, 128)


def local(
    tracer_dyn,
    courant_lat,
    courant_lon,
    conv_matrix,
    conv_mask,
    column_order,
    rain,
    scav_rate,
    pair_flag,
):
    n_lat = lax.axis_size("lat")
    n_lev = lax.axis_size("lev")
    tracers = tracer_dyn.shape[0]
    levels, columns = rain.shape
    lev_place = lax.axis_index("lev")
    pair_index = lax.axis_index("lat") % (n_lat // 2) * n_lev + lev_place
    flag = lax.dynamic_slice_in_dim(pair_flag, pair_index, 1)
    rates = jnp.broadcast_to(
        scav_rate.reshape(tracers // GROUP, GROUP, 1), (tracers // GROUP, GROUP, 128)
    )

    in_hbm = functools.partial(pltpu.with_memory_space_constraint, memory_space=pltpu.HBM)
    q = in_hbm(tiled_rows(tracer_dyn))
    lat, lon = in_hbm(tiled_rows(courant_lat)), in_hbm(tiled_rows(courant_lon))
    firsts = [sum(CHUNKS[:number]) for number in range(len(CHUNKS))]
    apart, face_move = (in_hbm(x) for x in (deinterleave(), face_rows(lat.shape[0])))
    place = lev_place.astype(jnp.int32).reshape(1)
    halos, sections, owns, partners, made = {}, {}, {}, {}, {}
    out = last = None
    for kind, number in ORDER:
        after = [] if last is None else [last]
        if kind == "extract":
            found = extract(
                apart, face_move, q, lat, lon, *SPANS[number], number == 0, after
            )
            north, south = found[:2]
            faces = found[2] if number == 0 else faces
            last = north
            high = shifted(south, "lat", -1)
            low = shifted(north, "lat", 1)
            halos[number] = (south, north, low, high)
        elif kind == "tables":
            made = tables(
                in_hbm(conv_matrix),
                in_hbm(conv_mask.reshape(1, columns)),
                in_hbm(column_order.reshape(1, columns)),
                in_hbm(rain),
                after,
            )
            last = made[2]
        elif kind == "advect":
            first, groups = firsts[number], CHUNKS[number]
            span = max(i for i in range(len(SPANS)) if SPANS[i][0] <= first)
            parts = advect(
                place, *halos[span], faces, halos[0][3], first - SPANS[span][0], groups, after
            )
            parts = list(parts)
            last = parts[0]
            for shift in (2, 1, 3):
                parts[shift] = turned(parts[shift], "lev", shift)
            sections[number] = parts
        elif kind == "physics":
            own = physics(
                place, scav_rate, sections[number], made, rates,
                firsts[number], CHUNKS[number], after,
            )
            own = own.reshape(-1, columns)
            last = owns[number] = own
            partners[number] = paired(own, "lat")
        else:
            out = choose(
                flag, owns[number], partners[number], out, (tracers * levels, columns),
                firsts[number], CHUNKS[number], after,
            )
    return out.reshape(tracers, levels, columns)


def solution(mesh):
    placed = (
        P(None, "lev", "lat", None),
        P("lev", "lat", None),
        P("lev", "lat", None),
        P(None, None, ("lat", "lev")),
        P(("lat", "lev")),
        P(("lat", "lev")),
        P(None, ("lat", "lev")),
        P(),
        P(),
    )

    return jax.shard_map(
        local, mesh=mesh, in_specs=placed, out_specs=P(None, None, ("lat", "lev")), check_vma=False
    )
```

```python
import functools
import itertools

import jax
import jax.numpy as jnp
import numpy as np
from jax import lax
from jax.experimental import pallas as pl
from jax.experimental.pallas import tpu as pltpu
from jax.sharding import PartitionSpec as P


GROUP = 8
CHUNKS = (1, 2, 2, 2, 1)
SPANS = ((0, 3), (3, 5))
ORDER = (
    ("extract", 0),
    ("extract", 1),
    ("advect", 0),
    ("tables", 0),
    ("advect", 1),
    ("physics", 0),
    ("physics", 1),
    ("advect", 2),
    ("advect", 3),
    ("physics", 2),
    ("advect", 4),
    ("physics", 3),
    ("physics", 4),
    ("choose", 0),
    ("choose", 1),
    ("choose", 2),
    ("choose", 3),
    ("choose", 4),
)
CAP = 256
P_BLOCK = 32
F32 = jnp.float32
BF16 = jnp.bfloat16


def deinterleave():
    move = np.zeros((256, 256), np.float32)
    for k, a, t, i in itertools.product(range(2), range(2), range(GROUP), range(8)):
        move[((k * 2 + a) * GROUP + t) * 8 + i, ((t * 2 + k) * 8 + i) * 2 + a] = 1
    return jnp.asarray(move, BF16)


def face_rows(levels):
    rows = levels * 8
    move = np.zeros((2 * rows, 2 * rows), np.float32)
    for a, r in itertools.product(range(2), range(rows)):
        move[a * rows + r, r * 2 + a] = 1
    return jnp.asarray(move, BF16)


def product(a, b):
    return jnp.dot(a, b, preferred_element_type=F32)


def two_levels(q_ref, pair):
    return q_ref[:, 2 * pair : 2 * pair + 2].reshape(2 * GROUP * 16, 128)


def moved_rows(move, blocks):
    moved = []
    for at in range(0, len(blocks), 2):
        some = blocks[at : at + 2]
        both = product(move, jnp.concatenate(some, axis=1))
        moved += [both[:, i * 128 : (i + 1) * 128] for i in range(len(some))]
    return moved


def extract_kernel(apart_ref, face_move_ref, q_ref, lat_ref, lon_ref, *refs, faces_too):
    outs = refs[-3:] if faces_too else refs[-2:]
    north_ref, south_ref = outs[:2]
    levels = q_ref.shape[1]
    rows = levels * GROUP * 8
    blocks = [two_levels(q_ref, pair) for pair in range(levels // 2)]
    for pair, apart in enumerate(moved_rows(apart_ref[...], blocks)):
        for k in range(2):
            spot = pair * 128 + k * 64
            south_ref[0, spot : spot + 64, :] = apart[k * 128 : k * 128 + 64].astype(BF16)
            north_ref[0, spot : spot + 64, :] = apart[k * 128 + 64 : k * 128 + 128].astype(BF16)
    if south_ref.shape[1] > rows:
        faces = lat_ref[...].reshape(levels * 16, 128)
        south_ref[0, rows:, :] = product(face_move_ref[: levels * 8], faces).astype(BF16)
    if faces_too:

        @pl.when(pl.program_id(0) == 0)
        def _():
            blocks = [ref[...].reshape(levels * 16, 128) for ref in (lat_ref, lon_ref)]
            for at, both in enumerate(moved_rows(face_move_ref[...], blocks)):
                outs[2][2 * at] = both[: levels * 8]
                outs[2][2 * at + 1] = both[levels * 8 :]


def whole_block(*shape, once=False):
    mode = {"pipeline_mode": pl.Buffered(1)} if once else {}
    return pl.BlockSpec(shape, lambda *_: (0,) * len(shape), **mode)


def extract(apart, face_move, q, lat, lon, first, groups, faces_too, after):
    levels = q.shape[1]
    rows = levels * GROUP * 8
    extra = levels * 8 if first == 0 else 0
    faces = (4, levels * 8, 128)
    return pl.pallas_call(
        functools.partial(extract_kernel, faces_too=faces_too),
        grid=(groups,),
        in_specs=[
            whole_block(*apart.shape),
            whole_block(*face_move.shape),
            pl.BlockSpec((GROUP, levels, 16, 128), lambda g: (g + first, 0, 0, 0)),
            whole_block(*lat.shape),
            whole_block(*lon.shape),
        ]
        + [pl.BlockSpec(memory_space=pl.ANY)] * len(after),
        out_specs=[
            pl.BlockSpec((1, rows, 128), lambda g: (g, 0, 0)),
            pl.BlockSpec((1, rows + extra, 128), lambda g: (g, 0, 0)),
        ]
        + [whole_block(*faces)] * faces_too,
        out_shape=[
            jax.ShapeDtypeStruct((groups, rows, 128), BF16),
            jax.ShapeDtypeStruct((groups, rows + extra, 128), BF16),
        ]
        + [jax.ShapeDtypeStruct(faces, F32)] * faces_too,
        cost_estimate=pl.CostEstimate(
            flops=groups * 10**6, bytes_accessed=groups * 1200000, transcendentals=0
        ),
        compiler_params=pltpu.CompilerParams(vmem_limit_bytes=7 << 20),
        name="extract",
    )(apart, face_move, q, lat, lon, *after)


def beside(x, lane, toward_east):
    if toward_east:
        turned = pltpu.roll(x, 127, 1)
        return jnp.where(lane == 127, pltpu.roll(turned, 7, 0), turned)
    turned = pltpu.roll(x, 1, 1)
    return jnp.where(lane == 0, pltpu.roll(turned, 1, 0), turned)


def advect_kernel(
    place_ref, south_ref, north_ref, low_ref, high_ref, faces_ref, above_ref, *refs
):
    outs, made = refs[-5:-1], refs[-1]
    levels = faces_ref.shape[1] // 8
    lane = lax.broadcasted_iota(jnp.int32, (8, 128), 1)

    def body(k, carry):
        at = pl.ds(pl.multiple_of(k * 8, 8), 8)
        edge = [faces_ref[0, at, :], faces_ref[1, at, :], above_ref[0, at, :].astype(F32)]
        terms = []
        for lat in range(2):
            south, north, west = edge[lat], edge[lat + 1], faces_ref[2 + lat, at, :]
            east = beside(west, lane, True)
            own = (
                1.0
                - (jnp.maximum(north, 0.0) - jnp.minimum(south, 0.0))
                - (jnp.maximum(east, 0.0) - jnp.minimum(west, 0.0))
            )
            terms.append(
                (
                    own,
                    jnp.maximum(south, 0.0),
                    -jnp.minimum(north, 0.0),
                    jnp.maximum(west, 0.0),
                    -jnp.minimum(east, 0.0),
                )
            )
        for t in range(0, GROUP, 2):
            spot = pl.multiple_of(k * 64 + t * 8, 16)
            columns = [
                ref[0, pl.ds(spot, 16), :].astype(F32)
                for ref in (low_ref, south_ref, north_ref, high_ref)
            ]
            results = [[], []]
            for part in range(2):
                column = [x[part * 8 : part * 8 + 8] for x in columns]
                rows = column[1:3]
                for lat in range(2):
                    own, from_s, from_n, from_w, from_e = terms[lat]
                    results[lat].append(
                        own * rows[lat]
                        + (from_s * column[lat] + from_n * column[lat + 2])
                        + (
                            from_w * beside(rows[lat], lane, False)
                            + from_e * beside(rows[lat], lane, True)
                        )
                    )
            for lat in range(2):
                for part in range(2):
                    spot = ((lat * GROUP + t + part) * levels + k) * 8
                    made[pl.ds(pl.multiple_of(spot, 8), 8), :] = results[lat][part]
        return carry

    lax.fori_loop(0, levels, body, 0)
    for shift, out in enumerate(outs):
        tile = 2 * lax.rem(place_ref[0] + shift, 4)
        for t, lat, half in itertools.product(range(GROUP), range(2), range(2)):
            start = tile + (lat * GROUP + t) * levels * 8 + half
            column = (2 * lat + half) * 128
            out[0, t * levels : (t + 1) * levels, column : column + 128] = made[
                pl.ds(start, levels, stride=8), :
            ].astype(BF16)


def advect(place, south, north, low, high, faces, above, halo_first, groups, after):
    levels = faces.shape[1] // 8
    rows = levels * GROUP
    halo = pl.BlockSpec((1, rows * 8, 128), lambda g: (g + halo_first, 0, 0))
    return pl.pallas_call(
        advect_kernel,
        grid=(groups,),
        in_specs=[
            pl.BlockSpec(memory_space=pltpu.SMEM),
            halo,
            halo,
            halo,
            halo,
            whole_block(*faces.shape),
            pl.BlockSpec((1, levels * 8, 128), lambda g: (0, GROUP, 0)),
        ]
        + [pl.BlockSpec(memory_space=pl.ANY)] * len(after),
        out_specs=[pl.BlockSpec((1, rows, 512), lambda g: (g, 0, 0))] * 4,
        scratch_shapes=[pltpu.VMEM((levels * 128, 128), F32)],
        out_shape=[jax.ShapeDtypeStruct((groups, rows, 512), BF16)] * 4,
        cost_estimate=pl.CostEstimate(
            flops=groups * 10**7, bytes_accessed=groups * 2000000, transcendentals=0
        ),
        compiler_params=pltpu.CompilerParams(vmem_limit_bytes=10 << 20),
        name="advect",
    )(place, south, north, low, high, faces, above, *after)


def table_kernel(matrix_ref, mask_ref, order_ref, rain_ref, *refs):
    small_ref, placing_ref, picking_ref, back_ref, wet_ref, all_ref, held, turned, sems = refs[-9:]
    columns = mask_ref.shape[1]
    levels = rain_ref.shape[0]
    pieces, per_piece = held.shape[:2]
    copies = [
        pltpu.make_async_copy(
            matrix_ref.at[pl.ds(i * per_piece, per_piece)], held.at[i], sems.at[i]
        )
        for i in range(pieces)
    ]
    for copy in copies:
        copy.start()

    mask = mask_ref[...]
    order = order_ref[...]
    row = lax.broadcasted_iota(jnp.int32, (columns, columns), 0)
    column = lax.broadcasted_iota(jnp.int32, (columns, columns), 1)
    earlier = jnp.where(row < column, 1.0, 0.0).astype(BF16)
    ones = jnp.where(mask > 0, 1.0, 0.0)
    wide = jnp.broadcast_to(ones, (8, columns)).astype(BF16)
    rank = product(wide, earlier)[0:1]
    rank = jnp.where(mask > 0, rank, -1.0).astype(jnp.int32)
    slot = lax.broadcasted_iota(jnp.int32, (CAP, columns), 0)
    back = jnp.where(slot == rank, 1.0, 0.0).astype(BF16)
    back_ref[...] = back
    whole = jnp.where(row == order, 1.0, 0.0)
    placing_ref[...] = jnp.where(mask > 0, 0.0, whole).astype(BF16)
    picking_ref[...] = crossed(back, whole.astype(BF16)).astype(BF16)
    rain = rain_ref[...]
    all_ref[...] = rain.astype(F32)
    nothing = jnp.zeros((CAP, 128 - levels), F32)
    wet_ref[...] = jnp.concatenate([crossed(back, rain), nothing], axis=1)
    gap = jnp.zeros((128 - levels, columns), BF16)
    for piece in range(pieces):
        copies[piece].wait()
        for k in range(0, per_piece, 2):
            both = jnp.concatenate([held[piece, k], gap, held[piece, k + 1], gap], axis=0)
            found = crossed(back_ref[...], both)
            for part in range(2):
                lanes = slice(part * 128, (part + 1) * 128)
                turned[pl.ds(k + part, CAP, stride=per_piece), :] = found[:, lanes]
        spot = piece * per_piece
        small_ref[:, spot : spot + per_piece, :] = (
            turned[...].reshape(CAP, per_piece, 128).astype(BF16)
        )


def crossed(a, b):
    return lax.dot_general(a, b, (((1,), (1,)), ((), ())), preferred_element_type=F32)


def tables(matrix, mask, order, rain, after):
    levels, _, columns = matrix.shape
    per_piece = 8
    shapes = [
        ((CAP, levels, 128), BF16),
        ((columns, columns), BF16),
        ((CAP, columns), BF16),
        ((CAP, columns), BF16),
        ((CAP, 128), F32),
        ((levels, columns), F32),
    ]
    return pl.pallas_call(
        table_kernel,
        grid=(1,),
        in_specs=[
            pl.BlockSpec(memory_space=pl.ANY),
            whole_block(1, columns),
            whole_block(1, columns),
            whole_block(levels, columns),
        ]
        + [pl.BlockSpec(memory_space=pl.ANY)] * len(after),
        out_specs=[whole_block(*shape, once=True) for shape, _ in shapes],
        out_shape=[jax.ShapeDtypeStruct(*x) for x in shapes],
        scratch_shapes=[
            pltpu.VMEM((levels // per_piece, per_piece, levels, columns), BF16),
            pltpu.VMEM((CAP * per_piece, 128), F32),
            pltpu.SemaphoreType.DMA((levels // per_piece,)),
        ],
        cost_estimate=pl.CostEstimate(
            flops=2 * levels * 128 * columns * CAP, bytes_accessed=12 * 10**6, transcendentals=0
        ),
        compiler_params=pltpu.CompilerParams(vmem_limit_bytes=20 << 20),
        name="tables",
    )(matrix, mask, order, rain, *after)


def physics_kernel(
    place_ref, scav_ref, part0, part1, part2, part3, placing_ref, picking_ref, back_ref,
    matrix_ref, rain_ref, wet_ref, *refs, first
):
    out_ref, columns_in, picked, mixed = refs[-4:]
    groups = part0.shape[0]
    levels = rain_ref.shape[0]
    part = part0.shape[1] // GROUP
    tracers = groups * GROUP

    columns_in[:, levels:, :] = jnp.zeros((tracers, 128 - levels, part0.shape[2]), BF16)
    for place in range(4):

        @pl.when(place_ref[0] == place)
        def _(place=place):
            for shift, ref in enumerate((part0, part1, part2, part3)):
                base = (place - shift) % 4 * part
                for g, t in itertools.product(range(groups), range(GROUP)):
                    columns_in[g * GROUP + t, base : base + part, :] = ref[
                        g, t * part : (t + 1) * part, :
                    ]

    for t in range(0, tracers, 2):
        both = crossed(picking_ref[...], columns_in[t : t + 2].reshape(256, part0.shape[2]))
        for part_at in range(2):
            lanes = slice(part_at * 128, (part_at + 1) * 128)
            g, row = divmod(t + part_at, GROUP)
            picked[g, pl.ds(row, CAP, stride=GROUP), :] = both[:, lanes]

    row = lax.broadcasted_iota(jnp.int32, (GROUP, 128), 0)
    rates = []
    for g in range(groups):
        rate = jnp.zeros((GROUP, 128), F32)
        for t in range(GROUP):
            rate = jnp.where(row == t, scav_ref[(first + g) * GROUP + t], rate)
        rates.append(rate)
    rate = jnp.concatenate(rates, axis=0)
    nothing = jnp.zeros((128 - levels, 128), BF16)

    def contract(block, carry):
        for inner in range(P_BLOCK):
            p = block * P_BLOCK + inner
            spot = pl.ds(pl.multiple_of(p * GROUP, GROUP), GROUP)
            mine = jnp.concatenate([picked[g, spot, :] for g in range(groups)], axis=0).astype(BF16)
            matrix = jnp.concatenate([matrix_ref[p], nothing], axis=0)
            wet = wet_ref[pl.ds(p, tracers, stride=0), :]
            washed = crossed(mine, matrix) * jnp.exp(-rate * wet)
            for g in range(groups):
                mixed[g, spot, :] = washed[g * GROUP : (g + 1) * GROUP]
        return carry

    lax.fori_loop(0, CAP // P_BLOCK, contract, 0)

    for g in range(groups):

        def finish(block, carry, g=g):
            row = block * 2
            at = g * GROUP + row
            both = columns_in[pl.ds(at, 2)].reshape(256, columns_in.shape[2])
            plain = product(both, placing_ref[...])
            for inner in range(2):
                spread = lax.dot_general(
                    mixed[g, pl.ds(row + inner, CAP, stride=GROUP), :].astype(BF16),
                    back_ref[...],
                    (((0,), (0,)), ((), ())),
                    preferred_element_type=F32,
                )[:levels]
                scav = scav_ref[first * GROUP + at + inner]
                dry = plain[inner * 128 : inner * 128 + levels]
                out_ref[at + inner] = (spread + dry * jnp.exp(-scav * rain_ref[...])).astype(BF16)
            return carry

        lax.fori_loop(0, GROUP // 2, finish, 0)


def physics(place, scav, parts, made, first, groups, after):
    matrix, placing, picking, back, wet, rain = made
    columns = parts[0].shape[2]
    levels = rain.shape[0]
    tracers = groups * GROUP
    flops = 2 * tracers * levels * columns * (columns + 3 * CAP)
    scalars = pl.BlockSpec(memory_space=pltpu.SMEM)
    operands = (placing, picking, back, matrix, rain, wet)
    return pl.pallas_call(
        functools.partial(physics_kernel, first=first),
        grid=(1,),
        in_specs=[scalars, scalars]
        + [whole_block(*x.shape, once=True) for x in (*parts, *operands)]
        + [pl.BlockSpec(memory_space=pl.ANY)] * len(after),
        out_specs=whole_block(tracers, levels, columns, once=True),
        scratch_shapes=[
            pltpu.VMEM((tracers, 128, columns), BF16),
            pltpu.VMEM((groups, CAP * GROUP, 128), F32),
            pltpu.VMEM((groups, CAP * GROUP, 128), F32),
        ],
        out_shape=jax.ShapeDtypeStruct((tracers, levels, columns), BF16),
        cost_estimate=pl.CostEstimate(
            flops=flops, bytes_accessed=groups * 1200000 + 6500000, transcendentals=0
        ),
        compiler_params=pltpu.CompilerParams(vmem_limit_bytes=(12 + 4 * groups) << 20),
        name="physics",
    )(place, scav, *parts, *operands, *after)


def choose_kernel(pair_ref, flag_ref, own_ref, partner_ref, *refs, first):
    out_ref, held, in_sems, out_sems = refs[-4:]
    pieces, rows = held.shape[:2]

    def copied_from(source):
        ins = [
            pltpu.make_async_copy(source.at[pl.ds(i * rows, rows)], held.at[i], in_sems.at[i])
            for i in range(pieces)
        ]
        outs = [
            pltpu.make_async_copy(
                held.at[i], out_ref.at[pl.ds(first + i * rows, rows)], out_sems.at[i]
            )
            for i in range(pieces)
        ]
        for copy in ins:
            copy.start()
        for i in range(pieces):
            ins[i].wait()
            outs[i].start()
        for copy in outs:
            copy.wait()

    flag = flag_ref[pair_ref[0]]

    @pl.when(flag > 0)
    def _():
        copied_from(partner_ref)

    @pl.when(flag <= 0)
    def _():
        copied_from(own_ref)


def choose(pair, flag, own, partner, whole, shape, first, groups, after):
    rows = shape[0] // sum(CHUNKS)
    pieces = 4 * groups
    operands = [own, partner]
    aliases = {}
    if whole is not None:
        operands.append(whole)
        aliases = {4: 0}
    operands += after
    anywhere = pl.BlockSpec(memory_space=pl.ANY)
    return pl.pallas_call(
        functools.partial(choose_kernel, first=first * rows),
        in_specs=[pl.BlockSpec(memory_space=pltpu.SMEM)] * 2 + [anywhere] * len(operands),
        out_specs=anywhere,
        scratch_shapes=[
            pltpu.VMEM((pieces, rows * groups // pieces, shape[1]), BF16),
            pltpu.SemaphoreType.DMA((pieces,)),
            pltpu.SemaphoreType.DMA((pieces,)),
        ],
        out_shape=jax.ShapeDtypeStruct(shape, BF16),
        input_output_aliases=aliases,
        cost_estimate=pl.CostEstimate(
            flops=0, bytes_accessed=groups * 1200000, transcendentals=0
        ),
        compiler_params=pltpu.CompilerParams(vmem_limit_bytes=8 << 20),
        name="choose",
    )(pair, flag, *operands)


def shifted(value, axis, steps):
    count = lax.axis_size(axis)
    pairs = [(i, i + steps) for i in range(count) if 0 <= i + steps < count]
    return lax.ppermute(value, axis, pairs)


def turned(value, axis, steps):
    count = lax.axis_size(axis)
    return lax.ppermute(value, axis, [(i, (i + steps) % count) for i in range(count)])


def paired(value, axis):
    count = lax.axis_size(axis)
    return lax.ppermute(value, axis, [(i, i ^ (count // 2)) for i in range(count)])


def tiled_rows(value):
    lead = value.shape[:-2]
    lats, lons = value.shape[-2:]
    split = value.reshape(*lead, lats, lons // 128, 128)
    return jnp.swapaxes(split, -3, -2).reshape(*lead, lats * lons // 128, 128)


def local(
    tracer_dyn,
    courant_lat,
    courant_lon,
    conv_matrix,
    conv_mask,
    column_order,
    rain,
    scav_rate,
    pair_flag,
):
    n_lat = lax.axis_size("lat")
    n_lev = lax.axis_size("lev")
    tracers = tracer_dyn.shape[0]
    levels, columns = rain.shape
    lev_place = lax.axis_index("lev")
    pair_index = lax.axis_index("lat") % (n_lat // 2) * n_lev + lev_place
    pair = pair_index.astype(jnp.int32).reshape(1)
    in_hbm = functools.partial(pltpu.with_memory_space_constraint, memory_space=pltpu.HBM)
    q = in_hbm(tiled_rows(tracer_dyn))
    lat, lon = in_hbm(tiled_rows(courant_lat)), in_hbm(tiled_rows(courant_lon))
    firsts = [sum(CHUNKS[:number]) for number in range(len(CHUNKS))]
    apart, face_move = (in_hbm(x) for x in (deinterleave(), face_rows(lat.shape[0])))
    place = lev_place.astype(jnp.int32).reshape(1)
    halos, sections, owns, partners, made = {}, {}, {}, {}, {}
    out = last = None
    for kind, number in ORDER:
        after = [] if last is None else [last]
        if kind == "extract":
            found = extract(
                apart, face_move, q, lat, lon, *SPANS[number], number == 0, after
            )
            north, south = found[:2]
            faces = found[2] if number == 0 else faces
            last = north
            high = shifted(south, "lat", -1)
            low = shifted(north, "lat", 1)
            halos[number] = (south, north, low, high)
        elif kind == "tables":
            made = tables(
                in_hbm(conv_matrix),
                in_hbm(conv_mask.reshape(1, columns)),
                in_hbm(column_order.reshape(1, columns)),
                in_hbm(rain),
                after,
            )
            last = made[2]
        elif kind == "advect":
            first, groups = firsts[number], CHUNKS[number]
            span = max(i for i in range(len(SPANS)) if SPANS[i][0] <= first)
            parts = advect(
                place, *halos[span], faces, halos[0][3], first - SPANS[span][0], groups, after
            )
            parts = list(parts)
            last = parts[0]
            for shift in (2, 1, 3):
                parts[shift] = turned(parts[shift], "lev", shift)
            sections[number] = parts
        elif kind == "physics":
            own = physics(
                place, scav_rate, sections[number], made,
                firsts[number], CHUNKS[number], after,
            )
            own = own.reshape(-1, columns)
            last = owns[number] = own
            partners[number] = paired(own, "lat")
        else:
            out = choose(
                pair, pair_flag, owns[number], partners[number], out, (tracers * levels, columns),
                firsts[number], CHUNKS[number], after,
            )
    return out.reshape(tracers, levels, columns)


def solution(mesh):
    placed = (
        P(None, "lev", "lat", None),
        P("lev", "lat", None),
        P("lev", "lat", None),
        P(None, None, ("lat", "lev")),
        P(("lat", "lev")),
        P(("lat", "lev")),
        P(None, ("lat", "lev")),
        P(),
        P(),
    )

    return jax.shard_map(
        local, mesh=mesh, in_specs=placed, out_specs=P(None, None, ("lat", "lev")), check_vma=False
    )
```

```python
import functools
import itertools

import jax
import jax.numpy as jnp
import numpy as np
from jax import lax
from jax.experimental import pallas as pl
from jax.experimental.pallas import tpu as pltpu
from jax.sharding import PartitionSpec as P


GROUP = 8
CHUNKS = (2, 1, 2, 2, 1)
SPANS = ((0, 2), (2, 6))
ORDER = (
    ("extract", 0),
    ("extract", 1),
    ("advect", 0),
    ("tables", 0),
    ("physics", 0),
    ("advect", 1),
    ("advect", 2),
    ("physics", 1),
    ("advect", 3),
    ("physics", 2),
    ("advect", 4),
    ("physics", 3),
    ("physics", 4),
    ("choose", 0),
    ("choose", 1),
    ("choose", 2),
    ("choose", 3),
    ("choose", 4),
)
CAP = 256
P_BLOCK = 32
F32 = jnp.float32
BF16 = jnp.bfloat16


def deinterleave():
    move = np.zeros((256, 256), np.float32)
    for k, a, t, i in itertools.product(range(2), range(2), range(GROUP), range(8)):
        move[((k * 2 + a) * GROUP + t) * 8 + i, ((t * 2 + k) * 8 + i) * 2 + a] = 1
    return jnp.asarray(move, BF16)


def face_rows(levels):
    rows = levels * 8
    move = np.zeros((2 * rows, 2 * rows), np.float32)
    for a, r in itertools.product(range(2), range(rows)):
        move[a * rows + r, r * 2 + a] = 1
    return jnp.asarray(move, BF16)


def product(a, b):
    return jnp.dot(a, b, preferred_element_type=F32)


def two_levels(q_ref, pair):
    return q_ref[:, 2 * pair : 2 * pair + 2].reshape(2 * GROUP * 16, 128)


def moved_rows(move, blocks):
    moved = []
    for at in range(0, len(blocks), 2):
        some = blocks[at : at + 2]
        both = product(move, jnp.concatenate(some, axis=1))
        moved += [both[:, i * 128 : (i + 1) * 128] for i in range(len(some))]
    return moved


def extract_kernel(apart_ref, face_move_ref, q_ref, lat_ref, lon_ref, *refs, faces_too):
    outs = refs[-3:] if faces_too else refs[-2:]
    north_ref, south_ref = outs[:2]
    levels = q_ref.shape[1]
    rows = levels * GROUP * 8
    blocks = [two_levels(q_ref, pair) for pair in range(levels // 2)]
    for pair, apart in enumerate(moved_rows(apart_ref[...], blocks)):
        for k in range(2):
            spot = pair * 128 + k * 64
            south_ref[0, spot : spot + 64, :] = apart[k * 128 : k * 128 + 64].astype(BF16)
            north_ref[0, spot : spot + 64, :] = apart[k * 128 + 64 : k * 128 + 128].astype(BF16)
    if south_ref.shape[1] > rows:
        faces = lat_ref[...].reshape(levels * 16, 128)
        south_ref[0, rows:, :] = product(face_move_ref[: levels * 8], faces).astype(BF16)
    if faces_too:

        @pl.when(pl.program_id(0) == 0)
        def _():
            blocks = [ref[...].reshape(levels * 16, 128) for ref in (lat_ref, lon_ref)]
            for at, both in enumerate(moved_rows(face_move_ref[...], blocks)):
                outs[2][2 * at] = both[: levels * 8]
                outs[2][2 * at + 1] = both[levels * 8 :]


def whole_block(*shape, once=False):
    mode = {"pipeline_mode": pl.Buffered(1)} if once else {}
    return pl.BlockSpec(shape, lambda *_: (0,) * len(shape), **mode)


def extract(apart, face_move, q, lat, lon, first, groups, faces_too, after):
    levels = q.shape[1]
    rows = levels * GROUP * 8
    extra = levels * 8 if first == 0 else 0
    faces = (4, levels * 8, 128)
    return pl.pallas_call(
        functools.partial(extract_kernel, faces_too=faces_too),
        grid=(groups,),
        in_specs=[
            whole_block(*apart.shape),
            whole_block(*face_move.shape),
            pl.BlockSpec((GROUP, levels, 16, 128), lambda g: (g + first, 0, 0, 0)),
            whole_block(*lat.shape),
            whole_block(*lon.shape),
        ]
        + [pl.BlockSpec(memory_space=pl.ANY)] * len(after),
        out_specs=[
            pl.BlockSpec((1, rows, 128), lambda g: (g, 0, 0)),
            pl.BlockSpec((1, rows + extra, 128), lambda g: (g, 0, 0)),
        ]
        + [whole_block(*faces)] * faces_too,
        out_shape=[
            jax.ShapeDtypeStruct((groups, rows, 128), BF16),
            jax.ShapeDtypeStruct((groups, rows + extra, 128), BF16),
        ]
        + [jax.ShapeDtypeStruct(faces, F32)] * faces_too,
        cost_estimate=pl.CostEstimate(
            flops=groups * 10**6, bytes_accessed=groups * 1200000, transcendentals=0
        ),
        compiler_params=pltpu.CompilerParams(vmem_limit_bytes=7 << 20),
        name="extract",
    )(apart, face_move, q, lat, lon, *after)


def beside(x, lane, toward_east):
    if toward_east:
        turned = pltpu.roll(x, 127, 1)
        return jnp.where(lane == 127, pltpu.roll(turned, 7, 0), turned)
    turned = pltpu.roll(x, 1, 1)
    return jnp.where(lane == 0, pltpu.roll(turned, 1, 0), turned)


def advect_kernel(
    place_ref, south_ref, north_ref, low_ref, high_ref, faces_ref, above_ref, *refs
):
    outs, made = refs[-5:-1], refs[-1]
    levels = faces_ref.shape[1] // 8
    lane = lax.broadcasted_iota(jnp.int32, (8, 128), 1)

    def body(k, carry):
        at = pl.ds(pl.multiple_of(k * 8, 8), 8)
        edge = [faces_ref[0, at, :], faces_ref[1, at, :], above_ref[0, at, :].astype(F32)]
        terms = []
        for lat in range(2):
            south, north, west = edge[lat], edge[lat + 1], faces_ref[2 + lat, at, :]
            east = beside(west, lane, True)
            own = (
                1.0
                - (jnp.maximum(north, 0.0) - jnp.minimum(south, 0.0))
                - (jnp.maximum(east, 0.0) - jnp.minimum(west, 0.0))
            )
            terms.append(
                (
                    own,
                    jnp.maximum(south, 0.0),
                    -jnp.minimum(north, 0.0),
                    jnp.maximum(west, 0.0),
                    -jnp.minimum(east, 0.0),
                )
            )
        for t in range(0, GROUP, 2):
            spot = pl.multiple_of(k * 64 + t * 8, 16)
            columns = [
                ref[0, pl.ds(spot, 16), :].astype(F32)
                for ref in (low_ref, south_ref, north_ref, high_ref)
            ]
            results = [[], []]
            for part in range(2):
                column = [x[part * 8 : part * 8 + 8] for x in columns]
                rows = column[1:3]
                for lat in range(2):
                    own, from_s, from_n, from_w, from_e = terms[lat]
                    results[lat].append(
                        own * rows[lat]
                        + (from_s * column[lat] + from_n * column[lat + 2])
                        + (
                            from_w * beside(rows[lat], lane, False)
                            + from_e * beside(rows[lat], lane, True)
                        )
                    )
            for lat in range(2):
                for part in range(2):
                    spot = ((lat * GROUP + t + part) * levels + k) * 8
                    made[pl.ds(pl.multiple_of(spot, 8), 8), :] = results[lat][part]
        return carry

    lax.fori_loop(0, levels, body, 0)
    for shift, out in enumerate(outs):
        tile = 2 * lax.rem(place_ref[0] + shift, 4)
        for t, lat, half in itertools.product(range(GROUP), range(2), range(2)):
            start = tile + (lat * GROUP + t) * levels * 8 + half
            column = (2 * lat + half) * 128
            out[0, t * levels : (t + 1) * levels, column : column + 128] = made[
                pl.ds(start, levels, stride=8), :
            ].astype(BF16)


def advect(place, south, north, low, high, faces, above, halo_first, groups, after):
    levels = faces.shape[1] // 8
    rows = levels * GROUP
    halo = pl.BlockSpec((1, rows * 8, 128), lambda g: (g + halo_first, 0, 0))
    return pl.pallas_call(
        advect_kernel,
        grid=(groups,),
        in_specs=[
            pl.BlockSpec(memory_space=pltpu.SMEM),
            halo,
            halo,
            halo,
            halo,
            whole_block(*faces.shape),
            pl.BlockSpec((1, levels * 8, 128), lambda g: (0, GROUP, 0)),
        ]
        + [pl.BlockSpec(memory_space=pl.ANY)] * len(after),
        out_specs=[pl.BlockSpec((1, rows, 512), lambda g: (g, 0, 0))] * 4,
        scratch_shapes=[pltpu.VMEM((levels * 128, 128), F32)],
        out_shape=[jax.ShapeDtypeStruct((groups, rows, 512), BF16)] * 4,
        cost_estimate=pl.CostEstimate(
            flops=groups * 10**7, bytes_accessed=groups * 2000000, transcendentals=0
        ),
        compiler_params=pltpu.CompilerParams(vmem_limit_bytes=10 << 20),
        name="advect",
    )(place, south, north, low, high, faces, above, *after)


def table_kernel(matrix_ref, mask_ref, order_ref, rain_ref, *refs):
    small_ref, placing_ref, picking_ref, back_ref, wet_ref, all_ref, held, turned, sems = refs[-9:]
    columns = mask_ref.shape[1]
    levels = rain_ref.shape[0]
    pieces, per_piece = held.shape[:2]
    copies = [
        pltpu.make_async_copy(
            matrix_ref.at[pl.ds(i * per_piece, per_piece)], held.at[i], sems.at[i]
        )
        for i in range(pieces)
    ]
    for copy in copies:
        copy.start()

    mask = mask_ref[...]
    order = order_ref[...]
    row = lax.broadcasted_iota(jnp.int32, (columns, columns), 0)
    column = lax.broadcasted_iota(jnp.int32, (columns, columns), 1)
    earlier = jnp.where(row < column, 1.0, 0.0).astype(BF16)
    ones = jnp.where(mask > 0, 1.0, 0.0)
    wide = jnp.broadcast_to(ones, (8, columns)).astype(BF16)
    rank = product(wide, earlier)[0:1]
    rank = jnp.where(mask > 0, rank, -1.0).astype(jnp.int32)
    slot = lax.broadcasted_iota(jnp.int32, (CAP, columns), 0)
    back = jnp.where(slot == rank, 1.0, 0.0).astype(BF16)
    back_ref[...] = back
    whole = jnp.where(row == order, 1.0, 0.0)
    placing_ref[...] = jnp.where(mask > 0, 0.0, whole).astype(BF16)
    picking_ref[...] = crossed(back, whole.astype(BF16)).astype(BF16)
    rain = rain_ref[...]
    all_ref[...] = rain.astype(F32)
    nothing = jnp.zeros((CAP, 128 - levels), F32)
    wet_ref[...] = jnp.concatenate([crossed(back, rain), nothing], axis=1)
    gap = jnp.zeros((128 - levels, columns), BF16)
    for piece in range(pieces):
        copies[piece].wait()
        for k in range(0, per_piece, 2):
            both = jnp.concatenate([held[piece, k], gap, held[piece, k + 1], gap], axis=0)
            found = crossed(back_ref[...], both)
            for part in range(2):
                lanes = slice(part * 128, (part + 1) * 128)
                turned[pl.ds(k + part, CAP, stride=per_piece), :] = found[:, lanes]
        spot = piece * per_piece
        small_ref[:, spot : spot + per_piece, :] = (
            turned[...].reshape(CAP, per_piece, 128).astype(BF16)
        )


def crossed(a, b):
    return lax.dot_general(a, b, (((1,), (1,)), ((), ())), preferred_element_type=F32)


def tables(matrix, mask, order, rain, after):
    levels, _, columns = matrix.shape
    per_piece = 8
    shapes = [
        ((CAP, levels, 128), BF16),
        ((columns, columns), BF16),
        ((CAP, columns), BF16),
        ((CAP, columns), BF16),
        ((CAP, 128), F32),
        ((levels, columns), F32),
    ]
    return pl.pallas_call(
        table_kernel,
        grid=(1,),
        in_specs=[
            pl.BlockSpec(memory_space=pl.ANY),
            whole_block(1, columns),
            whole_block(1, columns),
            whole_block(levels, columns),
        ]
        + [pl.BlockSpec(memory_space=pl.ANY)] * len(after),
        out_specs=[whole_block(*shape, once=True) for shape, _ in shapes],
        out_shape=[jax.ShapeDtypeStruct(*x) for x in shapes],
        scratch_shapes=[
            pltpu.VMEM((levels // per_piece, per_piece, levels, columns), BF16),
            pltpu.VMEM((CAP * per_piece, 128), F32),
            pltpu.SemaphoreType.DMA((levels // per_piece,)),
        ],
        cost_estimate=pl.CostEstimate(
            flops=2 * levels * 128 * columns * CAP, bytes_accessed=12 * 10**6, transcendentals=0
        ),
        compiler_params=pltpu.CompilerParams(vmem_limit_bytes=20 << 20),
        name="tables",
    )(matrix, mask, order, rain, *after)


def physics_kernel(
    place_ref, scav_ref, part0, part1, part2, part3, placing_ref, picking_ref, back_ref,
    matrix_ref, rain_ref, wet_ref, *refs, first
):
    out_ref, columns_in, picked, mixed, results, sems = refs[-6:]
    groups = part0.shape[0]
    levels = rain_ref.shape[0]
    part = part0.shape[1] // GROUP
    tracers = groups * GROUP

    columns_in[:, levels:, :] = jnp.zeros((tracers, 128 - levels, part0.shape[2]), BF16)
    for place in range(4):

        @pl.when(place_ref[0] == place)
        def _(place=place):
            for shift, ref in enumerate((part0, part1, part2, part3)):
                base = (place - shift) % 4 * part
                for g, t in itertools.product(range(groups), range(GROUP)):
                    columns_in[g * GROUP + t, base : base + part, :] = ref[
                        g, t * part : (t + 1) * part, :
                    ]

    for t in range(0, tracers, 2):
        both = crossed(picking_ref[...], columns_in[t : t + 2].reshape(256, part0.shape[2]))
        for part_at in range(2):
            lanes = slice(part_at * 128, (part_at + 1) * 128)
            g, row = divmod(t + part_at, GROUP)
            picked[g, pl.ds(row, CAP, stride=GROUP), :] = both[:, lanes]

    row = lax.broadcasted_iota(jnp.int32, (GROUP, 128), 0)
    rates = []
    for g in range(groups):
        rate = jnp.zeros((GROUP, 128), F32)
        for t in range(GROUP):
            rate = jnp.where(row == t, scav_ref[(first + g) * GROUP + t], rate)
        rates.append(rate)
    rate = jnp.concatenate(rates, axis=0)
    nothing = jnp.zeros((128 - levels, 128), BF16)

    def contract(block, carry):
        for inner in range(P_BLOCK):
            p = block * P_BLOCK + inner
            spot = pl.ds(pl.multiple_of(p * GROUP, GROUP), GROUP)
            mine = jnp.concatenate([picked[g, spot, :] for g in range(groups)], axis=0).astype(BF16)
            matrix = jnp.concatenate([matrix_ref[p], nothing], axis=0)
            wet = wet_ref[pl.ds(p, tracers, stride=0), :]
            washed = crossed(mine, matrix) * jnp.exp(-rate * wet)
            for g in range(groups):
                mixed[g, spot, :] = washed[g * GROUP : (g + 1) * GROUP]
        return carry

    lax.fori_loop(0, CAP // P_BLOCK, contract, 0)

    for g in range(groups):

        def finish(block, carry, g=g):
            row = block * 2
            at = g * GROUP + row
            both = columns_in[pl.ds(at, 2)].reshape(256, columns_in.shape[2])
            plain = product(both, placing_ref[...])
            for inner in range(2):
                spread = lax.dot_general(
                    mixed[g, pl.ds(row + inner, CAP, stride=GROUP), :].astype(BF16),
                    back_ref[...],
                    (((0,), (0,)), ((), ())),
                    preferred_element_type=F32,
                )[:levels]
                scav = scav_ref[first * GROUP + at + inner]
                dry = plain[inner * 128 : inner * 128 + levels]
                t = at + inner
                results[t] = (spread + dry * jnp.exp(-scav * rain_ref[...])).astype(BF16)
                pltpu.make_async_copy(results.at[t], out_ref.at[t], sems.at[t]).start()
            return carry

        lax.fori_loop(0, GROUP // 2, finish, 0)

    for t in range(tracers):
        pltpu.make_async_copy(results.at[t], out_ref.at[t], sems.at[t]).wait()


def physics(place, scav, parts, made, first, groups, after):
    matrix, placing, picking, back, wet, rain = made
    columns = parts[0].shape[2]
    levels = rain.shape[0]
    tracers = groups * GROUP
    flops = 2 * tracers * levels * columns * (columns + 3 * CAP)
    scalars = pl.BlockSpec(memory_space=pltpu.SMEM)
    operands = (placing, picking, back, matrix, rain, wet)
    return pl.pallas_call(
        functools.partial(physics_kernel, first=first),
        grid=(1,),
        in_specs=[scalars, scalars]
        + [whole_block(*x.shape, once=True) for x in (*parts, *operands)]
        + [pl.BlockSpec(memory_space=pl.ANY)] * len(after),
        out_specs=pl.BlockSpec(memory_space=pl.ANY),
        scratch_shapes=[
            pltpu.VMEM((tracers, 128, columns), BF16),
            pltpu.VMEM((groups, CAP * GROUP, 128), F32),
            pltpu.VMEM((groups, CAP * GROUP, 128), F32),
            pltpu.VMEM((tracers, levels, columns), BF16),
            pltpu.SemaphoreType.DMA((tracers,)),
        ],
        out_shape=jax.ShapeDtypeStruct((tracers, levels, columns), BF16),
        cost_estimate=pl.CostEstimate(
            flops=flops, bytes_accessed=groups * 1200000 + 6500000, transcendentals=0
        ),
        compiler_params=pltpu.CompilerParams(vmem_limit_bytes=(12 + 4 * groups) << 20),
        name="physics",
    )(place, scav, *parts, *operands, *after)


def choose_kernel(pair_ref, flag_ref, own_ref, partner_ref, *refs, first):
    out_ref, held, in_sems, out_sems = refs[-4:]
    pieces, rows = held.shape[:2]

    def copied_from(source):
        ins = [
            pltpu.make_async_copy(source.at[pl.ds(i * rows, rows)], held.at[i], in_sems.at[i])
            for i in range(pieces)
        ]
        outs = [
            pltpu.make_async_copy(
                held.at[i], out_ref.at[pl.ds(first + i * rows, rows)], out_sems.at[i]
            )
            for i in range(pieces)
        ]
        for copy in ins:
            copy.start()
        for i in range(pieces):
            ins[i].wait()
            outs[i].start()
        for copy in outs:
            copy.wait()

    flag = flag_ref[pair_ref[0]]

    @pl.when(flag > 0)
    def _():
        copied_from(partner_ref)

    @pl.when(flag <= 0)
    def _():
        copied_from(own_ref)


def choose(pair, flag, own, partner, whole, shape, first, groups, after):
    rows = shape[0] // sum(CHUNKS)
    pieces = 4 * groups
    operands = [own, partner]
    aliases = {}
    if whole is not None:
        operands.append(whole)
        aliases = {4: 0}
    operands += after
    anywhere = pl.BlockSpec(memory_space=pl.ANY)
    return pl.pallas_call(
        functools.partial(choose_kernel, first=first * rows),
        in_specs=[pl.BlockSpec(memory_space=pltpu.SMEM)] * 2 + [anywhere] * len(operands),
        out_specs=anywhere,
        scratch_shapes=[
            pltpu.VMEM((pieces, rows * groups // pieces, shape[1]), BF16),
            pltpu.SemaphoreType.DMA((pieces,)),
            pltpu.SemaphoreType.DMA((pieces,)),
        ],
        out_shape=jax.ShapeDtypeStruct(shape, BF16),
        input_output_aliases=aliases,
        cost_estimate=pl.CostEstimate(
            flops=0, bytes_accessed=groups * 1200000, transcendentals=0
        ),
        compiler_params=pltpu.CompilerParams(vmem_limit_bytes=8 << 20),
        name="choose",
    )(pair, flag, *operands)


def shifted(value, axis, steps):
    count = lax.axis_size(axis)
    pairs = [(i, i + steps) for i in range(count) if 0 <= i + steps < count]
    return lax.ppermute(value, axis, pairs)


def turned(value, axis, steps):
    count = lax.axis_size(axis)
    return lax.ppermute(value, axis, [(i, (i + steps) % count) for i in range(count)])


def paired(value, axis):
    count = lax.axis_size(axis)
    return lax.ppermute(value, axis, [(i, i ^ (count // 2)) for i in range(count)])


def tiled_rows(value):
    lead = value.shape[:-2]
    lats, lons = value.shape[-2:]
    split = value.reshape(*lead, lats, lons // 128, 128)
    return jnp.swapaxes(split, -3, -2).reshape(*lead, lats * lons // 128, 128)


def local(
    tracer_dyn,
    courant_lat,
    courant_lon,
    conv_matrix,
    conv_mask,
    column_order,
    rain,
    scav_rate,
    pair_flag,
):
    n_lat = lax.axis_size("lat")
    n_lev = lax.axis_size("lev")
    tracers = tracer_dyn.shape[0]
    levels, columns = rain.shape
    lev_place = lax.axis_index("lev")
    pair_index = lax.axis_index("lat") % (n_lat // 2) * n_lev + lev_place
    pair = pair_index.astype(jnp.int32).reshape(1)
    in_hbm = functools.partial(pltpu.with_memory_space_constraint, memory_space=pltpu.HBM)
    q = in_hbm(tiled_rows(tracer_dyn))
    lat, lon = in_hbm(tiled_rows(courant_lat)), in_hbm(tiled_rows(courant_lon))
    firsts = [sum(CHUNKS[:number]) for number in range(len(CHUNKS))]
    apart, face_move = (in_hbm(x) for x in (deinterleave(), face_rows(lat.shape[0])))
    place = lev_place.astype(jnp.int32).reshape(1)
    halos, sections, owns, partners, made = {}, {}, {}, {}, {}
    out = last = None
    for kind, number in ORDER:
        after = [] if last is None else [last]
        if kind == "extract":
            found = extract(
                apart, face_move, q, lat, lon, *SPANS[number], number == 0, after
            )
            north, south = found[:2]
            faces = found[2] if number == 0 else faces
            last = north
            high = shifted(south, "lat", -1)
            low = shifted(north, "lat", 1)
            halos[number] = (south, north, low, high)
        elif kind == "tables":
            made = tables(
                in_hbm(conv_matrix),
                in_hbm(conv_mask.reshape(1, columns)),
                in_hbm(column_order.reshape(1, columns)),
                in_hbm(rain),
                after,
            )
            last = made[2]
        elif kind == "advect":
            first, groups = firsts[number], CHUNKS[number]
            span = max(i for i in range(len(SPANS)) if SPANS[i][0] <= first)
            parts = advect(
                place, *halos[span], faces, halos[0][3], first - SPANS[span][0], groups, after
            )
            parts = list(parts)
            last = parts[0]
            for shift in (2, 1, 3):
                parts[shift] = turned(parts[shift], "lev", shift)
            sections[number] = parts
        elif kind == "physics":
            own = physics(
                place, scav_rate, sections[number], made,
                firsts[number], CHUNKS[number], after,
            )
            own = own.reshape(-1, columns)
            last = owns[number] = own
            partners[number] = paired(own, "lat")
        else:
            out = choose(
                pair, pair_flag, owns[number], partners[number], out, (tracers * levels, columns),
                firsts[number], CHUNKS[number], after,
            )
    return out.reshape(tracers, levels, columns)


def solution(mesh):
    placed = (
        P(None, "lev", "lat", None),
        P("lev", "lat", None),
        P("lev", "lat", None),
        P(None, None, ("lat", "lev")),
        P(("lat", "lev")),
        P(("lat", "lev")),
        P(None, ("lat", "lev")),
        P(),
        P(),
    )

    return jax.shard_map(
        local, mesh=mesh, in_specs=placed, out_specs=P(None, None, ("lat", "lev")), check_vma=False
    )
```

```python
import functools
import itertools

import jax
import jax.numpy as jnp
import numpy as np
from jax import lax
from jax.experimental import pallas as pl
from jax.experimental.pallas import tpu as pltpu
from jax.sharding import PartitionSpec as P


GROUP = 8
CHUNKS = (2, 1, 2, 2, 1)
SPANS = ((0, 3), (3, 5))
ORDER = (
    ("extract", 0),
    ("extract", 1),
    ("advect", 0),
    ("tables", 0),
    ("advect", 1),
    ("physics", 0),
    ("advect", 2),
    ("physics", 1),
    ("advect", 3),
    ("physics", 2),
    ("advect", 4),
    ("physics", 3),
    ("physics", 4),
    ("choose", 0),
    ("choose", 1),
    ("choose", 2),
    ("choose", 3),
    ("choose", 4),
)
CAP = 256
STREAMS = 4
P_BLOCK = 32
F32 = jnp.float32
BF16 = jnp.bfloat16


def deinterleave():
    move = np.zeros((256, 256), np.float32)
    for k, a, t, i in itertools.product(range(2), range(2), range(GROUP), range(8)):
        move[((k * 2 + a) * GROUP + t) * 8 + i, ((t * 2 + k) * 8 + i) * 2 + a] = 1
    return jnp.asarray(move, BF16)


def face_rows(levels):
    rows = levels * 8
    move = np.zeros((2 * rows, 2 * rows), np.float32)
    for a, r in itertools.product(range(2), range(rows)):
        move[a * rows + r, r * 2 + a] = 1
    return jnp.asarray(move, BF16)


def product(a, b):
    return jnp.dot(a, b, preferred_element_type=F32)


def two_levels(q_refs, pair):
    rows = [q_ref[:, 2 * pair : 2 * pair + 2].reshape(-1, 128) for q_ref in q_refs]
    return jnp.concatenate(rows, axis=0)


def moved_rows(move, blocks):
    moved = []
    for at in range(0, len(blocks), 2):
        some = blocks[at : at + 2]
        both = product(move, jnp.concatenate(some, axis=1))
        moved += [both[:, i * 128 : (i + 1) * 128] for i in range(len(some))]
    return moved


def extract_kernel(apart_ref, face_move_ref, lat_ref, lon_ref, *refs, faces_too):
    q_refs = refs[:STREAMS]
    outs = refs[-3:] if faces_too else refs[-2:]
    north_ref, south_ref = outs[:2]
    levels = q_refs[0].shape[1]
    rows = levels * GROUP * 8
    blocks = [two_levels(q_refs, pair) for pair in range(levels // 2)]
    for pair, apart in enumerate(moved_rows(apart_ref[...], blocks)):
        for k in range(2):
            spot = pair * 128 + k * 64
            south_ref[0, spot : spot + 64, :] = apart[k * 128 : k * 128 + 64].astype(BF16)
            north_ref[0, spot : spot + 64, :] = apart[k * 128 + 64 : k * 128 + 128].astype(BF16)
    if south_ref.shape[1] > rows:
        faces = lat_ref[...].reshape(levels * 16, 128)
        south_ref[0, rows:, :] = product(face_move_ref[: levels * 8], faces).astype(BF16)
    if faces_too:

        @pl.when(pl.program_id(0) == 0)
        def _():
            blocks = [ref[...].reshape(levels * 16, 128) for ref in (lat_ref, lon_ref)]
            for at, both in enumerate(moved_rows(face_move_ref[...], blocks)):
                outs[2][2 * at] = both[: levels * 8]
                outs[2][2 * at + 1] = both[levels * 8 :]


def whole_block(*shape, once=False):
    mode = {"pipeline_mode": pl.Buffered(1)} if once else {}
    return pl.BlockSpec(shape, lambda *_: (0,) * len(shape), **mode)


def extract(apart, face_move, q, lat, lon, first, groups, faces_too, after):
    levels = q.shape[1]
    rows = levels * GROUP * 8
    extra = levels * 8 if first == 0 else 0
    faces = (4, levels * 8, 128)
    return pl.pallas_call(
        functools.partial(extract_kernel, faces_too=faces_too),
        grid=(groups,),
        in_specs=[
            whole_block(*apart.shape),
            whole_block(*face_move.shape),
            whole_block(*lat.shape),
            whole_block(*lon.shape),
        ]
        + [
            pl.BlockSpec(
                (GROUP // STREAMS, levels, 16, 128),
                lambda g, i=i: ((g + first) * STREAMS + i, 0, 0, 0),
            )
            for i in range(STREAMS)
        ]
        + [pl.BlockSpec(memory_space=pl.ANY)] * len(after),
        out_specs=[
            pl.BlockSpec((1, rows, 128), lambda g: (g, 0, 0)),
            pl.BlockSpec((1, rows + extra, 128), lambda g: (g, 0, 0)),
        ]
        + [whole_block(*faces)] * faces_too,
        out_shape=[
            jax.ShapeDtypeStruct((groups, rows, 128), BF16),
            jax.ShapeDtypeStruct((groups, rows + extra, 128), BF16),
        ]
        + [jax.ShapeDtypeStruct(faces, F32)] * faces_too,
        cost_estimate=pl.CostEstimate(
            flops=groups * 10**6, bytes_accessed=groups * 1200000, transcendentals=0
        ),
        compiler_params=pltpu.CompilerParams(vmem_limit_bytes=7 << 20),
        name="extract",
    )(apart, face_move, lat, lon, *[q] * STREAMS, *after)


def beside(x, lane, toward_east):
    if toward_east:
        turned = pltpu.roll(x, 127, 1)
        return jnp.where(lane == 127, pltpu.roll(turned, 7, 0), turned)
    turned = pltpu.roll(x, 1, 1)
    return jnp.where(lane == 0, pltpu.roll(turned, 1, 0), turned)


def advect_kernel(
    place_ref, south_ref, north_ref, low_ref, high_ref, faces_ref, above_ref, *refs
):
    outs, made = refs[-5:-1], refs[-1]
    levels = faces_ref.shape[1] // 8
    lane = lax.broadcasted_iota(jnp.int32, (8, 128), 1)

    def body(k, carry):
        at = pl.ds(pl.multiple_of(k * 8, 8), 8)
        edge = [faces_ref[0, at, :], faces_ref[1, at, :], above_ref[0, at, :].astype(F32)]
        terms = []
        for lat in range(2):
            south, north, west = edge[lat], edge[lat + 1], faces_ref[2 + lat, at, :]
            east = beside(west, lane, True)
            own = (
                1.0
                - (jnp.maximum(north, 0.0) - jnp.minimum(south, 0.0))
                - (jnp.maximum(east, 0.0) - jnp.minimum(west, 0.0))
            )
            terms.append(
                (
                    own,
                    jnp.maximum(south, 0.0),
                    -jnp.minimum(north, 0.0),
                    jnp.maximum(west, 0.0),
                    -jnp.minimum(east, 0.0),
                )
            )
        for t in range(0, GROUP, 2):
            spot = pl.multiple_of(k * 64 + t * 8, 16)
            columns = [
                ref[0, pl.ds(spot, 16), :].astype(F32)
                for ref in (low_ref, south_ref, north_ref, high_ref)
            ]
            results = [[], []]
            for part in range(2):
                column = [x[part * 8 : part * 8 + 8] for x in columns]
                rows = column[1:3]
                for lat in range(2):
                    own, from_s, from_n, from_w, from_e = terms[lat]
                    results[lat].append(
                        own * rows[lat]
                        + (from_s * column[lat] + from_n * column[lat + 2])
                        + (
                            from_w * beside(rows[lat], lane, False)
                            + from_e * beside(rows[lat], lane, True)
                        )
                    )
            for lat in range(2):
                for part in range(2):
                    spot = ((lat * GROUP + t + part) * levels + k) * 8
                    made[pl.ds(pl.multiple_of(spot, 8), 8), :] = results[lat][part]
        return carry

    lax.fori_loop(0, levels, body, 0)
    for shift, out in enumerate(outs):
        tile = 2 * lax.rem(place_ref[0] + shift, 4)
        for t, lat, half in itertools.product(range(GROUP), range(2), range(2)):
            start = tile + (lat * GROUP + t) * levels * 8 + half
            column = (2 * lat + half) * 128
            out[0, t * levels : (t + 1) * levels, column : column + 128] = made[
                pl.ds(start, levels, stride=8), :
            ].astype(BF16)


def advect(place, south, north, low, high, faces, above, halo_first, groups, after):
    levels = faces.shape[1] // 8
    rows = levels * GROUP
    halo = pl.BlockSpec((1, rows * 8, 128), lambda g: (g + halo_first, 0, 0))
    return pl.pallas_call(
        advect_kernel,
        grid=(groups,),
        in_specs=[
            pl.BlockSpec(memory_space=pltpu.SMEM),
            halo,
            halo,
            halo,
            halo,
            whole_block(*faces.shape),
            pl.BlockSpec((1, levels * 8, 128), lambda g: (0, GROUP, 0)),
        ]
        + [pl.BlockSpec(memory_space=pl.ANY)] * len(after),
        out_specs=[pl.BlockSpec((1, rows, 512), lambda g: (g, 0, 0))] * 4,
        scratch_shapes=[pltpu.VMEM((levels * 128, 128), F32)],
        out_shape=[jax.ShapeDtypeStruct((groups, rows, 512), BF16)] * 4,
        cost_estimate=pl.CostEstimate(
            flops=groups * 10**7, bytes_accessed=groups * 2000000, transcendentals=0
        ),
        compiler_params=pltpu.CompilerParams(vmem_limit_bytes=10 << 20),
        name="advect",
    )(place, south, north, low, high, faces, above, *after)


def table_kernel(matrix_ref, mask_ref, order_ref, rain_ref, *refs):
    small_ref, placing_ref, picking_ref, back_ref, wet_ref, all_ref, held, turned, sems = refs[-9:]
    columns = mask_ref.shape[1]
    levels = rain_ref.shape[0]
    pieces, per_piece = held.shape[:2]
    copies = [
        pltpu.make_async_copy(
            matrix_ref.at[pl.ds(i * per_piece, per_piece)], held.at[i], sems.at[i]
        )
        for i in range(pieces)
    ]
    for copy in copies:
        copy.start()

    mask = mask_ref[...]
    order = order_ref[...]
    row = lax.broadcasted_iota(jnp.int32, (columns, columns), 0)
    column = lax.broadcasted_iota(jnp.int32, (columns, columns), 1)
    earlier = jnp.where(row < column, 1.0, 0.0).astype(BF16)
    ones = jnp.where(mask > 0, 1.0, 0.0)
    wide = jnp.broadcast_to(ones, (8, columns)).astype(BF16)
    rank = product(wide, earlier)[0:1]
    rank = jnp.where(mask > 0, rank, -1.0).astype(jnp.int32)
    slot = lax.broadcasted_iota(jnp.int32, (CAP, columns), 0)
    back = jnp.where(slot == rank, 1.0, 0.0).astype(BF16)
    back_ref[...] = back
    whole = jnp.where(row == order, 1.0, 0.0)
    placing_ref[...] = jnp.where(mask > 0, 0.0, whole).astype(BF16)
    picking_ref[...] = crossed(back, whole.astype(BF16)).astype(BF16)
    rain = rain_ref[...]
    all_ref[...] = rain.astype(F32)
    nothing = jnp.zeros((CAP, 128 - levels), F32)
    wet_ref[...] = jnp.concatenate([crossed(back, rain), nothing], axis=1)
    gap = jnp.zeros((128 - levels, columns), BF16)
    for piece in range(pieces):
        copies[piece].wait()
        for k in range(0, per_piece, 2):
            both = jnp.concatenate([held[piece, k], gap, held[piece, k + 1], gap], axis=0)
            found = crossed(back_ref[...], both)
            for part in range(2):
                lanes = slice(part * 128, (part + 1) * 128)
                turned[pl.ds(k + part, CAP, stride=per_piece), :] = found[:, lanes]
        spot = piece * per_piece
        small_ref[:, spot : spot + per_piece, :] = (
            turned[...].reshape(CAP, per_piece, 128).astype(BF16)
        )


def crossed(a, b):
    return lax.dot_general(a, b, (((1,), (1,)), ((), ())), preferred_element_type=F32)


def tables(matrix, mask, order, rain, after):
    levels, _, columns = matrix.shape
    per_piece = 8
    shapes = [
        ((CAP, levels, 128), BF16),
        ((columns, columns), BF16),
        ((CAP, columns), BF16),
        ((CAP, columns), BF16),
        ((CAP, 128), F32),
        ((levels, columns), F32),
    ]
    return pl.pallas_call(
        table_kernel,
        grid=(1,),
        in_specs=[
            pl.BlockSpec(memory_space=pl.ANY),
            whole_block(1, columns),
            whole_block(1, columns),
            whole_block(levels, columns),
        ]
        + [pl.BlockSpec(memory_space=pl.ANY)] * len(after),
        out_specs=[whole_block(*shape, once=True) for shape, _ in shapes],
        out_shape=[jax.ShapeDtypeStruct(*x) for x in shapes],
        scratch_shapes=[
            pltpu.VMEM((levels // per_piece, per_piece, levels, columns), BF16),
            pltpu.VMEM((CAP * per_piece, 128), F32),
            pltpu.SemaphoreType.DMA((levels // per_piece,)),
        ],
        cost_estimate=pl.CostEstimate(
            flops=2 * levels * 128 * columns * CAP, bytes_accessed=12 * 10**6, transcendentals=0
        ),
        compiler_params=pltpu.CompilerParams(vmem_limit_bytes=20 << 20),
        name="tables",
    )(matrix, mask, order, rain, *after)


def physics_kernel(
    place_ref, scav_ref, part0, part1, part2, part3, placing_ref, picking_ref, back_ref,
    matrix_ref, rain_ref, wet_ref, *refs, first
):
    out_ref, columns_in, picked, mixed, results, sems = refs[-6:]
    groups = part0.shape[0]
    levels = rain_ref.shape[0]
    part = part0.shape[1] // GROUP
    tracers = groups * GROUP

    columns_in[:, levels:, :] = jnp.zeros((tracers, 128 - levels, part0.shape[2]), BF16)
    for place in range(4):

        @pl.when(place_ref[0] == place)
        def _(place=place):
            for shift, ref in enumerate((part0, part1, part2, part3)):
                base = (place - shift) % 4 * part
                for g, t in itertools.product(range(groups), range(GROUP)):
                    columns_in[g * GROUP + t, base : base + part, :] = ref[
                        g, t * part : (t + 1) * part, :
                    ]

    for t in range(0, tracers, 2):
        both = crossed(picking_ref[...], columns_in[t : t + 2].reshape(256, part0.shape[2]))
        for part_at in range(2):
            lanes = slice(part_at * 128, (part_at + 1) * 128)
            g, row = divmod(t + part_at, GROUP)
            picked[g, pl.ds(row, CAP, stride=GROUP), :] = both[:, lanes]

    row = lax.broadcasted_iota(jnp.int32, (GROUP, 128), 0)
    rates = []
    for g in range(groups):
        rate = jnp.zeros((GROUP, 128), F32)
        for t in range(GROUP):
            rate = jnp.where(row == t, scav_ref[(first + g) * GROUP + t], rate)
        rates.append(rate)
    rate = jnp.concatenate(rates, axis=0)
    nothing = jnp.zeros((128 - levels, 128), BF16)

    def contract(block, carry):
        for inner in range(P_BLOCK):
            p = block * P_BLOCK + inner
            spot = pl.ds(pl.multiple_of(p * GROUP, GROUP), GROUP)
            mine = jnp.concatenate([picked[g, spot, :] for g in range(groups)], axis=0).astype(BF16)
            matrix = jnp.concatenate([matrix_ref[p], nothing], axis=0)
            wet = wet_ref[pl.ds(p, tracers, stride=0), :]
            washed = crossed(mine, matrix) * jnp.exp(-rate * wet)
            for g in range(groups):
                mixed[g, spot, :] = washed[g * GROUP : (g + 1) * GROUP]
        return carry

    lax.fori_loop(0, CAP // P_BLOCK, contract, 0)

    for g in range(groups):

        def finish(block, carry, g=g):
            row = block * 2
            at = g * GROUP + row
            both = columns_in[pl.ds(at, 2)].reshape(256, columns_in.shape[2])
            plain = product(both, placing_ref[...])
            for inner in range(2):
                spread = lax.dot_general(
                    mixed[g, pl.ds(row + inner, CAP, stride=GROUP), :].astype(BF16),
                    back_ref[...],
                    (((0,), (0,)), ((), ())),
                    preferred_element_type=F32,
                )[:levels]
                scav = scav_ref[first * GROUP + at + inner]
                dry = plain[inner * 128 : inner * 128 + levels]
                t = at + inner
                results[t] = (spread + dry * jnp.exp(-scav * rain_ref[...])).astype(BF16)
                pltpu.make_async_copy(results.at[t], out_ref.at[t], sems.at[t]).start()
            return carry

        lax.fori_loop(0, GROUP // 2, finish, 0)

    for t in range(tracers):
        pltpu.make_async_copy(results.at[t], out_ref.at[t], sems.at[t]).wait()


def physics(place, scav, parts, made, first, groups, after):
    matrix, placing, picking, back, wet, rain = made
    columns = parts[0].shape[2]
    levels = rain.shape[0]
    tracers = groups * GROUP
    flops = 2 * tracers * levels * columns * (columns + 3 * CAP)
    scalars = pl.BlockSpec(memory_space=pltpu.SMEM)
    operands = (placing, picking, back, matrix, rain, wet)
    return pl.pallas_call(
        functools.partial(physics_kernel, first=first),
        grid=(1,),
        in_specs=[scalars, scalars]
        + [whole_block(*x.shape, once=True) for x in (*parts, *operands)]
        + [pl.BlockSpec(memory_space=pl.ANY)] * len(after),
        out_specs=pl.BlockSpec(memory_space=pltpu.HBM),
        scratch_shapes=[
            pltpu.VMEM((tracers, 128, columns), BF16),
            pltpu.VMEM((groups, CAP * GROUP, 128), F32),
            pltpu.VMEM((groups, CAP * GROUP, 128), F32),
            pltpu.VMEM((tracers, levels, columns), BF16),
            pltpu.SemaphoreType.DMA((tracers,)),
        ],
        out_shape=jax.ShapeDtypeStruct((tracers, levels, columns), BF16),
        cost_estimate=pl.CostEstimate(
            flops=flops, bytes_accessed=groups * 1200000 + 6500000, transcendentals=0
        ),
        compiler_params=pltpu.CompilerParams(vmem_limit_bytes=(12 + 4 * groups) << 20),
        name="physics",
    )(place, scav, *parts, *operands, *after)


def choose_kernel(pair_ref, flag_ref, own_ref, partner_ref, *refs, first, near):
    out_ref, held, in_sems, out_sems = refs[-4:]
    pieces, rows = held.shape[:2]

    def copied_at_once(source):
        outs = [
            pltpu.make_async_copy(
                source.at[pl.ds(i * rows, rows)],
                out_ref.at[pl.ds(first + i * rows, rows)],
                out_sems.at[i],
            )
            for i in range(pieces)
        ]
        for copy in outs:
            copy.start()
        for copy in outs:
            copy.wait()

    def copied_from(source):
        ins = [
            pltpu.make_async_copy(source.at[pl.ds(i * rows, rows)], held.at[i], in_sems.at[i])
            for i in range(pieces)
        ]
        outs = [
            pltpu.make_async_copy(
                held.at[i], out_ref.at[pl.ds(first + i * rows, rows)], out_sems.at[i]
            )
            for i in range(pieces)
        ]
        for copy in ins:
            copy.start()
        for i in range(pieces):
            ins[i].wait()
            outs[i].start()
        for copy in outs:
            copy.wait()

    flag = flag_ref[pair_ref[0]]

    @pl.when(flag > 0)
    def _():
        (copied_at_once if near else copied_from)(partner_ref)

    if not near:

        @pl.when(flag <= 0)
        def _():
            copied_from(own_ref)


def choose(pair, flag, own, partner, whole, shape, first, groups, after, near=False):
    rows = shape[0] // sum(CHUNKS)
    pieces = 4 * groups
    operands = [own, partner]
    aliases = {}
    if whole is not None:
        operands.append(whole)
        aliases = {4: 0}
    operands += after
    anywhere = pl.BlockSpec(memory_space=pl.ANY)
    return pl.pallas_call(
        functools.partial(choose_kernel, first=first * rows, near=near),
        in_specs=[pl.BlockSpec(memory_space=pltpu.SMEM)] * 2
        + [anywhere, pl.BlockSpec(memory_space=pltpu.VMEM) if near else anywhere]
        + [anywhere] * (len(operands) - 2),
        out_specs=anywhere,
        scratch_shapes=[
            pltpu.VMEM((pieces, rows * groups // pieces, shape[1]), BF16),
            pltpu.SemaphoreType.DMA((pieces,)),
            pltpu.SemaphoreType.DMA((pieces,)),
        ],
        out_shape=jax.ShapeDtypeStruct(shape, BF16),
        input_output_aliases=aliases,
        cost_estimate=pl.CostEstimate(
            flops=0, bytes_accessed=groups * 1200000, transcendentals=0
        ),
        compiler_params=pltpu.CompilerParams(vmem_limit_bytes=8 << 20),
        name="choose",
    )(pair, flag, *operands)


def shifted(value, axis, steps):
    count = lax.axis_size(axis)
    pairs = [(i, i + steps) for i in range(count) if 0 <= i + steps < count]
    return lax.ppermute(value, axis, pairs)


def turned(value, axis, steps):
    count = lax.axis_size(axis)
    return lax.ppermute(value, axis, [(i, (i + steps) % count) for i in range(count)])


def paired(value, axis):
    count = lax.axis_size(axis)
    return lax.ppermute(value, axis, [(i, i ^ (count // 2)) for i in range(count)])


def tiled_rows(value):
    lead = value.shape[:-2]
    lats, lons = value.shape[-2:]
    split = value.reshape(*lead, lats, lons // 128, 128)
    return jnp.swapaxes(split, -3, -2).reshape(*lead, lats * lons // 128, 128)


def local(
    tracer_dyn,
    courant_lat,
    courant_lon,
    conv_matrix,
    conv_mask,
    column_order,
    rain,
    scav_rate,
    pair_flag,
):
    n_lat = lax.axis_size("lat")
    n_lev = lax.axis_size("lev")
    tracers = tracer_dyn.shape[0]
    levels, columns = rain.shape
    lev_place = lax.axis_index("lev")
    pair_index = lax.axis_index("lat") % (n_lat // 2) * n_lev + lev_place
    pair = pair_index.astype(jnp.int32).reshape(1)
    in_hbm = functools.partial(pltpu.with_memory_space_constraint, memory_space=pltpu.HBM)
    q = in_hbm(tiled_rows(tracer_dyn))
    lat, lon = in_hbm(tiled_rows(courant_lat)), in_hbm(tiled_rows(courant_lon))
    firsts = [sum(CHUNKS[:number]) for number in range(len(CHUNKS))]
    apart, face_move = (in_hbm(x) for x in (deinterleave(), face_rows(lat.shape[0])))
    place = lev_place.astype(jnp.int32).reshape(1)
    halos, sections, owns, partners, made = {}, {}, {}, {}, {}
    out = last = None
    for kind, number in ORDER:
        after = [] if last is None else [last]
        if kind == "extract":
            found = extract(
                apart, face_move, q, lat, lon, *SPANS[number], number == 0, after
            )
            north, south = found[:2]
            faces = found[2] if number == 0 else faces
            last = north
            high = shifted(south, "lat", -1)
            low = shifted(north, "lat", 1)
            halos[number] = (south, north, low, high)
        elif kind == "tables":
            made = tables(
                in_hbm(conv_matrix),
                in_hbm(conv_mask.reshape(1, columns)),
                in_hbm(column_order.reshape(1, columns)),
                in_hbm(rain),
                after,
            )
            last = made[2]
        elif kind == "advect":
            first, groups = firsts[number], CHUNKS[number]
            span = max(i for i in range(len(SPANS)) if SPANS[i][0] <= first)
            parts = advect(
                place, *halos[span], faces, halos[0][3], first - SPANS[span][0], groups, after
            )
            parts = list(parts)
            last = parts[0]
            for shift in (2, 1, 3):
                parts[shift] = turned(parts[shift], "lev", shift)
            sections[number] = parts
        elif kind == "physics":
            own = physics(
                place, scav_rate, sections[number], made,
                firsts[number], CHUNKS[number], after,
            )
            own = own.reshape(-1, columns)
            last = owns[number] = own
            partners[number] = paired(own, "lat")
        else:
            where = ((tracers * levels, columns), firsts[number], CHUNKS[number], after)
            if number + 1 < len(CHUNKS):
                out = choose(pair, pair_flag, owns[number], partners[number], out, *where)
            else:
                out = choose(pair, pair_flag, owns[number], owns[number], out, *where)
                out = choose(
                    pair, pair_flag, owns[number], partners[number], out, *where, near=True
                )
    return out.reshape(tracers, levels, columns)


def solution(mesh):
    placed = (
        P(None, "lev", "lat", None),
        P("lev", "lat", None),
        P("lev", "lat", None),
        P(None, None, ("lat", "lev")),
        P(("lat", "lev")),
        P(("lat", "lev")),
        P(None, ("lat", "lev")),
        P(),
        P(),
    )

    return jax.shard_map(
        local, mesh=mesh, in_specs=placed, out_specs=P(None, None, ("lat", "lev")), check_vma=False
    )
```

```python
import functools
import itertools

import jax
import jax.numpy as jnp
import numpy as np
from jax import lax
from jax.experimental import pallas as pl
from jax.experimental.pallas import tpu as pltpu
from jax.sharding import PartitionSpec as P


GROUP = 8
CHUNKS = (2, 1, 2, 2, 1)
SPANS = ((0, 3), (3, 5))
ORDER = (
    ("extract", 0),
    ("extract", 1),
    ("advect", 0),
    ("tables", 0),
    ("advect", 1),
    ("physics", 0),
    ("advect", 2),
    ("physics", 1),
    ("advect", 3),
    ("physics", 2),
    ("advect", 4),
    ("physics", 3),
    ("physics", 4),
    ("choose", 0),
    ("choose", 1),
    ("choose", 2),
    ("choose", 3),
    ("choose", 4),
)
CAP = 256
STREAMS = 4
P_BLOCK = 32
F32 = jnp.float32
BF16 = jnp.bfloat16


def deinterleave():
    move = np.zeros((256, 256), np.float32)
    for k, a, t, i in itertools.product(range(2), range(2), range(GROUP), range(8)):
        move[((k * 2 + a) * GROUP + t) * 8 + i, ((t * 2 + k) * 8 + i) * 2 + a] = 1
    return jnp.asarray(move, BF16)


def face_rows(levels):
    rows = levels * 8
    move = np.zeros((2 * rows, 2 * rows), np.float32)
    for a, r in itertools.product(range(2), range(rows)):
        move[a * rows + r, r * 2 + a] = 1
    return jnp.asarray(move, BF16)


def product(a, b):
    return jnp.dot(a, b, preferred_element_type=F32)


def two_levels(q_refs, pair):
    rows = [q_ref[:, 2 * pair : 2 * pair + 2].reshape(-1, 128) for q_ref in q_refs]
    return jnp.concatenate(rows, axis=0)


def moved_rows(move, blocks):
    moved = []
    for at in range(0, len(blocks), 2):
        some = blocks[at : at + 2]
        both = product(move, jnp.concatenate(some, axis=1))
        moved += [both[:, i * 128 : (i + 1) * 128] for i in range(len(some))]
    return moved


def extract_kernel(apart_ref, face_move_ref, lat_ref, lon_ref, *refs, faces_too):
    q_refs = refs[:STREAMS]
    outs = refs[-3:] if faces_too else refs[-2:]
    north_ref, south_ref = outs[:2]
    levels = q_refs[0].shape[1]
    rows = levels * GROUP * 8
    blocks = [two_levels(q_refs, pair) for pair in range(levels // 2)]
    for pair, apart in enumerate(moved_rows(apart_ref[...], blocks)):
        for k in range(2):
            spot = pair * 128 + k * 64
            south_ref[0, spot : spot + 64, :] = apart[k * 128 : k * 128 + 64].astype(BF16)
            north_ref[0, spot : spot + 64, :] = apart[k * 128 + 64 : k * 128 + 128].astype(BF16)
    if south_ref.shape[1] > rows:
        faces = lat_ref[...].reshape(levels * 16, 128)
        south_ref[0, rows:, :] = product(face_move_ref[: levels * 8], faces).astype(BF16)
    if faces_too:

        @pl.when(pl.program_id(0) == 0)
        def _():
            blocks = [ref[...].reshape(levels * 16, 128) for ref in (lat_ref, lon_ref)]
            for at, both in enumerate(moved_rows(face_move_ref[...], blocks)):
                outs[2][2 * at] = both[: levels * 8]
                outs[2][2 * at + 1] = both[levels * 8 :]


def whole_block(*shape, once=False):
    mode = {"pipeline_mode": pl.Buffered(1)} if once else {}
    return pl.BlockSpec(shape, lambda *_: (0,) * len(shape), **mode)


def extract(apart, face_move, q, lat, lon, first, groups, faces_too, after):
    levels = q.shape[1]
    rows = levels * GROUP * 8
    extra = levels * 8 if first == 0 else 0
    faces = (4, levels * 8, 128)
    return pl.pallas_call(
        functools.partial(extract_kernel, faces_too=faces_too),
        grid=(groups,),
        in_specs=[
            whole_block(*apart.shape),
            whole_block(*face_move.shape),
            whole_block(*lat.shape),
            whole_block(*lon.shape),
        ]
        + [
            pl.BlockSpec(
                (GROUP // STREAMS, levels, 16, 128),
                lambda g, i=i: ((g + first) * STREAMS + i, 0, 0, 0),
            )
            for i in range(STREAMS)
        ]
        + [pl.BlockSpec(memory_space=pl.ANY)] * len(after),
        out_specs=[
            pl.BlockSpec((1, rows, 128), lambda g: (g, 0, 0)),
            pl.BlockSpec((1, rows + extra, 128), lambda g: (g, 0, 0)),
        ]
        + [whole_block(*faces)] * faces_too,
        out_shape=[
            jax.ShapeDtypeStruct((groups, rows, 128), BF16),
            jax.ShapeDtypeStruct((groups, rows + extra, 128), BF16),
        ]
        + [jax.ShapeDtypeStruct(faces, F32)] * faces_too,
        cost_estimate=pl.CostEstimate(
            flops=groups * 10**6, bytes_accessed=groups * 1200000, transcendentals=0
        ),
        compiler_params=pltpu.CompilerParams(vmem_limit_bytes=7 << 20),
        name="extract",
    )(apart, face_move, lat, lon, *[q] * STREAMS, *after)


def beside(x, lane, toward_east):
    if toward_east:
        turned = pltpu.roll(x, 127, 1)
        return jnp.where(lane == 127, pltpu.roll(turned, 7, 0), turned)
    turned = pltpu.roll(x, 1, 1)
    return jnp.where(lane == 0, pltpu.roll(turned, 1, 0), turned)


def advect_kernel(
    place_ref, south_ref, north_ref, low_ref, high_ref, faces_ref, above_ref, *refs
):
    outs, made = refs[-5:-1], refs[-1]
    levels = faces_ref.shape[1] // 8
    lane = lax.broadcasted_iota(jnp.int32, (8, 128), 1)

    def body(k, carry):
        at = pl.ds(pl.multiple_of(k * 8, 8), 8)
        edge = [faces_ref[0, at, :], faces_ref[1, at, :], above_ref[0, at, :].astype(F32)]
        terms = []
        for lat in range(2):
            south, north, west = edge[lat], edge[lat + 1], faces_ref[2 + lat, at, :]
            east = beside(west, lane, True)
            own = (
                1.0
                - (jnp.maximum(north, 0.0) - jnp.minimum(south, 0.0))
                - (jnp.maximum(east, 0.0) - jnp.minimum(west, 0.0))
            )
            terms.append(
                (
                    own,
                    jnp.maximum(south, 0.0),
                    -jnp.minimum(north, 0.0),
                    jnp.maximum(west, 0.0),
                    -jnp.minimum(east, 0.0),
                )
            )
        for t in range(0, GROUP, 2):
            spot = pl.multiple_of(k * 64 + t * 8, 16)
            columns = [
                ref[0, pl.ds(spot, 16), :].astype(F32)
                for ref in (low_ref, south_ref, north_ref, high_ref)
            ]
            results = [[], []]
            for part in range(2):
                column = [x[part * 8 : part * 8 + 8] for x in columns]
                rows = column[1:3]
                for lat in range(2):
                    own, from_s, from_n, from_w, from_e = terms[lat]
                    results[lat].append(
                        own * rows[lat]
                        + (from_s * column[lat] + from_n * column[lat + 2])
                        + (
                            from_w * beside(rows[lat], lane, False)
                            + from_e * beside(rows[lat], lane, True)
                        )
                    )
            for lat in range(2):
                for part in range(2):
                    spot = ((lat * GROUP + t + part) * levels + k) * 8
                    made[pl.ds(pl.multiple_of(spot, 8), 8), :] = results[lat][part]
        return carry

    lax.fori_loop(0, levels, body, 0)
    for shift, out in enumerate(outs):
        tile = 2 * lax.rem(place_ref[0] + shift, 4)
        for t, lat, half in itertools.product(range(GROUP), range(2), range(2)):
            start = tile + (lat * GROUP + t) * levels * 8 + half
            column = (2 * lat + half) * 128
            out[0, t * levels : (t + 1) * levels, column : column + 128] = made[
                pl.ds(start, levels, stride=8), :
            ].astype(BF16)


def advect(place, south, north, low, high, faces, above, halo_first, groups, after):
    levels = faces.shape[1] // 8
    rows = levels * GROUP
    halo = pl.BlockSpec((1, rows * 8, 128), lambda g: (g + halo_first, 0, 0))
    return pl.pallas_call(
        advect_kernel,
        grid=(groups,),
        in_specs=[
            pl.BlockSpec(memory_space=pltpu.SMEM),
            halo,
            halo,
            halo,
            halo,
            whole_block(*faces.shape),
            pl.BlockSpec((1, levels * 8, 128), lambda g: (0, GROUP, 0)),
        ]
        + [pl.BlockSpec(memory_space=pl.ANY)] * len(after),
        out_specs=[pl.BlockSpec((1, rows, 512), lambda g: (g, 0, 0))] * 4,
        scratch_shapes=[pltpu.VMEM((levels * 128 + 64, 128), F32)],
        out_shape=[jax.ShapeDtypeStruct((groups, rows, 512), BF16)] * 4,
        cost_estimate=pl.CostEstimate(
            flops=groups * 10**7, bytes_accessed=groups * 2000000, transcendentals=0
        ),
        compiler_params=pltpu.CompilerParams(vmem_limit_bytes=10 << 20),
        name="advect",
    )(place, south, north, low, high, faces, above, *after)


def table_kernel(matrix_ref, mask_ref, order_ref, rain_ref, *refs):
    small_ref, placing_ref, picking_ref, back_ref, wet_ref, all_ref, held, turned, sems = refs[-9:]
    columns = mask_ref.shape[1]
    levels = rain_ref.shape[0]
    pieces, per_piece = held.shape[:2]
    copies = [
        pltpu.make_async_copy(
            matrix_ref.at[pl.ds(i * per_piece, per_piece)], held.at[i], sems.at[i]
        )
        for i in range(pieces)
    ]
    for copy in copies:
        copy.start()

    mask = mask_ref[...]
    order = order_ref[...]
    row = lax.broadcasted_iota(jnp.int32, (columns, columns), 0)
    column = lax.broadcasted_iota(jnp.int32, (columns, columns), 1)
    earlier = jnp.where(row < column, 1.0, 0.0).astype(BF16)
    ones = jnp.where(mask > 0, 1.0, 0.0)
    wide = jnp.broadcast_to(ones, (8, columns)).astype(BF16)
    rank = product(wide, earlier)[0:1]
    rank = jnp.where(mask > 0, rank, -1.0).astype(jnp.int32)
    slot = lax.broadcasted_iota(jnp.int32, (CAP, columns), 0)
    back = jnp.where(slot == rank, 1.0, 0.0).astype(BF16)
    back_ref[...] = back
    whole = jnp.where(row == order, 1.0, 0.0)
    placing_ref[...] = jnp.where(mask > 0, 0.0, whole).astype(BF16)
    picking_ref[...] = crossed(back, whole.astype(BF16)).astype(BF16)
    rain = rain_ref[...]
    all_ref[...] = rain.astype(F32)
    nothing = jnp.zeros((CAP, 128 - levels), F32)
    wet_ref[:CAP] = jnp.concatenate([crossed(back, rain), nothing], axis=1)
    wet_ref[CAP:] = jnp.zeros((16, 128), F32)
    gap = jnp.zeros((128 - levels, columns), BF16)
    for piece in range(pieces):
        copies[piece].wait()
        for k in range(0, per_piece, 2):
            both = jnp.concatenate([held[piece, k], gap, held[piece, k + 1], gap], axis=0)
            found = crossed(back_ref[...], both)
            for part in range(2):
                lanes = slice(part * 128, (part + 1) * 128)
                turned[pl.ds(k + part, CAP, stride=per_piece), :] = found[:, lanes]
        spot = piece * per_piece
        small_ref[:, spot : spot + per_piece, :] = (
            turned[: CAP * per_piece].reshape(CAP, per_piece, 128).astype(BF16)
        )


def crossed(a, b):
    return lax.dot_general(a, b, (((1,), (1,)), ((), ())), preferred_element_type=F32)


def tables(matrix, mask, order, rain, after):
    levels, _, columns = matrix.shape
    per_piece = 8
    shapes = [
        ((CAP, levels, 128), BF16),
        ((columns, columns), BF16),
        ((CAP, columns), BF16),
        ((CAP, columns), BF16),
        ((CAP + 16, 128), F32),
        ((levels, columns), F32),
    ]
    return pl.pallas_call(
        table_kernel,
        grid=(1,),
        in_specs=[
            pl.BlockSpec(memory_space=pl.ANY),
            whole_block(1, columns),
            whole_block(1, columns),
            whole_block(levels, columns),
        ]
        + [pl.BlockSpec(memory_space=pl.ANY)] * len(after),
        out_specs=[whole_block(*shape, once=True) for shape, _ in shapes],
        out_shape=[jax.ShapeDtypeStruct(*x) for x in shapes],
        scratch_shapes=[
            pltpu.VMEM((levels // per_piece, per_piece, levels, columns), BF16),
            pltpu.VMEM((CAP * per_piece + 8, 128), F32),
            pltpu.SemaphoreType.DMA((levels // per_piece,)),
        ],
        cost_estimate=pl.CostEstimate(
            flops=2 * levels * 128 * columns * CAP, bytes_accessed=12 * 10**6, transcendentals=0
        ),
        compiler_params=pltpu.CompilerParams(vmem_limit_bytes=20 << 20),
        name="tables",
    )(matrix, mask, order, rain, *after)


def physics_kernel(
    place_ref, scav_ref, part0, part1, part2, part3, placing_ref, picking_ref, back_ref,
    matrix_ref, rain_ref, wet_ref, *refs, first
):
    out_ref, columns_in, picked, mixed, results, sems = refs[-6:]
    groups = part0.shape[0]
    levels = rain_ref.shape[0]
    part = part0.shape[1] // GROUP
    tracers = groups * GROUP

    columns_in[:, levels:, :] = jnp.zeros((tracers, 128 - levels, part0.shape[2]), BF16)
    for place in range(4):

        @pl.when(place_ref[0] == place)
        def _(place=place):
            for shift, ref in enumerate((part0, part1, part2, part3)):
                base = (place - shift) % 4 * part
                for g, t in itertools.product(range(groups), range(GROUP)):
                    columns_in[g * GROUP + t, base : base + part, :] = ref[
                        g, t * part : (t + 1) * part, :
                    ]

    for t in range(0, tracers, 2):
        both = crossed(picking_ref[...], columns_in[t : t + 2].reshape(256, part0.shape[2]))
        for part_at in range(2):
            lanes = slice(part_at * 128, (part_at + 1) * 128)
            g, row = divmod(t + part_at, GROUP)
            picked[g, pl.ds(row, CAP, stride=GROUP), :] = both[:, lanes]

    row = lax.broadcasted_iota(jnp.int32, (GROUP, 128), 0)
    rates = []
    for g in range(groups):
        rate = jnp.zeros((GROUP, 128), F32)
        for t in range(GROUP):
            rate = jnp.where(row == t, scav_ref[(first + g) * GROUP + t], rate)
        rates.append(rate)
    rate = jnp.concatenate(rates, axis=0)
    nothing = jnp.zeros((128 - levels, 128), BF16)

    def contract(block, carry):
        for inner in range(P_BLOCK):
            p = block * P_BLOCK + inner
            spot = pl.ds(pl.multiple_of(p * GROUP, GROUP), GROUP)
            mine = jnp.concatenate([picked[g, spot, :] for g in range(groups)], axis=0).astype(BF16)
            matrix = jnp.concatenate([matrix_ref[p], nothing], axis=0)
            wet = wet_ref[pl.ds(p, tracers, stride=0), :]
            washed = crossed(mine, matrix) * jnp.exp(-rate * wet)
            for g in range(groups):
                mixed[g, spot, :] = washed[g * GROUP : (g + 1) * GROUP]
        return carry

    lax.fori_loop(0, CAP // P_BLOCK, contract, 0)

    for g in range(groups):

        def finish(block, carry, g=g):
            row = block * 2
            at = g * GROUP + row
            both = columns_in[pl.ds(at, 2)].reshape(256, columns_in.shape[2])
            plain = product(both, placing_ref[...])
            for inner in range(2):
                spread = lax.dot_general(
                    mixed[g, pl.ds(row + inner, CAP, stride=GROUP), :].astype(BF16),
                    back_ref[...],
                    (((0,), (0,)), ((), ())),
                    preferred_element_type=F32,
                )[:levels]
                scav = scav_ref[first * GROUP + at + inner]
                dry = plain[inner * 128 : inner * 128 + levels]
                t = at + inner
                results[t] = (spread + dry * jnp.exp(-scav * rain_ref[...])).astype(BF16)
                pltpu.make_async_copy(results.at[t], out_ref.at[t], sems.at[t]).start()
            return carry

        lax.fori_loop(0, GROUP // 2, finish, 0)

    for t in range(tracers):
        pltpu.make_async_copy(results.at[t], out_ref.at[t], sems.at[t]).wait()


def physics(place, scav, parts, made, first, groups, after):
    matrix, placing, picking, back, wet, rain = made
    columns = parts[0].shape[2]
    levels = rain.shape[0]
    tracers = groups * GROUP
    flops = 2 * tracers * levels * columns * (columns + 3 * CAP)
    scalars = pl.BlockSpec(memory_space=pltpu.SMEM)
    operands = (placing, picking, back, matrix, rain, wet)
    return pl.pallas_call(
        functools.partial(physics_kernel, first=first),
        grid=(1,),
        in_specs=[scalars, scalars]
        + [whole_block(*x.shape, once=True) for x in (*parts, *operands)]
        + [pl.BlockSpec(memory_space=pl.ANY)] * len(after),
        out_specs=pl.BlockSpec(memory_space=pltpu.HBM),
        scratch_shapes=[
            pltpu.VMEM((tracers, 128, columns), BF16),
            pltpu.VMEM((groups, CAP * GROUP + 8, 128), F32),
            pltpu.VMEM((groups, CAP * GROUP + 8, 128), F32),
            pltpu.VMEM((tracers, levels, columns), BF16),
            pltpu.SemaphoreType.DMA((tracers,)),
        ],
        out_shape=jax.ShapeDtypeStruct((tracers, levels, columns), BF16),
        cost_estimate=pl.CostEstimate(
            flops=flops, bytes_accessed=groups * 1200000 + 6500000, transcendentals=0
        ),
        compiler_params=pltpu.CompilerParams(vmem_limit_bytes=(12 + 4 * groups) << 20),
        name="physics",
    )(place, scav, *parts, *operands, *after)


def choose_kernel(pair_ref, flag_ref, own_ref, partner_ref, *refs, first, near):
    out_ref, held, in_sems, out_sems = refs[-4:]
    pieces, rows = held.shape[:2]

    def copied_at_once(source):
        outs = [
            pltpu.make_async_copy(
                source.at[pl.ds(i * rows, rows)],
                out_ref.at[pl.ds(first + i * rows, rows)],
                out_sems.at[i],
            )
            for i in range(pieces)
        ]
        for copy in outs:
            copy.start()
        for copy in outs:
            copy.wait()

    def copied_from(source):
        ins = [
            pltpu.make_async_copy(source.at[pl.ds(i * rows, rows)], held.at[i], in_sems.at[i])
            for i in range(pieces)
        ]
        outs = [
            pltpu.make_async_copy(
                held.at[i], out_ref.at[pl.ds(first + i * rows, rows)], out_sems.at[i]
            )
            for i in range(pieces)
        ]
        for copy in ins:
            copy.start()
        for i in range(pieces):
            ins[i].wait()
            outs[i].start()
        for copy in outs:
            copy.wait()

    flag = flag_ref[pair_ref[0]]

    @pl.when(flag > 0)
    def _():
        (copied_at_once if near else copied_from)(partner_ref)

    if not near:

        @pl.when(flag <= 0)
        def _():
            copied_from(own_ref)


def choose(pair, flag, own, partner, whole, shape, first, groups, after, near=False):
    rows = shape[0] // sum(CHUNKS)
    pieces = 4 * groups
    operands = [own, partner]
    aliases = {}
    if whole is not None:
        operands.append(whole)
        aliases = {4: 0}
    operands += after
    anywhere = pl.BlockSpec(memory_space=pl.ANY)
    return pl.pallas_call(
        functools.partial(choose_kernel, first=first * rows, near=near),
        in_specs=[pl.BlockSpec(memory_space=pltpu.SMEM)] * 2
        + [anywhere, pl.BlockSpec(memory_space=pltpu.VMEM) if near else anywhere]
        + [anywhere] * (len(operands) - 2),
        out_specs=anywhere,
        scratch_shapes=[
            pltpu.VMEM((pieces, rows * groups // pieces, shape[1]), BF16),
            pltpu.SemaphoreType.DMA((pieces,)),
            pltpu.SemaphoreType.DMA((pieces,)),
        ],
        out_shape=jax.ShapeDtypeStruct(shape, BF16),
        input_output_aliases=aliases,
        cost_estimate=pl.CostEstimate(
            flops=0, bytes_accessed=groups * 1200000, transcendentals=0
        ),
        compiler_params=pltpu.CompilerParams(vmem_limit_bytes=8 << 20),
        name="choose",
    )(pair, flag, *operands)


def shifted(value, axis, steps):
    count = lax.axis_size(axis)
    pairs = [(i, i + steps) for i in range(count) if 0 <= i + steps < count]
    return lax.ppermute(value, axis, pairs)


def turned(value, axis, steps):
    count = lax.axis_size(axis)
    return lax.ppermute(value, axis, [(i, (i + steps) % count) for i in range(count)])


def paired(value, axis):
    count = lax.axis_size(axis)
    return lax.ppermute(value, axis, [(i, i ^ (count // 2)) for i in range(count)])


def tiled_rows(value):
    lead = value.shape[:-2]
    lats, lons = value.shape[-2:]
    split = value.reshape(*lead, lats, lons // 128, 128)
    return jnp.swapaxes(split, -3, -2).reshape(*lead, lats * lons // 128, 128)


def local(
    tracer_dyn,
    courant_lat,
    courant_lon,
    conv_matrix,
    conv_mask,
    column_order,
    rain,
    scav_rate,
    pair_flag,
):
    n_lat = lax.axis_size("lat")
    n_lev = lax.axis_size("lev")
    tracers = tracer_dyn.shape[0]
    levels, columns = rain.shape
    lev_place = lax.axis_index("lev")
    pair_index = lax.axis_index("lat") % (n_lat // 2) * n_lev + lev_place
    pair = pair_index.astype(jnp.int32).reshape(1)
    in_hbm = functools.partial(pltpu.with_memory_space_constraint, memory_space=pltpu.HBM)
    q = in_hbm(tiled_rows(tracer_dyn))
    lat, lon = in_hbm(tiled_rows(courant_lat)), in_hbm(tiled_rows(courant_lon))
    firsts = [sum(CHUNKS[:number]) for number in range(len(CHUNKS))]
    apart, face_move = (in_hbm(x) for x in (deinterleave(), face_rows(lat.shape[0])))
    place = lev_place.astype(jnp.int32).reshape(1)
    halos, sections, owns, partners, made = {}, {}, {}, {}, {}
    out = last = None
    for kind, number in ORDER:
        after = [] if last is None else [last]
        if kind == "extract":
            found = extract(
                apart, face_move, q, lat, lon, *SPANS[number], number == 0, after
            )
            north, south = found[:2]
            faces = found[2] if number == 0 else faces
            last = north
            high = shifted(south, "lat", -1)
            low = shifted(north, "lat", 1)
            halos[number] = (south, north, low, high)
        elif kind == "tables":
            made = tables(
                in_hbm(conv_matrix),
                in_hbm(conv_mask.reshape(1, columns)),
                in_hbm(column_order.reshape(1, columns)),
                in_hbm(rain),
                after,
            )
            last = made[2]
        elif kind == "advect":
            first, groups = firsts[number], CHUNKS[number]
            span = max(i for i in range(len(SPANS)) if SPANS[i][0] <= first)
            parts = advect(
                place, *halos[span], faces, halos[0][3], first - SPANS[span][0], groups, after
            )
            parts = list(parts)
            last = parts[0]
            for shift in (2, 1, 3):
                parts[shift] = turned(parts[shift], "lev", shift)
            sections[number] = parts
        elif kind == "physics":
            own = physics(
                place, scav_rate, sections[number], made,
                firsts[number], CHUNKS[number], after,
            )
            own = own.reshape(-1, columns)
            last = owns[number] = own
            partners[number] = paired(own, "lat")
        else:
            where = ((tracers * levels, columns), firsts[number], CHUNKS[number], after)
            if number + 1 < len(CHUNKS):
                out = choose(pair, pair_flag, owns[number], partners[number], out, *where)
            else:
                out = choose(pair, pair_flag, owns[number], owns[number], out, *where)
                out = choose(
                    pair, pair_flag, owns[number], partners[number], out, *where, near=True
                )
    return out.reshape(tracers, levels, columns)


def solution(mesh):
    placed = (
        P(None, "lev", "lat", None),
        P("lev", "lat", None),
        P("lev", "lat", None),
        P(None, None, ("lat", "lev")),
        P(("lat", "lev")),
        P(("lat", "lev")),
        P(None, ("lat", "lev")),
        P(),
        P(),
    )

    return jax.shard_map(
        local, mesh=mesh, in_specs=placed, out_specs=P(None, None, ("lat", "lev")), check_vma=False
    )
```
